32 devices in a mesh: dp: 16 (over z, y, core), tile: 2 (over x).
Axes of the slice: x: 2, y: 2, z: 4, core: 2. Of those that a mesh axis runs over, the one named last changes fastest.
Arguments:
- tokens: bfloat16 [16, 1024, 768], P('dp', 'tile'), may hold values from -11 to 11
- segment_ids: int32 [16, 1024], P('dp'), may hold values from 0 to 7, never falling along the last dimension, each value on 1 to 256 neighbouring positions
- keep_mask: int32 [16, 1024], P('dp'), may hold values 0 or 1
- gain_one: float32 [768], replicated, may hold values from 0.25 to 1.75
- bias_one: float32 [768], replicated, may hold values from -3 to 3
- qkv_weight: bfloat16 [768, 2304], replicated, may hold values from -0.21875 to 0.21875
- query_bias: float32 [768], replicated, may hold values from -3 to 3
- value_bias: float32 [768], replicated, may hold values from -3 to 3
- out_weight: bfloat16 [768, 768], replicated, may hold values from -2 to 2
- out_bias: float32 [768], replicated, may hold values from -3 to 3
- gain_two: float32 [768], replicated, may hold values from 0.25 to 1.75
- bias_two: float32 [768], replicated, may hold values from -3 to 3
- fc1_weight: bfloat16 [768, 3072], replicated, may hold values from -0.21875 to 0.21875
- fc1_bias: float32 [3072], replicated, may hold values from -3 to 3
- fc2_weight: bfloat16 [3072, 768], replicated, may hold values from -0.15625 to 0.15625
- fc2_bias: float32 [768], replicated, may hold values from -3 to 3
- cotangent: bfloat16 [16, 1024, 768], P('dp', 'tile'), may hold values from -6 to 6
Outputs:
- output: bfloat16 [16, 1024, 768], P('dp', 'tile')
- grad_tokens: bfloat16 [16, 1024, 768], P('dp', 'tile')
- gain_one_grad: float32 [768], replicated
- bias_one_grad: float32 [768], replicated
- qkv_grad: float32 [768, 2304], P('dp', 'tile')
- query_bias_grad: float32 [768], replicated
- value_bias_grad: float32 [768], replicated
- out_grad: float32 [768, 768], P('dp', 'tile')
- out_bias_grad: float32 [768], replicated
- gain_two_grad: float32 [768], replicated
- bias_two_grad: float32 [768], replicated
- fc1_grad: float32 [768, 3072], P('dp', 'tile')
- fc1_bias_grad: float32 [3072], replicated
- fc2_grad: float32 [3072, 768], P('dp', 'tile')
- fc2_bias_grad: float32 [768], replicated
- root_mean: float32 [4], replicated
The draws below stay inside these ranges and needn't reach their ends.
Inputs may be any that keep to these rules, and one draw needn't show every extreme that they name: `segment_ids`: within a sequence the ids never fall; each of the 8 images has 1 to 256 slots, and one has exactly 256.
All inputs are finite; a program needn't handle non-finite values. No bound on the sum of `keep_mask` on one device may be relied on, other than what follows from the above.
Results may differ from the reference program's by a relative error of at most 0.017.
Values may be sent and summed in bfloat16 or wider, within the bound.
A program may use at most 192 MiB of HBM per device.

```python
import math
import jax
import jax.numpy as jnp
import numpy as np
from jax import lax

D = 768
HEADS = 12
HEAD_DIM = 64
FF = 3072
L = 1024
IMAGES = 8
SEQ_DEV = 1
MOST = 256
SEQS = 16
N_DP = 16


def draw_tokens(key, part):
    level_key = jax.random.fold_in(key, 11)
    noise_key = jax.random.fold_in(key, 23)
    steps = jnp.arange(SEQS, dtype=jnp.float32) / max(SEQS - 1, 1)
    jitter = jax.random.uniform(level_key, (SEQS,), jnp.float32, 0.85, 1.15)
    level = 0.6 * jnp.exp(steps * math.log(3.0)) * jitter
    noise = jax.random.truncated_normal(noise_key, -5.0, 5.0, (SEQS, L, D), jnp.float32)
    return (level[:, None, None] * noise).astype(jnp.bfloat16)


def plant(drawn, own_key, least, high):
    longest = drawn.shape.index(max(drawn.shape))
    spots = []
    for shift in (0, 1):
        where = [jax.random.randint(jax.random.fold_in(own_key, axis), (), 0, length) for axis, length in enumerate(drawn.shape)]
        where[longest] = (where[longest] + shift) % drawn.shape[longest]
        spots.append(tuple(where))
    return drawn.at[spots[0]].set(least).at[spots[1]].set(high)


def block_scale(stream_key, shape, pieces, low, high):
    def one(dim, parts):
        draws = jax.random.uniform(jax.random.fold_in(jax.random.fold_in(stream_key, 6), dim), (parts,), jnp.float32, low / len(pieces), high / len(pieces))
        return jnp.repeat(jnp.exp(draws), shape[dim] // parts).reshape((-1,) + (1,) * (len(shape) - dim - 1))

    loudness = one(*pieces[0])
    for cut in pieces[1:]:
        loudness = loudness * one(*cut)
    return loudness


def split_up(number_of, total, most, lean):
    loads = [(1 << 20) // math.isqrt(standing ** lean) + 1 for standing in range(2, number_of + 1)]
    spare, counts = total - most - (number_of - 1), [1] * (number_of - 1)
    while spare > 0:
        candidates = [i for i in range(number_of - 1) if counts[i] < most]
        pool, budget = sum([loads[i] for i in candidates]), spare
        for i in candidates:
            extra = min(most - counts[i], max(1, budget * loads[i] // pool), spare)
            counts[i] = counts[i] + extra
            spare = spare - extra
    return np.array([most] + counts)


def uneven_parts(rng, number_of, total, limit, lean):
    if number_of == 2:
        one = jax.random.randint(rng, (), max(1, total - limit), min(limit, total - 1) + 1)
        return jnp.stack([one, total - one])
    lengths = jnp.asarray(split_up(number_of, total, limit, lean), jnp.int32)
    twos = (number_of - 1) // 2
    donor, receiver = lengths[1:1 + 2 * twos:2], lengths[2:2 + 2 * twos:2]
    slack = jnp.minimum(donor - 1, limit - receiver)
    passed = jax.random.randint(jax.random.fold_in(rng, 1), (twos,), 0, 1 << 20) % (slack + 1)
    lengths = lengths.at[1:1 + 2 * twos:2].set(donor - passed).at[2:2 + 2 * twos:2].set(receiver + passed)
    return lengths[jax.random.permutation(jax.random.fold_in(rng, 2), number_of)]


def bell_draw(rng, extent, width, most, shards=(), kind=jnp.bfloat16):
    values = width * jax.random.normal(rng, extent, jnp.float32)
    if shards:
        values = values * block_scale(rng, extent, shards, -0.22, 0.18)
    return jnp.clip(values, -most, most).astype(kind)


def setup_inputs(seed: int = 0) -> dict:
    key_of = jax.random.split(jax.random.key(seed), 18)
    tokens = draw_tokens(jax.random.fold_in(key_of[17], 71), 0)
    segment_ids = jax.vmap(lambda own: jnp.searchsorted(jnp.cumsum(uneven_parts(own, IMAGES, L, MOST, 1)), jnp.arange(L), side="right"))(jax.random.split(key_of[1], SEQS)).reshape((SEQS, L)).astype(jnp.int32)
    keep_mask = plant((jax.random.randint(key_of[2], (SEQS, L), 0, 64) < 59).astype(jnp.int32), jax.random.fold_in(key_of[2], 1), 0, 1)
    gain_one = jnp.clip(1.0 + 0.15 * jax.random.normal(key_of[3], (D,), jnp.float32), 0.25, 1.75)
    bias_one = bell_draw(key_of[4], (D,), 0.5, 3.0, (), jnp.float32)
    qkv_weight = bell_draw(key_of[5], (D, 3 * D), D ** -0.5, 0.21875)
    query_bias = bell_draw(key_of[6], (D,), 0.5, 3.0, (), jnp.float32)
    value_bias = bell_draw(key_of[7], (D,), 0.5, 3.0, (), jnp.float32)
    out_weight = bell_draw(key_of[8], (D, D), (max(D // 96, 2)) ** -0.5, 2.0)
    out_bias = bell_draw(key_of[9], (D,), 0.5, 3.0, (), jnp.float32)
    gain_two = jnp.clip(1.0 + 0.15 * jax.random.normal(key_of[10], (D,), jnp.float32), 0.25, 1.75)
    bias_two = bell_draw(key_of[11], (D,), 0.5, 3.0, (), jnp.float32)
    fc1_weight = bell_draw(key_of[12], (D, FF), D ** -0.5, 0.21875)
    fc1_bias = bell_draw(key_of[13], (FF,), 0.5, 3.0, (), jnp.float32)
    fc2_weight = bell_draw(key_of[14], (FF, D), (FF // 2) ** -0.5, 0.15625)
    fc2_bias = bell_draw(key_of[15], (D,), 0.5, 3.0, (), jnp.float32)
    cotangent = bell_draw(key_of[16], (SEQS, L, D), 1.0, 6.0, ((0, 16), (1, 2)))
    return dict(tokens=tokens, segment_ids=segment_ids, keep_mask=keep_mask, gain_one=gain_one, bias_one=bias_one, qkv_weight=qkv_weight, query_bias=query_bias, value_bias=value_bias, out_weight=out_weight, out_bias=out_bias, gain_two=gain_two, bias_two=bias_two, fc1_weight=fc1_weight, fc1_bias=fc1_bias, fc2_weight=fc2_weight, fc2_bias=fc2_bias, cotangent=cotangent)


@jax.custom_vjp
def low(v):
    return lax.optimization_barrier(v.astype(jnp.bfloat16)).astype(jnp.float32)

@jax.custom_vjp
def low_back(v):
    return v

def low_keep(v):
    return (low(v), None)

def low_pass(kept, grad):
    return (grad,)

def back_keep(v):
    return (v, None)

def back_low(kept, grad):
    return (low(grad),)
low.defvjp(low_keep, low_pass)
low_back.defvjp(back_keep, back_low)

def layer_norm(values, norm_gain, norm_bias):
    average = lax.optimization_barrier(jnp.mean(values, axis=-1, keepdims=True))
    centred = values - average
    variance = lax.optimization_barrier(jnp.mean(centred * centred, axis=-1, keepdims=True))
    return centred * lax.rsqrt(variance + 1e-06) * norm_gain + norm_bias

def project(values, matrix):
    return jnp.einsum('gld,de->gle', values, matrix, precision=lax.Precision.HIGHEST)

def block_forward(params, values, segment, keeping):
    gain_one, bias_one, qkv_weight, query_bias, value_bias, out_weight, out_bias, gain_two, bias_two, fc1_weight, fc1_bias, fc2_weight, fc2_bias = params
    groups = values.shape[0]
    normed = low(layer_norm(values, gain_one, bias_one))
    key_bias = jnp.zeros_like(query_bias)
    projected = project(normed, qkv_weight) + jnp.concatenate([query_bias, key_bias, value_bias])
    projected = low(low_back(projected))
    queries = projected[..., :D].reshape(groups, L, HEADS, HEAD_DIM)
    keys_all = projected[..., D:2 * D].reshape(groups, L, HEADS, HEAD_DIM)
    values_all = projected[..., 2 * D:].reshape(groups, L, HEADS, HEAD_DIM)
    scores = jnp.einsum('gqhe,gkhe->ghqk', queries, keys_all, precision=lax.Precision.HIGHEST) * HEAD_DIM ** (-0.5)
    scores = low_back(scores)
    places = jnp.arange(L, dtype=jnp.int32)
    same_image = segment[:, :, None] == segment[:, None, :]
    usable = (keeping[:, None, :] == 1) | (places[:, None] == places[None, :])[None]
    allowed = (same_image & usable)[:, None]
    masked = jnp.where(allowed, scores, -1e+30)
    shifted = masked - lax.optimization_barrier(jnp.max(masked, axis=-1, keepdims=True))
    exponent = jnp.exp(shifted)
    probs = low(exponent / lax.optimization_barrier(jnp.sum(exponent, axis=-1, keepdims=True)))
    attended = jnp.einsum('ghqk,gkhe->gqhe', probs, values_all, precision=lax.Precision.HIGHEST).reshape(groups, L, D)
    attended = low(low_back(attended))
    branch_one = low_back(project(attended, out_weight) + out_bias)
    hidden = values + branch_one
    normed_two = low(layer_norm(hidden, gain_two, bias_two))
    inner = low_back(project(normed_two, fc1_weight) + fc1_bias)
    active = low(jax.nn.gelu(inner, approximate=False))
    branch_two = project(active, fc2_weight) + fc2_bias
    result = hidden + branch_two
    weighting = keeping.astype(jnp.float32)[..., None]
    squares = [jnp.sum(weighting * member * member) for member in (values, branch_one, branch_two, result)]
    sums = jnp.stack(squares + [jnp.sum(weighting)])
    return (result, sums)

def reference(tokens, segment_ids, keep_mask, gain_one, bias_one, qkv_weight, query_bias, value_bias, out_weight, out_bias, gain_two, bias_two, fc1_weight, fc1_bias, fc2_weight, fc2_bias, cotangent):
    weights = (gain_one, bias_one, qkv_weight, query_bias, value_bias, out_weight, out_bias, gain_two, bias_two, fc1_weight, fc1_bias, fc2_weight, fc2_bias)
    floats = tuple((member.astype(jnp.float32) for member in weights))
    shaped_ids = segment_ids.reshape(N_DP, SEQ_DEV, L)
    shaped_keep = keep_mask.reshape(N_DP, SEQ_DEV, L)
    blocked = jax.checkpoint(block_forward)

    def forward(values, *params):
        shaped = values.reshape(N_DP, SEQ_DEV, L, D)

        def advance(carry, items):
            block, segment, keeping = items
            result, sums = blocked(params, block, segment, keeping)
            return (carry + sums, result)
        totals, results = lax.scan(advance, jnp.zeros((5,), jnp.float32), (shaped, shaped_ids, shaped_keep))
        return (results.reshape(SEQS, L, D), totals)
    output, backward, totals = jax.vjp(forward, tokens.astype(jnp.float32), *floats, has_aux=True)
    gradients = backward(cotangent.astype(jnp.float32))
    root_mean = jnp.sqrt(totals[:4] / (totals[4] * D))
    return (output.astype(jnp.bfloat16), gradients[0].astype(jnp.bfloat16), gradients[1], gradients[2], gradients[3], gradients[4], gradients[5], gradients[6], gradients[7], gradients[8], gradients[9], gradients[10], gradients[11], gradients[12], gradients[13], root_mean)
```

```python
import jax
import jax.numpy as jnp
from jax import lax
from jax.experimental import pallas as pl
from jax.experimental.pallas import tpu as pltpu
from jax.sharding import PartitionSpec as P

HEAD_DIM = 64
PAIR = 2 * HEAD_DIM
MASKED = -1e30
MESH = pl.DeviceIdType.MESH
BF = jnp.bfloat16
F32 = jnp.float32
NT = (((1,), (1,)), ((), ()))
TN = (((0,), (0,)), ((), ()))


def mm(a, b):
    return jnp.dot(a, b, preferred_element_type=F32)


def mm_nt(a, b):
    return lax.dot_general(a, b, NT, preferred_element_type=F32)


def mm_tn(a, b):
    return lax.dot_general(a, b, TN, preferred_element_type=F32)


def any_spec():
    return pl.BlockSpec(memory_space=pl.ANY)


def vmem_spec():
    return pl.BlockSpec(memory_space=pltpu.VMEM)


def attention_forward(
    tok, info, gain, bias, w_hbm, pbias, proj_out, norm_out, att_out, lse_out,
    x, w, proj, norm, att, lse, mask, sems, send_sem, recv_sem,
):
    rows, width = norm.shape
    half = rows // 2
    heads = width // HEAD_DIM
    t = lax.axis_index("tile")
    far, near = t * half, (1 - t) * half
    barrier = pltpu.get_barrier_semaphore()
    pl.semaphore_signal(barrier, inc=1, device_id={"tile": 1 - t}, device_id_type=MESH)
    load_far = pltpu.make_async_copy(tok.at[pl.ds(far, half)], x.at[pl.ds(0, half)], sems.at[0])
    load_near = pltpu.make_async_copy(tok.at[pl.ds(near, half)], x.at[pl.ds(half, half)], sems.at[1])
    load_w = pltpu.make_async_copy(w_hbm, w, sems.at[2])
    load_far.start()
    load_near.start()
    load_w.start()
    pl.semaphore_wait(barrier, 1)
    halo = pltpu.make_async_remote_copy(
        tok.at[pl.ds(near, half)], x.at[pl.ds(rows, half)], send_sem, recv_sem,
        device_id={"tile": 1 - t}, device_id_type=MESH,
    )
    halo.start()

    seg_row = info[1:2, :]
    seg_col = jnp.transpose(info[...].astype(F32))[:, 0:1].astype(jnp.int32)
    key_at = lax.broadcasted_iota(jnp.int32, (half, rows + half), 1)
    for part in range(2):
        query_at = lax.broadcasted_iota(jnp.int32, (half, rows + half), 0) + part * half
        same = seg_col[part * half : (part + 1) * half] == seg_row
        mask[pl.ds(part * half, half), :] = jnp.where(same | (query_at == key_at), 0.0, MASKED)

    def normalize(start, count):
        step = 128

        def one(i, _):
            at = pl.ds(pl.multiple_of(start + i * step, step), step)
            v = x[at, :].astype(F32)
            centred = v - jnp.mean(v, axis=-1, keepdims=True)
            var = jnp.mean(centred * centred, axis=-1, keepdims=True)
            norm_at = centred * lax.rsqrt(var + 1e-06) * gain[...] + bias[...]
            x[at, :] = norm_at.astype(BF)
            return 0

        lax.fori_loop(0, count // step, one, 0)

    def project(start, count):
        cols = 768

        def one(i, _):
            at = pl.ds(pl.multiple_of(i * cols, cols), cols)
            block = mm(x[pl.ds(start, count), :], w[:, at]) + pbias[:, at]
            low = block.astype(BF)
            scale = jnp.where(i * cols < width, HEAD_DIM ** (-0.5), 1.0).astype(BF)
            proj[pl.ds(start, count), at] = low * scale
            return 0

        lax.fori_loop(0, 3 * width // cols, one, 0)

    lane = lax.broadcasted_iota(jnp.int32, (1, PAIR), 1)
    low_half = lane < HEAD_DIM

    def attend(start, keys):
        def one(p, _):
            at = pl.multiple_of(p * PAIR, PAIR)
            q = proj[pl.ds(start, half), pl.ds(at, PAIR)]
            k = proj[pl.ds(0, keys), pl.ds(width + at, PAIR)]
            v = proj[pl.ds(0, keys), pl.ds(2 * width + at, PAIR)]
            total = None
            tops = []
            for head in range(2):
                mine = low_half if head == 0 else ~low_half
                qh = jnp.where(mine, q, 0).astype(BF)
                s = mm_nt(qh, k) + mask[pl.ds(start, half), pl.ds(0, keys)]
                top = jnp.max(s, axis=-1, keepdims=True)
                e = jnp.exp(s - top).astype(BF)
                ones = jnp.broadcast_to(jnp.where(mine, 1.0, 0.0).astype(BF), (keys, PAIR))
                vh = jnp.concatenate([jnp.where(mine, v, 0).astype(BF), ones], axis=1)
                part = mm(e, vh)
                total = part if total is None else total + part
                tops.append(top)
            sums = total[:, PAIR:]
            att[pl.ds(start, half), pl.ds(at, PAIR)] = (total[:, :PAIR] / sums).astype(BF)
            logs = jnp.log(sums)
            lane_of = lax.broadcasted_iota(jnp.int32, (half, PAIR), 1)
            acc = lse[pl.ds(start, half), :]
            acc = jnp.where(lane_of == 2 * p, tops[0] + logs[:, 0:1], acc)
            acc = jnp.where(lane_of == 2 * p + 1, tops[1] + logs[:, HEAD_DIM : HEAD_DIM + 1], acc)
            lse[pl.ds(start, half), :] = acc
            return 0

        lax.fori_loop(0, heads // 2, one, 0, unroll=6)

    lse[...] = jnp.zeros_like(lse)
    load_far.wait()
    load_near.wait()
    normalize(0, rows)
    norm_copy = pltpu.make_async_copy(x.at[pl.ds(0, rows)], norm_out, sems.at[0])
    norm_copy.start()
    load_w.wait()
    project(0, rows)
    attend(0, rows)
    halo.wait()
    normalize(rows, half)
    project(rows, half)
    proj_copy = pltpu.make_async_copy(proj, proj_out, sems.at[1])
    proj_copy.start()
    attend(half, rows + half)
    att_copy = pltpu.make_async_copy(att, att_out, sems.at[2])
    att_copy.start()
    lse_out[...] = jnp.transpose(lse[...])[:16, :]
    norm_copy.wait()
    proj_copy.wait()
    att_copy.wait()


def call_forward(tokens, info, gain, bias, w, pbias):
    rows, width = tokens.shape
    half = rows // 2
    sds = jax.ShapeDtypeStruct
    return pl.pallas_call(
        attention_forward,
        out_shape=(
            sds((rows + half, 3 * width), BF),
            sds((rows, width), BF),
            sds((rows, width), BF),
            sds((16, rows), F32),
        ),
        in_specs=[any_spec(), vmem_spec(), vmem_spec(), vmem_spec(), any_spec(), vmem_spec()],
        out_specs=(any_spec(), any_spec(), any_spec(), vmem_spec()),
        scratch_shapes=[
            pltpu.VMEM((rows + half, width), BF),
            pltpu.VMEM((width, 3 * width), BF),
            pltpu.VMEM((rows + half, 3 * width), BF),
            pltpu.VMEM((rows, width), BF),
            pltpu.VMEM((rows, width), BF),
            pltpu.VMEM((rows, PAIR), F32),
            pltpu.VMEM((rows, rows + half), F32),
            pltpu.SemaphoreType.DMA((3,)),
            pltpu.SemaphoreType.DMA,
            pltpu.SemaphoreType.DMA,
        ],
        compiler_params=pltpu.CompilerParams(collective_id=0, has_side_effects=True, vmem_limit_bytes=60 << 20),
        name="attention_forward",
    )(tokens, info, gain, bias, w, pbias)


def gelu_and_slope(z):
    bell = jnp.exp(z * z * -0.5)
    t = 1.0 / (1.0 + jnp.abs(z) * (0.3275911 * 0.7071067811865476))
    tail = t * (0.127414796 + t * (-0.142248368 + t * (0.7107068705 + t * (-0.7265760135 + t * 0.5307027145)))) * bell
    upper = jnp.where(z >= 0, 1.0 - tail, tail)
    return z * upper, upper + z * bell * 0.3989422804014327


def mlp(
    tok, att_hbm, dy_hbm, keep_col, ow_hbm, ob, g2, b2, w1_hbm, b1, w2_hbm, c2,
    out_hbm, dh_hbm, db_hbm, da_hbm, delta_out, f1_hbm, f2_hbm, vec_out, b1g_out,
    x, att, dy, ow, w1, w2, hidden, xhat, rstd, n2, n2t, z, da, act, di, acc, dn, f1, f2, obuf, sems,
):
    rows, width = hidden.shape
    half = rows // 2
    chunks, _, cols = w1.shape
    t = lax.axis_index("tile")
    far, near = t * half, (1 - t) * half
    copies = []

    def fetch(src, dst, i):
        c = pltpu.make_async_copy(src, dst, sems.at[i])
        c.start()
        return c

    got_att = fetch(att_hbm, att, 0)
    got_ow = fetch(ow_hbm, ow, 1)
    got_x = [fetch(tok.at[pl.ds(far, half)], x.at[pl.ds(0, half)], 2), fetch(tok.at[pl.ds(near, half)], x.at[pl.ds(half, half)], 3)]
    got_dy = [fetch(dy_hbm.at[pl.ds(far, half)], dy.at[pl.ds(0, half)], 4), fetch(dy_hbm.at[pl.ds(near, half)], dy.at[pl.ds(half, half)], 5)]
    got_w = []
    for c in range(chunks):
        got_w.append(fetch(w1_hbm.at[:, pl.ds(c * cols, cols)], w1.at[c], 6 + c))
        got_w.append(fetch(w2_hbm.at[pl.ds(c * cols, cols)], w2.at[c], 6 + chunks + c))
    got_att.wait()
    got_ow.wait()
    for g in got_x:
        g.wait()
    rb = 128
    vec_out[...] = jnp.zeros_like(vec_out)

    def add_vec(i, v):
        vec_out[i : i + 1, :] += jnp.sum(v, axis=0, keepdims=True)

    def front(i, _):
        at = pl.ds(pl.multiple_of(i * rb, rb), rb)
        branch = mm(att[at, :], ow[...]) + ob[...]
        xs = x[at, :].astype(F32)
        h = xs + branch
        hidden[at, :] = h
        kept = keep_col[at, :][:, 0:1]
        add_vec(0, kept * xs * xs)
        add_vec(1, kept * branch * branch)
        centred = h - jnp.mean(h, axis=-1, keepdims=True)
        r = lax.rsqrt(jnp.mean(centred * centred, axis=-1, keepdims=True) + 1e-06)
        xh = centred * r
        xhat[at, :] = xh
        rstd[at, :] = jnp.broadcast_to(r, (rb, 128))
        n2[at, :] = (xh * g2[...] + b2[...]).astype(BF)
        return 0

    lax.fori_loop(0, rows // rb, front, 0)
    n2t[...] = jnp.transpose(n2[...])
    acc[...] = jnp.zeros_like(acc)
    dn[...] = jnp.zeros_like(dn)
    for g in got_dy:
        g.wait()
    for c in range(2 * chunks):
        got_w[c].wait()

    def chunk(c, _):
        w1c, w2c = w1.at[c], w2.at[c]
        z[...] = mm(n2[...], w1c[...]) + b1[c]
        da[...] = mm_nt(dy[...], w2c[...])
        gr = 64
        bsum = jnp.zeros((1, cols), F32)
        for i in range(rows // gr):
            at = pl.ds(i * gr, gr)
            a, s = gelu_and_slope(z[at, :])
            act[at, :] = a.astype(BF)
            d = (da[at, :] * s).astype(BF)
            di[at, :] = d
            bsum = bsum + jnp.sum(d.astype(F32), axis=0, keepdims=True)
        b1g_out[c] = bsum
        acc[...] += mm(act[...], w2c[...])
        dn[...] += mm_nt(di[...], w1c[...])
        f1[c] = mm(n2t[...], di[...]).astype(BF)
        f2[c] = mm_tn(act[...], dy[...]).astype(BF)
        return 0

    lax.fori_loop(0, chunks, chunk, 0, unroll=1)

    def back(i, _):
        at = pl.ds(pl.multiple_of(i * rb, rb), rb)
        branch = acc[at, :] + c2[...]
        result = hidden[at, :] + branch
        obuf[at, :] = result.astype(BF)
        kept = keep_col[at, :][:, 0:1]
        add_vec(2, kept * branch * branch)
        add_vec(3, kept * result * result)
        g = dn[at, :]
        xh = xhat[at, :]
        add_vec(4, g * xh)
        add_vec(5, g)
        gy = g * g2[...]
        mean_gy = jnp.mean(gy, axis=-1, keepdims=True)
        mean_gx = jnp.mean(gy * xh, axis=-1, keepdims=True)
        dys = dy[at, :].astype(F32)
        add_vec(7, dys)
        dh = dys + rstd[at, :][:, 0:1] * (gy - mean_gy - xh * mean_gx)
        hidden[at, :] = dh
        low = dh.astype(BF)
        n2[at, :] = low
        add_vec(6, low.astype(F32))
        return 0

    lax.fori_loop(0, rows // rb, back, 0)
    copies.append(fetch(obuf.at[pl.ds(0, half)], out_hbm.at[pl.ds(far, half)], 0))
    copies.append(fetch(obuf.at[pl.ds(half, half)], out_hbm.at[pl.ds(near, half)], 1))
    copies.append(fetch(hidden, dh_hbm, 2))
    copies.append(fetch(n2, db_hbm, 3))
    copies.append(fetch(f1, f1_hbm, 4))
    copies.append(fetch(f2, f2_hbm, 5))
    d_att = mm_nt(n2[...], ow[...])
    x[...] = d_att.astype(BF)
    copies.append(fetch(x, da_hbm, 6))
    heads = width // HEAD_DIM
    head_of = lax.broadcasted_iota(jnp.int32, (16, width), 1) // HEAD_DIM
    mine = (head_of == lax.broadcasted_iota(jnp.int32, (16, width), 0)).astype(F32).astype(BF)
    prod = x[...].astype(F32) * att[...].astype(F32)
    hi = prod.astype(BF)
    lo = (prod - hi.astype(F32)).astype(BF)
    delta_out[...] = mm_nt(mine, hi) + mm_nt(mine, lo)
    for c in copies:
        c.wait()


def call_mlp(tokens, att, dy, keep_col, ow, ob, g2, b2, w1, b1, w2, c2):
    rows, width = tokens.shape
    hid = w1.shape[1]
    cols = width
    chunks = hid // cols
    sds = jax.ShapeDtypeStruct
    V = pltpu.VMEM
    return pl.pallas_call(
        mlp,
        out_shape=(
            sds((rows, width), BF), sds((rows, width), F32), sds((rows, width), BF), sds((rows, width), BF),
            sds((16, rows), F32), sds((chunks, width, cols), BF), sds((chunks, cols, width), BF),
            sds((8, width), F32), sds((chunks, 1, cols), F32),
        ),
        in_specs=[any_spec(), any_spec(), any_spec(), vmem_spec(), any_spec(), vmem_spec(), vmem_spec(), vmem_spec(), any_spec(), vmem_spec(), any_spec(), vmem_spec()],
        out_specs=(any_spec(),) * 4 + (vmem_spec(), any_spec(), any_spec(), vmem_spec(), vmem_spec()),
        scratch_shapes=[
            V((rows, width), BF), V((rows, width), BF), V((rows, width), BF), V((width, width), BF),
            V((chunks, width, cols), BF), V((chunks, cols, width), BF),
            V((rows, width), F32), V((rows, width), F32), V((rows, 128), F32), V((rows, width), BF), V((width, rows), BF),
            V((rows, cols), F32), V((rows, cols), F32), V((rows, cols), BF), V((rows, cols), BF),
            V((rows, width), F32), V((rows, width), F32), V((chunks, width, cols), BF), V((chunks, cols, width), BF),
            V((rows, width), BF),
            pltpu.SemaphoreType.DMA((6 + 2 * chunks,)),
        ],
        compiler_params=pltpu.CompilerParams(vmem_limit_bytes=62 << 20),
        name="feed_forward",
    )(tokens, att, dy, keep_col, ow, ob, g2, b2, w1, b1.reshape(chunks, 1, cols), w2, c2)


def attention_backward(
    tok, info, gain, proj_hbm, norm_hbm, att_hbm, dh_hbm, db_hbm, da_hbm, lse, delta, w_hbm,
    gt_hbm, qg_hbm, og_hbm, vec_out,
    x, proj, norm, att, dh, db, da, w, normt, attt, stat, mask, near_key, near_query, dk, dv, dproj, dn, qg, og, obuf, sems, send_sems, recv_sems,
):
    rows, width = norm.shape
    half = rows // 2
    heads = width // HEAD_DIM
    t = lax.axis_index("tile")
    far, near = t * half, (1 - t) * half
    barrier = pltpu.get_barrier_semaphore()
    pl.semaphore_signal(barrier, inc=1, device_id={"tile": 1 - t}, device_id_type=MESH)

    def fetch(src, dst, i):
        c = pltpu.make_async_copy(src, dst, sems.at[i])
        c.start()
        return c

    got_proj = fetch(proj_hbm, proj, 0)
    got_da = fetch(da_hbm, da.at[pl.ds(0, rows)], 1)
    got_att = fetch(att_hbm, att, 2)
    got_db = fetch(db_hbm, db, 3)
    got_norm = fetch(norm_hbm, norm, 4)
    got_w = fetch(w_hbm, w, 5)
    got_dh = fetch(dh_hbm, dh, 6)
    got_x = [fetch(tok.at[pl.ds(far, half)], x.at[pl.ds(0, half)], 7), fetch(tok.at[pl.ds(near, half)], x.at[pl.ds(half, half)], 8)]
    pl.semaphore_wait(barrier, 1)
    halos = []
    for i, (src, dst) in enumerate(
        (
            (da_hbm.at[pl.ds(half, half)], da.at[pl.ds(rows, half)]),
            (lse.at[:, pl.ds(half, half)], stat.at[0]),
            (delta.at[:, pl.ds(half, half)], stat.at[1]),
        )
    ):
        h = pltpu.make_async_remote_copy(src, dst, send_sems.at[i], recv_sems.at[i], device_id={"tile": 1 - t}, device_id_type=MESH)
        h.start()
        halos.append(h)

    seg_row = info[0:1, :]
    key_col = jnp.transpose(info[...].astype(F32))[:, 1:2].astype(jnp.int32)
    key_at = lax.broadcasted_iota(jnp.int32, (half, rows), 0)
    query_at = lax.broadcasted_iota(jnp.int32, (half, rows), 1)
    for part in range(2):
        same = key_col[part * half : (part + 1) * half] == seg_row[:, :rows]
        mask[pl.ds(part * half, half), :] = jnp.where(same | (query_at == key_at + part * half), 0.0, MASKED)
    near_key[...] = jnp.where(key_col[half:rows] == seg_row[:, rows:], 0.0, MASKED)
    near_query[...] = jnp.where(key_col[rows:] == seg_row[:, half:rows], 0.0, MASKED)
    got_att.wait()
    attt[...] = jnp.transpose(att[...])
    got_db.wait()
    og[...] = mm(attt[...], db[...]).astype(BF)
    got_norm.wait()
    normt[...] = jnp.transpose(norm[...])
    got_proj.wait()
    got_da.wait()

    lane = lax.broadcasted_iota(jnp.int32, (1, PAIR), 1)

    def cut(v, head):
        return jnp.where((lane < HEAD_DIM) == (head == 0), v, 0).astype(BF)

    def own(p, _):
        at = pl.multiple_of(p * PAIR, PAIR)
        col = pl.ds(at, PAIR)
        kcol, vcol = pl.ds(width + at, PAIR), pl.ds(2 * width + at, PAIR)
        q, k, v = proj[pl.ds(0, rows), col], proj[:, kcol], proj[:, vcol]
        do = da[pl.ds(0, rows), col]
        gq = gk = gv = gn = None
        for head in range(2):
            qh, kh, doh = cut(q, head), cut(k, head), cut(do, head)
            ls = lse[pl.ds(2 * p + head, 1), :]
            de = delta[pl.ds(2 * p + head, 1), :]
            s = mm_nt(k[:rows], qh) + mask[...]
            prob = jnp.exp(s - ls)
            dp = mm_nt(v[:rows], doh)
            ds = (prob * (dp - de)).astype(BF)
            low = prob.astype(BF)
            a = mm(low, doh)
            b = mm(ds, qh)
            c = mm_tn(ds, kh[:rows])
            s2 = mm_nt(k[rows:], qh[half:]) + near_query[...]
            prob2 = jnp.exp(s2 - ls[:, half:])
            dp2 = mm_nt(v[rows:], doh[half:])
            ds2 = (prob2 * (dp2 - de[:, half:])).astype(BF)
            d = mm_tn(ds2, kh[rows:])
            gv = a if gv is None else gv + a
            gk = b if gk is None else gk + b
            gq = c if gq is None else gq + c
            gn = d if gn is None else gn + d
        scale = HEAD_DIM ** (-0.5)
        dproj[pl.ds(0, half), col] = (gq[:half] * scale).astype(BF)
        dproj[pl.ds(half, half), col] = ((gq[half:] + gn) * scale).astype(BF)
        dproj[pl.ds(0, half), kcol] = gk[:half].astype(BF)
        dproj[pl.ds(0, half), vcol] = gv[:half].astype(BF)
        dk[:, col] = gk[half:]
        dv[:, col] = gv[half:]
        return 0

    def halo(p, _):
        at = pl.multiple_of(p * PAIR, PAIR)
        col = pl.ds(at, PAIR)
        kcol, vcol = pl.ds(width + at, PAIR), pl.ds(2 * width + at, PAIR)
        q, k, v = proj[pl.ds(rows, half), col], proj[pl.ds(half, half), kcol], proj[pl.ds(half, half), vcol]
        do = da[pl.ds(rows, half), col]
        gk, gv = dk[:, col], dv[:, col]
        for head in range(2):
            qh, doh = cut(q, head), cut(do, head)
            ls = stat[0, pl.ds(2 * p + head, 1), :]
            de = stat[1, pl.ds(2 * p + head, 1), :]
            prob = jnp.exp(mm_nt(k, qh) + near_key[...] - ls)
            ds = (prob * (mm_nt(v, doh) - de)).astype(BF)
            gv = gv + mm(prob.astype(BF), doh)
            gk = gk + mm(ds, qh)
        dproj[pl.ds(half, half), kcol] = gk.astype(BF)
        dproj[pl.ds(half, half), vcol] = gv.astype(BF)
        return 0

    lax.fori_loop(0, heads // 2, own, 0, unroll=6)
    for h in halos:
        h.wait()
    lax.fori_loop(0, heads // 2, halo, 0, unroll=6)
    got_w.wait()
    got_dh.wait()
    for g in got_x:
        g.wait()
    vec_out[...] = jnp.zeros_like(vec_out)

    def add_vec(i, v):
        vec_out[i : i + 1, :] += jnp.sum(v, axis=0, keepdims=True)

    for j in range(3):
        cols = pl.ds(j * width, width)
        qg[j] = mm(normt[...], dproj[:, cols]).astype(BF)
    dn[...] = mm_nt(dproj[...], w[...])
    rb = 128

    def back(i, _):
        at = pl.ds(pl.multiple_of(i * rb, rb), rb)
        xs = x[at, :].astype(F32)
        centred = xs - jnp.mean(xs, axis=-1, keepdims=True)
        r = lax.rsqrt(jnp.mean(centred * centred, axis=-1, keepdims=True) + 1e-06)
        xh = centred * r
        g = dn[at, :]
        add_vec(0, g * xh)
        add_vec(1, g)
        gy = g * gain[...]
        mean_gy = jnp.mean(gy, axis=-1, keepdims=True)
        mean_gx = jnp.mean(gy * xh, axis=-1, keepdims=True)
        obuf[at, :] = (dh[at, :] + r * (gy - mean_gy - xh * mean_gx)).astype(BF)
        add_vec(2, dproj[at, pl.ds(0, width)].astype(F32))
        add_vec(3, dproj[at, pl.ds(2 * width, width)].astype(F32))
        return 0

    lax.fori_loop(0, rows // rb, back, 0)
    copies = [
        fetch(obuf.at[pl.ds(0, half)], gt_hbm.at[pl.ds(far, half)], 0),
        fetch(obuf.at[pl.ds(half, half)], gt_hbm.at[pl.ds(near, half)], 1),
        fetch(qg, qg_hbm, 2),
        fetch(og, og_hbm, 3),
    ]
    for c in copies:
        c.wait()


def call_backward(tokens, info, gain, proj, norm, att, dh, db, da, lse, delta, w):
    rows, width = tokens.shape
    half = rows // 2
    sds = jax.ShapeDtypeStruct
    V = pltpu.VMEM
    return pl.pallas_call(
        attention_backward,
        out_shape=(sds((rows, width), BF), sds((3, width, width), BF), sds((width, width), BF), sds((8, width), F32)),
        in_specs=[any_spec(), vmem_spec(), vmem_spec()] + [any_spec()] * 6 + [vmem_spec(), vmem_spec(), any_spec()],
        out_specs=(any_spec(),) * 3 + (vmem_spec(),),
        scratch_shapes=[
            V((rows, width), BF), V((rows + half, 3 * width), BF), V((rows, width), BF), V((rows, width), BF),
            V((rows, width), F32), V((rows, width), BF), V((rows + half, width), BF), V((width, 3 * width), BF),
            V((width, rows), BF), V((width, rows), BF), V((2, 16, half), F32),
            V((rows, rows), F32), V((half, half), F32), V((half, half), F32),
            V((half, width), F32), V((half, width), F32), V((rows, 3 * width), BF), V((rows, width), F32),
            V((3, width, width), BF), V((width, width), BF), V((rows, width), BF),
            pltpu.SemaphoreType.DMA((9,)), pltpu.SemaphoreType.DMA((3,)), pltpu.SemaphoreType.DMA((3,)),
        ],
        compiler_params=pltpu.CompilerParams(collective_id=1, has_side_effects=True, vmem_limit_bytes=62 << 20),
        name="attention_backward",
    )(tokens, info, gain, proj, norm, att, dh, db, da, lse, delta, w)


def layer_norm(values, norm_gain, norm_bias):
    average = jnp.mean(values, axis=-1, keepdims=True)
    centred = values - average
    variance = jnp.mean(centred * centred, axis=-1, keepdims=True)
    return centred * lax.rsqrt(variance + 1e-06) * norm_gain + norm_bias


def exact_gelu(values):
    return jax.nn.gelu(values, approximate=False)


def on_device_general(
    tokens,
    segment_ids,
    keep_mask,
    gain_one,
    bias_one,
    qkv_weight,
    query_bias,
    value_bias,
    out_weight,
    out_bias,
    gain_two,
    bias_two,
    fc1_weight,
    fc1_bias,
    fc2_weight,
    fc2_bias,
    cotangent,
):
    sequences, tile_rows, model_width = tokens.shape
    length = segment_ids.shape[1]
    count_rows = sequences * tile_rows
    head_block = 4 * HEAD_DIM
    score_scale = HEAD_DIM ** (-0.5)
    offset = lax.axis_index("tile") * tile_rows
    query_ids = lax.dynamic_slice_in_dim(segment_ids, offset, tile_rows, 1)
    query_keep = lax.dynamic_slice_in_dim(keep_mask, offset, tile_rows, 1)
    positions = offset + jnp.arange(tile_rows, dtype=jnp.int32)
    key_places = jnp.arange(length, dtype=jnp.int32)
    own_slot = positions[:, None] == key_places[None, :]
    usable = (keep_mask[:, None, :] == 1) | own_slot[None]
    allowed = ((query_ids[:, :, None] == segment_ids[:, None, :]) & usable)[:, None]
    flattened = tokens.reshape(count_rows, model_width).astype(jnp.float32)
    normed = layer_norm(flattened, gain_one, bias_one)
    normed_low = normed.astype(jnp.bfloat16)
    key_bias = jnp.zeros_like(query_bias)
    projected = jnp.dot(
        normed_low, qkv_weight, preferred_element_type=jnp.float32
    ) + jnp.concatenate([query_bias, key_bias, value_bias])
    projected_low = projected.astype(jnp.bfloat16).reshape(sequences, tile_rows, 3 * model_width)
    queries = projected_low[..., :model_width]
    shared_local = projected_low[..., model_width:]
    shared_all = lax.all_gather(shared_local, "tile", axis=1, tiled=True)
    keys_all = shared_all[..., :model_width]
    values_all = shared_all[..., model_width:]
    key_count = shared_all.shape[1]

    def split_heads(source, column):
        sliced = source[..., column : column + head_block]
        return sliced.reshape(sliced.shape[0], sliced.shape[1], 4, HEAD_DIM)

    def block_scores(query_part, key_part):
        scores = (
            jnp.einsum("sqhe,skhe->shqk", query_part, key_part, preferred_element_type=jnp.float32)
            * score_scale
        )
        return jnp.where(allowed, scores, -1e30)

    attended_parts = []
    logsums = []
    for column in range(0, model_width, head_block):
        masked = block_scores(split_heads(queries, column), split_heads(keys_all, column))
        row_peak = jnp.max(masked, axis=-1, keepdims=True)
        exponent = jnp.exp(masked - row_peak)
        row_total = jnp.sum(exponent, axis=-1, keepdims=True)
        softmax_probs = (exponent / row_total).astype(jnp.bfloat16)
        logsums.append(row_peak + jnp.log(row_total))
        attended_parts.append(
            jnp.einsum(
                "shqk,skhe->sqhe",
                softmax_probs,
                split_heads(values_all, column),
                preferred_element_type=jnp.float32,
            )
        )
    attended = jnp.concatenate(attended_parts, axis=2)
    attended_low = attended.reshape(count_rows, model_width).astype(jnp.bfloat16)
    branch_one = jnp.dot(attended_low, out_weight, preferred_element_type=jnp.float32) + out_bias
    hidden = flattened + branch_one
    normed_two = layer_norm(hidden, gain_two, bias_two)
    normed_two_low = normed_two.astype(jnp.bfloat16)
    inner = jnp.dot(normed_two_low, fc1_weight, preferred_element_type=jnp.float32) + fc1_bias
    active_low = exact_gelu(inner).astype(jnp.bfloat16)
    branch_two = jnp.dot(active_low, fc2_weight, preferred_element_type=jnp.float32) + fc2_bias
    result = hidden + branch_two
    output = result.astype(jnp.bfloat16).reshape(sequences, tile_rows, model_width)
    weighting = query_keep.reshape(count_rows, 1).astype(jnp.float32)
    squares = [
        jnp.sum(weighting * member * member)
        for member in (flattened, branch_one, branch_two, result)
    ]
    stats = jnp.stack(squares + [jnp.sum(weighting)])
    grad_result = cotangent.reshape(count_rows, model_width)
    fc2_grad = jnp.einsum("nf,nd->fd", active_low, grad_result, preferred_element_type=jnp.float32)
    fc2_bias_grad = jnp.sum(grad_result.astype(jnp.float32), axis=0)
    grad_active = jnp.einsum(
        "nd,fd->nf", grad_result, fc2_weight, preferred_element_type=jnp.float32
    )
    inner_value, gelu_back = jax.vjp(exact_gelu, inner)
    grad_inner_low = gelu_back(grad_active)[0].astype(jnp.bfloat16)
    fc1_grad = jnp.einsum(
        "nd,nf->df", normed_two_low, grad_inner_low, preferred_element_type=jnp.float32
    )
    fc1_bias_grad = jnp.sum(grad_inner_low.astype(jnp.float32), axis=0)
    grad_normed_two = jnp.einsum(
        "nf,df->nd", grad_inner_low, fc1_weight, preferred_element_type=jnp.float32
    )
    normed_again, norm_back_two = jax.vjp(layer_norm, hidden, gain_two, bias_two)
    grad_hidden_part, gain_two_grad, bias_two_grad = norm_back_two(grad_normed_two)
    grad_hidden = grad_result.astype(jnp.float32) + grad_hidden_part
    grad_branch_low = grad_hidden.astype(jnp.bfloat16)
    out_grad = jnp.einsum(
        "nd,ne->de", attended_low, grad_branch_low, preferred_element_type=jnp.float32
    )
    out_bias_grad = jnp.sum(grad_branch_low.astype(jnp.float32), axis=0)
    grad_attended_low = (
        jnp.einsum("ne,de->nd", grad_branch_low, out_weight, preferred_element_type=jnp.float32)
        .astype(jnp.bfloat16)
        .reshape(sequences, tile_rows, model_width)
    )
    query_grads = []
    key_grads = []
    value_grads = []
    for block_index, column in enumerate(range(0, model_width, head_block)):
        query_part = split_heads(queries, column)
        key_part = split_heads(keys_all, column)
        value_part = split_heads(values_all, column)
        grad_part = split_heads(grad_attended_low, column)
        masked = block_scores(query_part, key_part)
        probs_again = jnp.exp(masked - logsums[block_index])
        grad_probs = jnp.einsum(
            "sqhe,skhe->shqk", grad_part, value_part, preferred_element_type=jnp.float32
        )
        centre = jnp.sum(probs_again * grad_probs, axis=-1, keepdims=True)
        grad_scores = (probs_again * (grad_probs - centre)).astype(jnp.bfloat16)
        query_grads.append(
            jnp.einsum("shqk,skhe->sqhe", grad_scores, key_part, preferred_element_type=jnp.float32)
            * score_scale
        )
        key_grads.append(
            jnp.einsum(
                "shqk,sqhe->skhe", grad_scores, query_part, preferred_element_type=jnp.float32
            )
            * score_scale
        )
        value_grads.append(
            jnp.einsum(
                "shqk,sqhe->skhe",
                probs_again.astype(jnp.bfloat16),
                grad_part,
                preferred_element_type=jnp.float32,
            )
        )
    grad_query = jnp.concatenate(query_grads, axis=2).reshape(sequences, tile_rows, model_width)
    grad_key_full = jnp.concatenate(key_grads, axis=2).reshape(sequences, key_count, model_width)
    grad_value_full = jnp.concatenate(value_grads, axis=2).reshape(
        sequences, key_count, model_width
    )
    grad_shared_full = jnp.concatenate([grad_key_full, grad_value_full], axis=-1)
    grad_shared = lax.psum_scatter(
        grad_shared_full.astype(jnp.bfloat16), "tile", scatter_dimension=1, tiled=True
    ).astype(jnp.float32)
    grad_projected_low = (
        jnp.concatenate([grad_query, grad_shared], axis=-1)
        .astype(jnp.bfloat16)
        .reshape(count_rows, 3 * model_width)
    )
    qkv_grad = jnp.einsum(
        "nd,ne->de", normed_low, grad_projected_low, preferred_element_type=jnp.float32
    )
    column_sums = jnp.sum(grad_projected_low.astype(jnp.float32), axis=0)
    query_bias_grad = column_sums[:model_width]
    value_bias_grad = column_sums[2 * model_width :]
    grad_normed = jnp.einsum(
        "ne,de->nd", grad_projected_low, qkv_weight, preferred_element_type=jnp.float32
    )
    normed_first, norm_back_one = jax.vjp(layer_norm, flattened, gain_one, bias_one)
    grad_tokens_part, gain_one_grad, bias_one_grad = norm_back_one(grad_normed)
    grad_tokens = (
        (grad_hidden + grad_tokens_part)
        .astype(jnp.bfloat16)
        .reshape(sequences, tile_rows, model_width)
    )
    totals_small = lax.psum(
        (
            gain_one_grad,
            bias_one_grad,
            query_bias_grad,
            value_bias_grad,
            out_bias_grad,
            gain_two_grad,
            bias_two_grad,
            fc1_bias_grad,
            fc2_bias_grad,
            stats,
        ),
        ("dp", "tile"),
    )
    matrices = (qkv_grad, out_grad, fc1_grad, fc2_grad)
    row_shares = (
        lax.psum_scatter(
            matrices[0].astype(jnp.bfloat16), "dp", scatter_dimension=0, tiled=True
        ).astype(jnp.float32),
        lax.psum_scatter(
            matrices[1].astype(jnp.bfloat16), "dp", scatter_dimension=0, tiled=True
        ).astype(jnp.float32),
        lax.psum_scatter(
            matrices[2].astype(jnp.bfloat16), "dp", scatter_dimension=0, tiled=True
        ).astype(jnp.float32),
        lax.psum_scatter(
            matrices[3].astype(jnp.bfloat16), "dp", scatter_dimension=0, tiled=True
        ).astype(jnp.float32),
    )
    reduced = (
        lax.psum_scatter(
            row_shares[0].astype(jnp.bfloat16), "tile", scatter_dimension=1, tiled=True
        ).astype(jnp.float32),
        lax.psum_scatter(
            row_shares[1].astype(jnp.bfloat16), "tile", scatter_dimension=1, tiled=True
        ).astype(jnp.float32),
        lax.psum_scatter(
            row_shares[2].astype(jnp.bfloat16), "tile", scatter_dimension=1, tiled=True
        ).astype(jnp.float32),
        lax.psum_scatter(
            row_shares[3].astype(jnp.bfloat16), "tile", scatter_dimension=1, tiled=True
        ).astype(jnp.float32),
    )
    totals = totals_small[9]
    root_mean = jnp.sqrt(totals[:4] / (totals[4] * model_width))
    return (
        output,
        grad_tokens,
        totals_small[0],
        totals_small[1],
        reduced[0],
        totals_small[2],
        totals_small[3],
        reduced[1],
        totals_small[4],
        totals_small[5],
        totals_small[6],
        reduced[2],
        totals_small[7],
        reduced[3],
        totals_small[8],
        root_mean,
    )


def on_device(tokens,segment_ids,keep_mask,gain_one,bias_one,qkv_weight,query_bias,value_bias,out_weight,out_bias,gain_two,bias_two,fc1_weight,fc1_bias,fc2_weight,fc2_bias,cotangent):
    _,rows,width=tokens.shape; half=rows//2
    t=lax.axis_index("tile"); base=t*rows
    ofs=(base+t*half,base+(1-t)*half,(1-t)*rows+t*half)
    def order(v): return jnp.concatenate([lax.dynamic_slice_in_dim(v,o,half,0) for o in ofs])
    s=order(segment_ids[0]); k=order(keep_mask[0])
    info=jnp.concatenate([jnp.stack([s,jnp.where(k==1,s,-1)]),jnp.zeros((6,s.shape[0]),jnp.int32)])
    row=lambda v:v[None]
    pb=jnp.concatenate([query_bias,jnp.zeros_like(query_bias),value_bias])[None]
    proj,norm,att,lse=call_forward(tokens[0],info,row(gain_one),row(bias_one),qkv_weight,pb)
    kc=jnp.broadcast_to(k[:rows,None].astype(jnp.float32),(rows,128))
    out,dh,db,da,delta,f1,f2,vec,b1g=call_mlp(tokens[0],att,cotangent[0],kc,out_weight,row(out_bias),row(gain_two),row(bias_two),fc1_weight,fc1_bias,fc2_weight,row(fc2_bias))
    gt,qg,og,vec2=call_backward(tokens[0],info,row(gain_one),proj,norm,att,dh,db,da,lse,delta,qkv_weight)
    stats=jnp.concatenate([vec[:4].sum(1),k[:rows].astype(jnp.float32).sum()[None]])
    small=lax.psum((vec2[0],vec2[1],vec2[2],vec2[3],vec[6],vec[4],vec[5],b1g.reshape(-1),vec[7],stats),("dp","tile"))
    mats=(qg.swapaxes(0,1).reshape(width,3*width),og,f1.swapaxes(0,1).reshape(width,-1),f2.reshape(-1,width))
    red=[]
    for m in mats:
        m=lax.psum_scatter(m,"dp",scatter_dimension=0,tiled=True)
        red.append(lax.psum_scatter(m,"tile",scatter_dimension=1,tiled=True).astype(jnp.float32))
    tot=small[9]
    rm=jnp.sqrt(tot[:4]/(tot[4]*width))
    return (out[None],gt[None],small[0],small[1],red[0],small[2],small[3],red[1],small[4],small[5],small[6],red[2],small[7],red[3],small[8],rm)
def fits(mesh):
    return mesh.shape["tile"] == 2 and mesh.shape["dp"] == 16


def solution(mesh):
    S=P("dp","tile",None); D=P("dp",None)
    placed=(S,D,D)+(P(),)*13+(S,)
    T=P("dp","tile")
    return jax.shard_map(on_device if fits(mesh) else on_device_general,mesh=mesh,in_specs=placed,out_specs=(S,S,P(),P(),T,P(),P(),T,P(),P(),P(),T,P(),T,P(),P()),check_vma=False)
```

```python
import itertools

import jax
import jax.numpy as jnp
from jax import lax
from jax.experimental import pallas as pl
from jax.experimental.pallas import tpu as pltpu
from jax.sharding import PartitionSpec as P

HEAD_DIM = 64
PAIR = 2 * HEAD_DIM
MASKED = -1e30
MESH = pl.DeviceIdType.MESH
BF = jnp.bfloat16
F32 = jnp.float32
NT = (((1,), (1,)), ((), ()))
TN = (((0,), (0,)), ((), ()))


def mm(a, b):
    return jnp.dot(a, b, preferred_element_type=F32)


def mm_nt(a, b):
    return lax.dot_general(a, b, NT, preferred_element_type=F32)


def mm_tn(a, b):
    return lax.dot_general(a, b, TN, preferred_element_type=F32)


def any_spec():
    return pl.BlockSpec(memory_space=pl.ANY)


def vmem_spec():
    return pl.BlockSpec(memory_space=pltpu.VMEM)


def attention_forward(
    tok, info, gain, bias, w_hbm, pbias, proj_out, norm_out, att_out, lse_out,
    x, w, proj, norm, att, lse, mask, sems, send_sem, recv_sem,
):
    rows, width = norm.shape
    half = rows // 2
    heads = width // HEAD_DIM
    t = lax.axis_index("tile")
    far, near = t * half, (1 - t) * half
    barrier = pltpu.get_barrier_semaphore()
    pl.semaphore_signal(barrier, inc=1, device_id={"tile": 1 - t}, device_id_type=MESH)
    load_far = pltpu.make_async_copy(tok.at[pl.ds(far, half)], x.at[pl.ds(0, half)], sems.at[0])
    load_near = pltpu.make_async_copy(tok.at[pl.ds(near, half)], x.at[pl.ds(half, half)], sems.at[1])
    load_w = pltpu.make_async_copy(w_hbm, w, sems.at[2])
    load_far.start()
    load_near.start()
    load_w.start()
    pl.semaphore_wait(barrier, 1)
    halo = pltpu.make_async_remote_copy(
        tok.at[pl.ds(near, half)], x.at[pl.ds(rows, half)], send_sem, recv_sem,
        device_id={"tile": 1 - t}, device_id_type=MESH,
    )
    halo.start()

    seg_row = info[1:2, :]
    seg_col = jnp.transpose(info[...].astype(F32))[:, 0:1].astype(jnp.int32)
    key_at = lax.broadcasted_iota(jnp.int32, (half, rows + half), 1)
    for part in range(2):
        query_at = lax.broadcasted_iota(jnp.int32, (half, rows + half), 0) + part * half
        same = seg_col[part * half : (part + 1) * half] == seg_row
        mask[pl.ds(part * half, half), :] = jnp.where(same | (query_at == key_at), 0.0, MASKED)

    def normalize(start, count):
        step = 128

        def one(i, _):
            at = pl.ds(pl.multiple_of(start + i * step, step), step)
            v = x[at, :].astype(F32)
            centred = v - jnp.mean(v, axis=-1, keepdims=True)
            var = jnp.mean(centred * centred, axis=-1, keepdims=True)
            norm_at = centred * lax.rsqrt(var + 1e-06) * gain[...] + bias[...]
            x[at, :] = norm_at.astype(BF)
            return 0

        lax.fori_loop(0, count // step, one, 0)

    def project(start, count):
        cols = 768

        def one(i, _):
            at = pl.ds(pl.multiple_of(i * cols, cols), cols)
            block = mm(x[pl.ds(start, count), :], w[:, at]) + pbias[:, at]
            low = block.astype(BF)
            scale = jnp.where(i * cols < width, HEAD_DIM ** (-0.5), 1.0).astype(BF)
            proj[pl.ds(start, count), at] = low * scale
            return 0

        lax.fori_loop(0, 3 * width // cols, one, 0)

    lane = lax.broadcasted_iota(jnp.int32, (1, PAIR), 1)
    low_half = lane < HEAD_DIM

    def attend(start, keys):
        def one(p, _):
            at = pl.multiple_of(p * PAIR, PAIR)
            q = proj[pl.ds(start, half), pl.ds(at, PAIR)]
            k = proj[pl.ds(0, keys), pl.ds(width + at, PAIR)]
            v = proj[pl.ds(0, keys), pl.ds(2 * width + at, PAIR)]
            total = None
            tops = []
            for head in range(2):
                mine = low_half if head == 0 else ~low_half
                qh = jnp.where(mine, q, 0).astype(BF)
                s = mm_nt(qh, k) + mask[pl.ds(start, half), pl.ds(0, keys)]
                top = jnp.max(s, axis=-1, keepdims=True)
                e = jnp.exp(s - top).astype(BF)
                ones = jnp.broadcast_to(jnp.where(mine, 1.0, 0.0).astype(BF), (keys, PAIR))
                vh = jnp.concatenate([jnp.where(mine, v, 0).astype(BF), ones], axis=1)
                part = mm(e, vh)
                total = part if total is None else total + part
                tops.append(top)
            sums = total[:, PAIR:]
            att[pl.ds(start, half), pl.ds(at, PAIR)] = (total[:, :PAIR] / sums).astype(BF)
            logs = jnp.log(sums)
            lane_of = lax.broadcasted_iota(jnp.int32, (half, PAIR), 1)
            acc = lse[pl.ds(start, half), :]
            acc = jnp.where(lane_of == 2 * p, tops[0] + logs[:, 0:1], acc)
            acc = jnp.where(lane_of == 2 * p + 1, tops[1] + logs[:, HEAD_DIM : HEAD_DIM + 1], acc)
            lse[pl.ds(start, half), :] = acc
            return 0

        lax.fori_loop(0, heads // 2, one, 0, unroll=6)

    lse[...] = jnp.zeros_like(lse)
    load_far.wait()
    load_near.wait()
    normalize(0, rows)
    norm_copy = pltpu.make_async_copy(x.at[pl.ds(0, rows)], norm_out, sems.at[0])
    norm_copy.start()
    load_w.wait()
    project(0, rows)
    attend(0, rows)
    halo.wait()
    normalize(rows, half)
    project(rows, half)
    proj_copy = pltpu.make_async_copy(proj, proj_out, sems.at[1])
    proj_copy.start()
    attend(half, rows + half)
    att_copy = pltpu.make_async_copy(att, att_out, sems.at[2])
    att_copy.start()
    lse_out[...] = jnp.transpose(lse[...])[:16, :]
    norm_copy.wait()
    proj_copy.wait()
    att_copy.wait()


def call_forward(tokens, info, gain, bias, w, pbias):
    rows, width = tokens.shape
    half = rows // 2
    sds = jax.ShapeDtypeStruct
    return pl.pallas_call(
        attention_forward,
        out_shape=(
            sds((rows + half, 3 * width), BF),
            sds((rows, width), BF),
            sds((rows, width), BF),
            sds((16, rows), F32),
        ),
        in_specs=[any_spec(), vmem_spec(), vmem_spec(), vmem_spec(), any_spec(), vmem_spec()],
        out_specs=(any_spec(), any_spec(), any_spec(), vmem_spec()),
        scratch_shapes=[
            pltpu.VMEM((rows + half, width), BF),
            pltpu.VMEM((width, 3 * width), BF),
            pltpu.VMEM((rows + half, 3 * width), BF),
            pltpu.VMEM((rows, width), BF),
            pltpu.VMEM((rows, width), BF),
            pltpu.VMEM((rows, PAIR), F32),
            pltpu.VMEM((rows, rows + half), F32),
            pltpu.SemaphoreType.DMA((3,)),
            pltpu.SemaphoreType.DMA,
            pltpu.SemaphoreType.DMA,
        ],
        compiler_params=pltpu.CompilerParams(collective_id=0, has_side_effects=True, vmem_limit_bytes=60 << 20),
        name="attention_forward",
    )(tokens, info, gain, bias, w, pbias)


def gelu_and_slope(z):
    bell = jnp.exp(z * z * -0.5)
    t = 1.0 / (1.0 + jnp.abs(z) * (0.3275911 * 0.7071067811865476))
    tail = t * (0.127414796 + t * (-0.142248368 + t * (0.7107068705 + t * (-0.7265760135 + t * 0.5307027145)))) * bell
    upper = jnp.where(z >= 0, 1.0 - tail, tail)
    return z * upper, upper + z * bell * 0.3989422804014327


def place():
    d = lax.axis_index("dp")
    return dict(core=d % 2, y=d // 2 % 2, z0=d // 4 % 2, z1=d // 8, x=lax.axis_index("tile"))


def peer(at, bit):
    if bit == "x":
        return {"tile": 1 - at["x"]}
    step = dict(core=1, y=2, z0=4, z1=8)[bit]
    d = lax.axis_index("dp")
    return {"dp": d + step - 2 * step * at[bit]}


def greet(at, bits):
    barrier = pltpu.get_barrier_semaphore()
    for bit in bits:
        pl.semaphore_signal(barrier, inc=1, device_id=peer(at, bit), device_id_type=MESH)
    return barrier


def send(at, bit, src, dst, send_sem, recv_sem):
    c = pltpu.make_async_remote_copy(src, dst, send_sem, recv_sem, device_id=peer(at, bit), device_id_type=MESH)
    c.start()
    return c


def feed_forward(
    tok, att_hbm, dy_hbm, keep_col, ow_hbm, ob, g2, b2, w1_hbm, b1, w2_hbm, c2,
    out_hbm, dh_hbm, db_hbm, da_hbm, delta_out, vec_out, pa_hbm, pb_hbm, pc_hbm, pd_hbm,
    x, att, dy, ow, w1, w2, hidden, xhat, rstd, n2, n2t, z, da, act, di, acc, dn, f1, f2, obuf,
    r1, r2, pa, pb, pc, pd, sems, core_send, core_recv, next_send, next_recv,
):
    rows, width = hidden.shape
    half = rows // 2
    cols = width
    chunks = w2.shape[0] // cols
    at = place()
    t = at["x"]
    far, near = t * half, (1 - t) * half
    barrier = greet(at, ("core", "x", "y", "z0"))

    def fetch(src, dst, i):
        c = pltpu.make_async_copy(src, dst, sems.at[i])
        c.start()
        return c

    got_att = fetch(att_hbm, att, 0)
    got_ow = fetch(ow_hbm, ow, 1)
    got_x = [fetch(tok.at[pl.ds(far, half)], x.at[pl.ds(0, half)], 2), fetch(tok.at[pl.ds(near, half)], x.at[pl.ds(half, half)], 3)]
    got_dy = [fetch(dy_hbm.at[pl.ds(far, half)], dy.at[pl.ds(0, half)], 4), fetch(dy_hbm.at[pl.ds(near, half)], dy.at[pl.ds(half, half)], 5)]
    for c in range(chunks):
        fetch(w1_hbm.at[:, pl.ds(c * cols, cols)], w1.at[:, pl.ds(c * cols, cols)], 6 + 2 * c)
        fetch(w2_hbm.at[pl.ds(c * cols, cols)], w2.at[pl.ds(c * cols, cols)], 7 + 2 * c)
    got_att.wait()
    got_ow.wait()
    for g in got_x:
        g.wait()
    rb = 128
    vec_out[...] = jnp.zeros_like(vec_out)

    def add_vec(i, v):
        vec_out[i : i + 1, :] += jnp.sum(v, axis=0, keepdims=True)

    def front(i, _):
        rs = pl.ds(pl.multiple_of(i * rb, rb), rb)
        branch = mm(att[rs, :], ow[...]) + ob[...]
        xs = x[rs, :].astype(F32)
        h = xs + branch
        hidden[rs, :] = h
        kept = keep_col[rs, :][:, 0:1]
        add_vec(0, kept * xs * xs)
        add_vec(1, kept * branch * branch)
        centred = h - jnp.mean(h, axis=-1, keepdims=True)
        r = lax.rsqrt(jnp.mean(centred * centred, axis=-1, keepdims=True) + 1e-06)
        xh = centred * r
        xhat[rs, :] = xh
        rstd[rs, :] = jnp.broadcast_to(r, (rb, 128))
        n2[rs, :] = (xh * g2[...] + b2[...]).astype(BF)
        return 0

    lax.fori_loop(0, rows // rb, front, 0)
    vec_out[12:13, 0:128] = jnp.sum(keep_col[...], axis=0, keepdims=True)
    n2t[...] = jnp.transpose(n2[...])
    for g in got_dy:
        g.wait()
    pl.semaphore_wait(barrier, 4)

    def core_copies(c):
        hi, lo = c // 2, c % 2
        other = 1 - at["core"]
        pairs = ((f1.at[hi, lo, :, :, :, other], r1.at[hi, lo]), (f2.at[hi, lo, :, :, other], r2.at[hi, lo]))
        return [
            pltpu.make_async_remote_copy(s, d, core_send.at[i, c], core_recv.at[i, c], device_id=peer(at, "core"), device_id_type=MESH)
            for i, (s, d) in enumerate(pairs)
        ]

    def next_copies(c):
        hi, lo = c // 2, c % 2
        jobs = (
            ("x", r2.at[hi, lo, 1 - t, :, :, pl.ds(0, 256)], pa.at[hi, lo]),
            ("y", r2.at[hi, lo, :, 1 - at["y"], :, pl.ds(256, 128)], pb.at[hi, lo]),
            ("y", r1.at[hi, lo, :, :, 1 - at["y"], :, pl.ds(0, 256)], pc.at[hi, lo]),
            ("z0", r1.at[hi, lo, :, 1 - at["z0"], :, :, pl.ds(256, 512)], pd.at[hi, lo]),
        )
        return [
            pltpu.make_async_remote_copy(s, d, next_send.at[i, c], next_recv.at[i, c], device_id=peer(at, bit), device_id_type=MESH)
            for i, (bit, s, d) in enumerate(jobs)
        ]

    def pass_on(c):
        hi, lo = c // 2, c % 2
        mine = at["core"]
        for copy in core_copies(c):
            copy.wait()

        def one(i, _):
            a, b, d = i // 4, i // 2 % 2, i % 2
            r1[hi, lo, a, b, d] += f1[hi, lo, a, b, d, mine]
            return 0

        lax.fori_loop(0, 8, one, 0, unroll=2)

        def two(i, _):
            r2[hi, lo, i // 2, i % 2] += f2[hi, lo, i // 2, i % 2, mine]
            return 0

        lax.fori_loop(0, 4, two, 0)
        for copy in next_copies(c):
            copy.start()

    def chunk(c, _):
        hi, lo = c // 2, c % 2
        for i in range(2):
            pltpu.make_async_copy(w2_hbm.at[pl.ds(0, cols)], w2.at[pl.ds(0, cols)], sems.at[6 + 2 * c + i]).wait()
        here = pl.ds(pl.multiple_of(c * cols, cols), cols)
        z[...] = mm(n2[...], w1[:, here]) + b1[c]
        da[...] = mm_nt(dy[...], w2[here, :])
        gr = 64
        bsum = jnp.zeros((1, cols), F32)
        for i in range(rows // gr):
            rs = pl.ds(i * gr, gr)
            a, s = gelu_and_slope(z[rs, :])
            act[rs, here] = a.astype(BF)
            d = (da[rs, :] * s).astype(BF)
            di[rs, here] = d
            bsum = bsum + jnp.sum(d.astype(F32), axis=0, keepdims=True)
        vec_out[pl.ds(8 + c, 1), :] = bsum

        @pl.when(c > 0)
        def _():
            pass_on(c - 1)

        f1[hi, lo] = mm(n2t[...], di[:, here]).astype(BF).reshape(f1.shape[2:])
        g = mm_tn(act[:, here], dy[...]).astype(BF)
        f2[hi, lo, 0] = g[:, : width // 2].reshape(f2.shape[3:])
        f2[hi, lo, 1] = g[:, width // 2 :].reshape(f2.shape[3:])
        for copy in core_copies(c):
            copy.start()
        return 0

    lax.fori_loop(0, chunks, chunk, 0)
    acc[...] = mm(act[...], w2[...])
    pass_on(chunks - 1)
    dn[...] = mm_nt(di[...], w1[...])

    def back(i, _):
        rs = pl.ds(pl.multiple_of(i * rb, rb), rb)
        branch = acc[rs, :] + c2[...]
        result = hidden[rs, :] + branch
        obuf[rs, :] = result.astype(BF)
        kept = keep_col[rs, :][:, 0:1]
        add_vec(2, kept * branch * branch)
        add_vec(3, kept * result * result)
        g = dn[rs, :]
        xh = xhat[rs, :]
        add_vec(4, g * xh)
        add_vec(5, g)
        gy = g * g2[...]
        mean_gy = jnp.mean(gy, axis=-1, keepdims=True)
        mean_gx = jnp.mean(gy * xh, axis=-1, keepdims=True)
        dys = dy[rs, :].astype(F32)
        add_vec(7, dys)
        dh = dys + rstd[rs, :][:, 0:1] * (gy - mean_gy - xh * mean_gx)
        hidden[rs, :] = dh
        low = dh.astype(BF)
        n2[rs, :] = low
        add_vec(6, low.astype(F32))
        return 0

    lax.fori_loop(0, rows // rb, back, 0)
    copies = [
        fetch(obuf.at[pl.ds(0, half)], out_hbm.at[pl.ds(far, half)], 0),
        fetch(obuf.at[pl.ds(half, half)], out_hbm.at[pl.ds(near, half)], 1),
        fetch(hidden, dh_hbm, 2),
        fetch(n2, db_hbm, 3),
    ]
    d_att = mm_nt(n2[...], ow[...])
    x[...] = d_att.astype(BF)
    copies.append(fetch(x, da_hbm, 4))
    heads = width // HEAD_DIM
    head_of = lax.broadcasted_iota(jnp.int32, (16, width), 1) // HEAD_DIM
    mine = (head_of == lax.broadcasted_iota(jnp.int32, (16, width), 0)).astype(F32).astype(BF)
    prod = x[...].astype(F32) * att[...].astype(F32)
    hi = prod.astype(BF)
    lo = (prod - hi.astype(F32)).astype(BF)
    delta_out[...] = mm_nt(mine, hi) + mm_nt(mine, lo)

    def settle(c, _):
        hi, lo = c // 2, c % 2
        for copy in next_copies(c):
            copy.wait()
        for i in range(2):
            pa[hi, lo, i] += r2[hi, lo, t, i, :, 0:256]
            pb[hi, lo, i] += r2[hi, lo, i, at["y"], :, 256:384]
            for j in range(2):
                pc[hi, lo, i, j] += r1[hi, lo, i, j, at["y"], :, 0:256]
                pd[hi, lo, i, j] += r1[hi, lo, i, at["z0"], j, :, 256:768]
        return 0

    lax.fori_loop(0, chunks, settle, 0)
    for i, (src, dst) in enumerate(((pa, pa_hbm), (pb, pb_hbm), (pc, pc_hbm), (pd, pd_hbm))):
        copies.append(fetch(src, dst, 6 + i))
    for c in copies:
        c.wait()


def call_feed_forward(tokens, att, dy, keep_col, ow, ob, g2, b2, w1, b1, w2, c2):
    rows, width = tokens.shape
    hid = w1.shape[1]
    cols = width
    chunks = hid // cols
    block, wide = width // 16, hid // 16
    sds = jax.ShapeDtypeStruct
    V = pltpu.VMEM
    parts = ((2, 2, 2, wide, 256), (2, 2, 2, wide, 128), (2, 2, 2, 2, block, 256), (2, 2, 2, 2, block, 512))
    return pl.pallas_call(
        feed_forward,
        out_shape=(
            sds((rows, width), BF), sds((rows, width), F32), sds((rows, width), BF), sds((rows, width), BF),
            sds((16, rows), F32), sds((16, width), F32),
        ) + tuple(sds(s, BF) for s in parts),
        in_specs=[any_spec(), any_spec(), any_spec(), vmem_spec(), any_spec(), vmem_spec(), vmem_spec(), vmem_spec(), any_spec(), vmem_spec(), any_spec(), vmem_spec()],
        out_specs=(any_spec(),) * 4 + (vmem_spec(), vmem_spec()) + (any_spec(),) * 4,
        scratch_shapes=[
            V((rows, width), BF), V((rows, width), BF), V((rows, width), BF), V((width, width), BF),
            V((width, hid), BF), V((hid, width), BF),
            V((rows, width), F32), V((rows, width), F32), V((rows, 128), F32), V((rows, width), BF), V((width, rows), BF),
            V((rows, cols), F32), V((rows, cols), F32), V((rows, hid), BF), V((rows, hid), BF),
            V((rows, width), F32), V((rows, width), F32),
            V((2, 2, 2, 2, 2, 2, block, cols), BF), V((2, 2, 2, 2, 2, wide, width // 2), BF),
            V((rows, width), BF),
            V((2, 2, 2, 2, 2, block, cols), BF), V((2, 2, 2, 2, wide, width // 2), BF),
        ] + [V(s, BF) for s in parts] + [
            pltpu.SemaphoreType.DMA((6 + 2 * chunks,)),
            pltpu.SemaphoreType.DMA((2, chunks)), pltpu.SemaphoreType.DMA((2, chunks)),
            pltpu.SemaphoreType.DMA((4, chunks)), pltpu.SemaphoreType.DMA((4, chunks)),
        ],
        compiler_params=pltpu.CompilerParams(collective_id=2, has_side_effects=True, vmem_limit_bytes=63 << 20),
        name="feed_forward",
    )(tokens, att, dy, keep_col, ow, ob, g2, b2, w1, b1.reshape(chunks, 1, cols), w2, c2)


class Share:
    def __init__(self, at, ref, dims, buffers, send_sems, recv_sems, first):
        self.at, self.ref, self.dims, self.buffers = at, ref, dims, list(buffers)
        self.sems, self.next = (send_sems, recv_sems), first

    def start(self, bit):
        self.axis = self.dims.index(bit)
        self.mine = self.at[bit]
        lead = (slice(None),) * self.axis
        self.other = self.buffers.pop(0)
        i, self.next = self.next, self.next + 1
        self.copy = send(self.at, bit, self.ref.at[lead + (1 - self.mine,)], self.other, self.sems[0].at[i], self.sems[1].at[i])

    def kept(self, index):
        return self.ref[index[: self.axis] + (self.mine,) + index[self.axis :]]

    def finish(self):
        self.copy.wait()
        lead = self.other.shape[:-2]
        for index in itertools.product(*map(range, lead)):
            self.other[index] = self.other[index] + self.kept(index)
        self.ref = self.other
        self.dims = self.dims[: self.axis] + self.dims[self.axis + 1 :]

    def last(self, put):
        self.copy.wait()
        lead = self.other.shape[:-2]
        for index in itertools.product(*map(range, lead)):
            put(index, self.other[index].astype(F32) + self.kept(index).astype(F32))


class Total:
    def __init__(self, at, ref, buffers, send_sems, recv_sems, first):
        self.at, self.ref, self.buffers = at, ref, buffers
        self.sems, self.next, self.stage = (send_sems, recv_sems), first, 0

    def start(self, bit):
        i = self.next + self.stage
        self.copy = send(self.at, bit, self.ref, self.buffers.at[2 * self.stage], self.sems[0].at[i], self.sems[1].at[i])

    def finish(self):
        self.copy.wait()
        got, new = self.buffers.at[2 * self.stage], self.buffers.at[2 * self.stage + 1]
        new[...] = self.ref[...] + got[...]
        self.ref, self.stage = new, self.stage + 1


BITS = ("core", "y", "z0", "z1", "x")
PART_A = (("z1", "z0", "y"), ("y", "z0", "z1"))
PART_B = (("z1", "z0", "x"), ("z0", "x", "z1"))
PART_C = (("x", "j", "z1", "z0"), ("x", "z0", "z1"))
PART_D = (("x", "j", "z1", "y"), ("y", "x", "z1"))
MATRIX = ("z1", "z0", "y", "core", "x")
ORDERS = (("core", "x", "y", "z0", "z1"), ("core", "y", "z0", "x", "z1"), ("core", "z0", "x", "y", "z1"))
OUT_ORDER = ("core", "z0", "y", "x", "z1")


def stage_shapes(dims, order, rows, cols):
    left, shapes = list(dims), []
    for bit in order:
        left.remove(bit)
        shapes.append((2,) * len(left) + (rows, cols))
    return shapes


def attention_backward(
    tok, info, gain, proj_hbm, norm_hbm, att_hbm, dh_hbm, db_hbm, da_hbm, lse, delta, w_hbm, vec, pa_hbm, pb_hbm, pc_hbm, pd_hbm,
    gt_hbm, qkv_out, out_out, fc1_out, fc2_out, vec_out, late_out,
    x, proj, norm, att, dh, db, da, w, normt, attt, stat, mask, near_key, near_query, dk, dv, dproj, dn, qg, og, obuf,
    pa, pb, pc, pd, late, early_buf, late_buf, *rest,
):
    rows, width = norm.shape
    half = rows // 2
    heads = width // HEAD_DIM
    stage_bufs, (sems, send_sems, recv_sems) = list(rest[:-3]), rest[-3:]
    at = place()
    t = at["x"]
    far, near = t * half, (1 - t) * half
    barrier = greet(at, BITS)

    def fetch(src, dst, i):
        c = pltpu.make_async_copy(src, dst, sems.at[i])
        c.start()
        return c

    got_att = fetch(att_hbm, att, 2)
    got_db = fetch(db_hbm, db, 3)
    got_parts = [fetch(s, d, 9 + i) for i, (s, d) in enumerate(((pa_hbm, pa), (pb_hbm, pb), (pc_hbm, pc), (pd_hbm, pd)))]
    got_proj = fetch(proj_hbm, proj, 0)
    got_da = fetch(da_hbm, da.at[pl.ds(0, rows)], 1)
    got_norm = fetch(norm_hbm, norm, 4)
    got_w = fetch(w_hbm, w, 5)
    got_dh = fetch(dh_hbm, dh, 6)
    got_x = [fetch(tok.at[pl.ds(far, half)], x.at[pl.ds(0, half)], 7), fetch(tok.at[pl.ds(near, half)], x.at[pl.ds(half, half)], 8)]
    pl.semaphore_wait(barrier, 5)
    halos = [
        send(at, "x", src, dst, send_sems.at[i], recv_sems.at[i])
        for i, (src, dst) in enumerate(
            (
                (da_hbm.at[pl.ds(half, half)], da.at[pl.ds(rows, half)]),
                (lse.at[:, pl.ds(half, half)], stat.at[0]),
                (delta.at[:, pl.ds(half, half)], stat.at[1]),
            )
        )
    ]
    used = [3]

    def share(ref, dims, count):
        bufs, first = [stage_bufs.pop(0) for _ in range(count)], used[0]
        used[0] += count
        return Share(at, ref, dims, bufs, send_sems, recv_sems, first)

    A = share(pa, PART_A[0], 3)
    B = share(pb, PART_B[0], 3)
    C = share(pc, PART_C[0], 3)
    D = share(pd, PART_D[0], 3)
    O = share(og, MATRIX, 5)
    Q = [share(qg.at[i], MATRIX, 5) for i in range(3)]
    early = Total(at, vec, early_buf, send_sems, recv_sems, used[0])
    later = Total(at, late, late_buf, send_sems, recv_sems, used[0] + 5)
    for g in got_parts:
        g.wait()
    for s, part in ((A, PART_A), (B, PART_B), (C, PART_C), (D, PART_D)):
        s.start(part[1][0])
    early.start(BITS[0])
    got_att.wait()
    attt[...] = jnp.transpose(att[...])
    got_db.wait()
    for i in range(2):
        og_half = mm(attt[...], db[:, i * (width // 2) : (i + 1) * (width // 2)]).astype(BF)
        og[:, :, :, :, i] = og_half.reshape((2, 2, 2, 2) + og.shape[-2:])
    O.start(OUT_ORDER[0])

    seg_row = info[0:1, :]
    key_col = jnp.transpose(info[...].astype(F32))[:, 1:2].astype(jnp.int32)
    key_at = lax.broadcasted_iota(jnp.int32, (half, rows), 0)
    query_at = lax.broadcasted_iota(jnp.int32, (half, rows), 1)
    for part in range(2):
        same = key_col[part * half : (part + 1) * half] == seg_row[:, :rows]
        mask[pl.ds(part * half, half), :] = jnp.where(same | (query_at == key_at + part * half), 0.0, MASKED)
    near_key[...] = jnp.where(key_col[half:rows] == seg_row[:, rows:], 0.0, MASKED)
    near_query[...] = jnp.where(key_col[rows:] == seg_row[:, half:rows], 0.0, MASKED)
    got_norm.wait()
    normt[...] = jnp.transpose(norm[...])
    got_proj.wait()
    got_da.wait()

    lane = lax.broadcasted_iota(jnp.int32, (1, PAIR), 1)

    def cut(v, head):
        return jnp.where((lane < HEAD_DIM) == (head == 0), v, 0).astype(BF)

    def own(p):
        c = p * PAIR
        col = pl.ds(c, PAIR)
        kcol, vcol = pl.ds(width + c, PAIR), pl.ds(2 * width + c, PAIR)
        q, k, v = proj[pl.ds(0, rows), col], proj[:, kcol], proj[:, vcol]
        do = da[pl.ds(0, rows), col]
        gq = gk = gv = gn = None
        for head in range(2):
            qh, kh, doh = cut(q, head), cut(k, head), cut(do, head)
            ls = lse[pl.ds(2 * p + head, 1), :]
            de = delta[pl.ds(2 * p + head, 1), :]
            s = mm_nt(k[:rows], qh) + mask[...]
            prob = jnp.exp(s - ls)
            dp = mm_nt(v[:rows], doh)
            ds = (prob * (dp - de)).astype(BF)
            low = prob.astype(BF)
            a = mm(low, doh)
            b = mm(ds, qh)
            c = mm_tn(ds, kh[:rows])
            s2 = mm_nt(k[rows:], qh[half:]) + near_query[...]
            prob2 = jnp.exp(s2 - ls[:, half:])
            dp2 = mm_nt(v[rows:], doh[half:])
            ds2 = (prob2 * (dp2 - de[:, half:])).astype(BF)
            d = mm_tn(ds2, kh[rows:])
            gv = a if gv is None else gv + a
            gk = b if gk is None else gk + b
            gq = c if gq is None else gq + c
            gn = d if gn is None else gn + d
        scale = HEAD_DIM ** (-0.5)
        dproj[pl.ds(0, half), col] = (gq[:half] * scale).astype(BF)
        dproj[pl.ds(half, half), col] = ((gq[half:] + gn) * scale).astype(BF)
        dproj[pl.ds(0, half), kcol] = gk[:half].astype(BF)
        dproj[pl.ds(0, half), vcol] = gv[:half].astype(BF)
        dk[:, col] = gk[half:]
        dv[:, col] = gv[half:]

    def halo(p):
        c = p * PAIR
        col = pl.ds(c, PAIR)
        kcol, vcol = pl.ds(width + c, PAIR), pl.ds(2 * width + c, PAIR)
        q, k, v = proj[pl.ds(rows, half), col], proj[pl.ds(half, half), kcol], proj[pl.ds(half, half), vcol]
        do = da[pl.ds(rows, half), col]
        gk, gv = dk[:, col], dv[:, col]
        for head in range(2):
            qh, doh = cut(q, head), cut(do, head)
            ls = stat[0, pl.ds(2 * p + head, 1), :]
            de = stat[1, pl.ds(2 * p + head, 1), :]
            prob = jnp.exp(mm_nt(k, qh) + near_key[...] - ls)
            ds = (prob * (mm_nt(v, doh) - de)).astype(BF)
            gv = gv + mm(prob.astype(BF), doh)
            gk = gk + mm(ds, qh)
        dproj[pl.ds(half, half), kcol] = gk.astype(BF)
        dproj[pl.ds(half, half), vcol] = gv.astype(BF)

    third = heads // 4
    for p in range(third):
        own(p)
    O.finish()
    O.start(OUT_ORDER[1])
    early.finish()
    early.start(BITS[1])
    for p in range(third, heads // 2):
        own(p)
    for s, part in ((A, PART_A), (B, PART_B), (C, PART_C), (D, PART_D)):
        s.finish()
        s.start(part[1][1])
    O.finish()
    O.start(OUT_ORDER[2])
    early.finish()
    early.start(BITS[2])
    for h in halos:
        h.wait()
    for p in range(heads // 2):
        halo(p)
    early.finish()
    early.start(BITS[3])
    O.finish()
    O.start(OUT_ORDER[3])
    third = width // 2
    for j in range(3):
        g = mm(normt[...], dproj[:, pl.ds(j * width, width)]).astype(BF)
        for i in range(2):
            side, part = divmod(2 * j + i, 3)
            qg[part, :, :, :, :, side] = g[:, i * third : (i + 1) * third].reshape((2, 2, 2, 2) + qg.shape[-2:])
    for i in range(3):
        Q[i].start(ORDERS[i][0])
    for s, part in ((A, PART_A), (B, PART_B), (C, PART_C), (D, PART_D)):
        s.finish()
        s.start(part[1][2])
    O.finish()
    O.start(OUT_ORDER[4])
    early.finish()
    early.start(BITS[4])
    got_w.wait()
    dn[...] = mm_nt(dproj[...], w[...])
    for i in range(3):
        Q[i].finish()
        Q[i].start(ORDERS[i][1])
    got_dh.wait()
    for g in got_x:
        g.wait()
    late[...] = jnp.zeros_like(late)

    def add_vec(i, v):
        late[i : i + 1, :] += jnp.sum(v, axis=0, keepdims=True)

    rb = 128

    def back(i, _):
        rs = pl.ds(pl.multiple_of(i * rb, rb), rb)
        xs = x[rs, :].astype(F32)
        centred = xs - jnp.mean(xs, axis=-1, keepdims=True)
        r = lax.rsqrt(jnp.mean(centred * centred, axis=-1, keepdims=True) + 1e-06)
        xh = centred * r
        g = dn[rs, :]
        add_vec(0, g * xh)
        add_vec(1, g)
        gy = g * gain[...]
        mean_gy = jnp.mean(gy, axis=-1, keepdims=True)
        mean_gx = jnp.mean(gy * xh, axis=-1, keepdims=True)
        obuf[rs, :] = (dh[rs, :] + r * (gy - mean_gy - xh * mean_gx)).astype(BF)
        add_vec(2, dproj[rs, pl.ds(0, width)].astype(F32))
        add_vec(3, dproj[rs, pl.ds(2 * width, width)].astype(F32))
        return 0

    lax.fori_loop(0, rows // rb, back, 0)
    later.start(BITS[0])
    copies = [
        fetch(obuf.at[pl.ds(0, half)], gt_hbm.at[pl.ds(far, half)], 0),
        fetch(obuf.at[pl.ds(half, half)], gt_hbm.at[pl.ds(near, half)], 1),
    ]
    def put_a(i, v):
        fc2_out[:, 0:256] = v

    def put_b(i, v):
        fc2_out[:, 256:384] = v

    def put_c(i, v):
        fc1_out[:, pl.ds(i[0] * width, 256)] = v

    def put_d(i, v):
        fc1_out[:, pl.ds(i[0] * width + 256, 512)] = v

    def put_o(i, v):
        out_out[...] = v

    early.finish()
    vec_out[...] = early.ref[...]
    for s, put in ((A, put_a), (B, put_b), (C, put_c), (D, put_d), (O, put_o)):
        s.last(put)
    for stage in range(1, 5):
        later.finish()
        later.start(BITS[stage])
        for i in range(3):
            if stage < 4:
                Q[i].finish()
                Q[i].start(ORDERS[i][stage + 1])
            else:

                def put_q(_, v, i=i):
                    qkv_out[:, pl.ds(i * third, third)] = v

                Q[i].last(put_q)
    later.finish()
    late_out[...] = later.ref[...]
    for c in copies:
        c.wait()


def call_attention_backward(tokens, info, gain, proj, norm, att, dh, db, da, lse, delta, w, vec, pa, pb, pc, pd):
    rows, width = tokens.shape
    half = rows // 2
    block, wide = width // 16, pa.shape[-2]
    sds = jax.ShapeDtypeStruct
    V = pltpu.VMEM
    stages = (
        stage_shapes(*PART_A, wide, 256)
        + stage_shapes(*PART_B, wide, 128)
        + stage_shapes(*PART_C, block, 256)
        + stage_shapes(*PART_D, block, 512)
        + stage_shapes(MATRIX, OUT_ORDER, block, width // 2)
        + [s for order in ORDERS for s in stage_shapes(MATRIX, order, block, width // 2)]
    )
    copies = 3 + len(stages) + 10
    return pl.pallas_call(
        attention_backward,
        out_shape=(
            sds((rows, width), BF), sds((block, 3 * width // 2), F32), sds((block, width // 2), F32), sds((block, 2 * width), F32),
            sds((wide, width // 2), F32), sds((16, width), F32), sds((8, width), F32),
        ),
        in_specs=[any_spec(), vmem_spec(), vmem_spec()] + [any_spec()] * 6 + [vmem_spec(), vmem_spec(), any_spec(), vmem_spec()] + [any_spec()] * 4,
        out_specs=(any_spec(),) + (vmem_spec(),) * 6,
        scratch_shapes=[
            V((rows, width), BF), V((rows + half, 3 * width), BF), V((rows, width), BF), V((rows, width), BF),
            V((rows, width), F32), V((rows, width), BF), V((rows + half, width), BF), V((width, 3 * width), BF),
            V((width, rows), BF), V((width, rows), BF), V((2, 16, half), F32),
            V((rows, rows), F32), V((half, half), F32), V((half, half), F32),
            V((half, width), F32), V((half, width), F32), V((rows, 3 * width), BF), V((rows, width), F32),
            V((3, 2, 2, 2, 2, 2, block, width // 2), BF), V((2, 2, 2, 2, 2, block, width // 2), BF), V((rows, width), BF),
        ] + [V(p.shape, BF) for p in (pa, pb, pc, pd)] + [V((8, width), F32), V((10, 16, width), F32), V((10, 8, width), F32)]
        + [V(s, BF) for s in stages] + [
            pltpu.SemaphoreType.DMA((13,)), pltpu.SemaphoreType.DMA((copies,)), pltpu.SemaphoreType.DMA((copies,)),
        ],
        compiler_params=pltpu.CompilerParams(collective_id=1, has_side_effects=True, vmem_limit_bytes=63 << 20),
        name="attention_backward",
    )(tokens, info, gain, proj, norm, att, dh, db, da, lse, delta, w, vec, pa, pb, pc, pd)


def finish(out_in, gt_in, qkv_in, o_in, f1_in, f2_in, vec, late, out, gt, g1, b1, qkv, qb, vb, o, ob, g2, b2, f1, f1b, f2, f2b, rm, buf, sems):
    pairs = ((out_in, out), (gt_in, gt))
    loads = [pltpu.make_async_copy(src, buf.at[i], sems.at[i]) for i, (src, _) in enumerate(pairs)]
    for c in loads:
        c.start()
    qkv[...], o[...], f1[...], f2[...] = qkv_in[...], o_in[...], f1_in[...], f2_in[...]
    width = g1.shape[0]
    for ref, src, i in ((g1, late, 0), (b1, late, 1), (qb, late, 2), (vb, late, 3), (ob, vec, 6), (g2, vec, 4), (b2, vec, 5), (f2b, vec, 7)):
        ref[...] = src[i, :]
    for i in range(4):
        f1b[pl.ds(i * width, width)] = vec[8 + i, :]
    sums = jnp.sum(vec[0:4, :], axis=1, keepdims=True)
    rm[...] = jnp.sqrt(sums / (vec[12:13, 0:1] * width)) + jnp.zeros((4, 128), F32)
    stores = []
    for i, (_, dst) in enumerate(pairs):
        loads[i].wait()
        c = pltpu.make_async_copy(buf.at[i], dst, sems.at[2 + i])
        c.start()
        stores.append(c)
    for c in stores:
        c.wait()


def call_finish(out, gt, qkv, o, f1, f2, vec, late, hid):
    rows, width = out.shape
    sds = jax.ShapeDtypeStruct
    line = sds((width,), F32)
    shapes = (
        sds(out.shape, BF), sds(gt.shape, BF), line, line, sds(qkv.shape, F32), line, line, sds(o.shape, F32), line, line, line,
        sds(f1.shape, F32), sds((hid,), F32), sds(f2.shape, F32), line, sds((4, 128), F32),
    )
    return pl.pallas_call(
        finish,
        out_shape=shapes,
        in_specs=[any_spec(), any_spec()] + [vmem_spec()] * 6,
        out_specs=(any_spec(), any_spec()) + (vmem_spec(),) * 14,
        scratch_shapes=[pltpu.VMEM((2, rows, width), BF), pltpu.SemaphoreType.DMA((4,))],
        name="finish",
    )(out, gt, qkv, o, f1, f2, vec, late)


def layer_norm(values, norm_gain, norm_bias):
    average = jnp.mean(values, axis=-1, keepdims=True)
    centred = values - average
    variance = jnp.mean(centred * centred, axis=-1, keepdims=True)
    return centred * lax.rsqrt(variance + 1e-06) * norm_gain + norm_bias


def exact_gelu(values):
    return jax.nn.gelu(values, approximate=False)


def on_device_general(
    tokens,
    segment_ids,
    keep_mask,
    gain_one,
    bias_one,
    qkv_weight,
    query_bias,
    value_bias,
    out_weight,
    out_bias,
    gain_two,
    bias_two,
    fc1_weight,
    fc1_bias,
    fc2_weight,
    fc2_bias,
    cotangent,
):
    sequences, tile_rows, model_width = tokens.shape
    length = segment_ids.shape[1]
    count_rows = sequences * tile_rows
    head_block = 4 * HEAD_DIM
    score_scale = HEAD_DIM ** (-0.5)
    offset = lax.axis_index("tile") * tile_rows
    query_ids = lax.dynamic_slice_in_dim(segment_ids, offset, tile_rows, 1)
    query_keep = lax.dynamic_slice_in_dim(keep_mask, offset, tile_rows, 1)
    positions = offset + jnp.arange(tile_rows, dtype=jnp.int32)
    key_places = jnp.arange(length, dtype=jnp.int32)
    own_slot = positions[:, None] == key_places[None, :]
    usable = (keep_mask[:, None, :] == 1) | own_slot[None]
    allowed = ((query_ids[:, :, None] == segment_ids[:, None, :]) & usable)[:, None]
    flattened = tokens.reshape(count_rows, model_width).astype(jnp.float32)
    normed = layer_norm(flattened, gain_one, bias_one)
    normed_low = normed.astype(jnp.bfloat16)
    key_bias = jnp.zeros_like(query_bias)
    projected = jnp.dot(
        normed_low, qkv_weight, preferred_element_type=jnp.float32
    ) + jnp.concatenate([query_bias, key_bias, value_bias])
    projected_low = projected.astype(jnp.bfloat16).reshape(sequences, tile_rows, 3 * model_width)
    queries = projected_low[..., :model_width]
    shared_local = projected_low[..., model_width:]
    shared_all = lax.all_gather(shared_local, "tile", axis=1, tiled=True)
    keys_all = shared_all[..., :model_width]
    values_all = shared_all[..., model_width:]
    key_count = shared_all.shape[1]

    def split_heads(source, column):
        sliced = source[..., column : column + head_block]
        return sliced.reshape(sliced.shape[0], sliced.shape[1], 4, HEAD_DIM)

    def block_scores(query_part, key_part):
        scores = (
            jnp.einsum("sqhe,skhe->shqk", query_part, key_part, preferred_element_type=jnp.float32)
            * score_scale
        )
        return jnp.where(allowed, scores, -1e30)

    attended_parts = []
    logsums = []
    for column in range(0, model_width, head_block):
        masked = block_scores(split_heads(queries, column), split_heads(keys_all, column))
        row_peak = jnp.max(masked, axis=-1, keepdims=True)
        exponent = jnp.exp(masked - row_peak)
        row_total = jnp.sum(exponent, axis=-1, keepdims=True)
        softmax_probs = (exponent / row_total).astype(jnp.bfloat16)
        logsums.append(row_peak + jnp.log(row_total))
        attended_parts.append(
            jnp.einsum(
                "shqk,skhe->sqhe",
                softmax_probs,
                split_heads(values_all, column),
                preferred_element_type=jnp.float32,
            )
        )
    attended = jnp.concatenate(attended_parts, axis=2)
    attended_low = attended.reshape(count_rows, model_width).astype(jnp.bfloat16)
    branch_one = jnp.dot(attended_low, out_weight, preferred_element_type=jnp.float32) + out_bias
    hidden = flattened + branch_one
    normed_two = layer_norm(hidden, gain_two, bias_two)
    normed_two_low = normed_two.astype(jnp.bfloat16)
    inner = jnp.dot(normed_two_low, fc1_weight, preferred_element_type=jnp.float32) + fc1_bias
    active_low = exact_gelu(inner).astype(jnp.bfloat16)
    branch_two = jnp.dot(active_low, fc2_weight, preferred_element_type=jnp.float32) + fc2_bias
    result = hidden + branch_two
    output = result.astype(jnp.bfloat16).reshape(sequences, tile_rows, model_width)
    weighting = query_keep.reshape(count_rows, 1).astype(jnp.float32)
    squares = [
        jnp.sum(weighting * member * member)
        for member in (flattened, branch_one, branch_two, result)
    ]
    stats = jnp.stack(squares + [jnp.sum(weighting)])
    grad_result = cotangent.reshape(count_rows, model_width)
    fc2_grad = jnp.einsum("nf,nd->fd", active_low, grad_result, preferred_element_type=jnp.float32)
    fc2_bias_grad = jnp.sum(grad_result.astype(jnp.float32), axis=0)
    grad_active = jnp.einsum(
        "nd,fd->nf", grad_result, fc2_weight, preferred_element_type=jnp.float32
    )
    inner_value, gelu_back = jax.vjp(exact_gelu, inner)
    grad_inner_low = gelu_back(grad_active)[0].astype(jnp.bfloat16)
    fc1_grad = jnp.einsum(
        "nd,nf->df", normed_two_low, grad_inner_low, preferred_element_type=jnp.float32
    )
    fc1_bias_grad = jnp.sum(grad_inner_low.astype(jnp.float32), axis=0)
    grad_normed_two = jnp.einsum(
        "nf,df->nd", grad_inner_low, fc1_weight, preferred_element_type=jnp.float32
    )
    normed_again, norm_back_two = jax.vjp(layer_norm, hidden, gain_two, bias_two)
    grad_hidden_part, gain_two_grad, bias_two_grad = norm_back_two(grad_normed_two)
    grad_hidden = grad_result.astype(jnp.float32) + grad_hidden_part
    grad_branch_low = grad_hidden.astype(jnp.bfloat16)
    out_grad = jnp.einsum(
        "nd,ne->de", attended_low, grad_branch_low, preferred_element_type=jnp.float32
    )
    out_bias_grad = jnp.sum(grad_branch_low.astype(jnp.float32), axis=0)
    grad_attended_low = (
        jnp.einsum("ne,de->nd", grad_branch_low, out_weight, preferred_element_type=jnp.float32)
        .astype(jnp.bfloat16)
        .reshape(sequences, tile_rows, model_width)
    )
    query_grads = []
    key_grads = []
    value_grads = []
    for block_index, column in enumerate(range(0, model_width, head_block)):
        query_part = split_heads(queries, column)
        key_part = split_heads(keys_all, column)
        value_part = split_heads(values_all, column)
        grad_part = split_heads(grad_attended_low, column)
        masked = block_scores(query_part, key_part)
        probs_again = jnp.exp(masked - logsums[block_index])
        grad_probs = jnp.einsum(
            "sqhe,skhe->shqk", grad_part, value_part, preferred_element_type=jnp.float32
        )
        centre = jnp.sum(probs_again * grad_probs, axis=-1, keepdims=True)
        grad_scores = (probs_again * (grad_probs - centre)).astype(jnp.bfloat16)
        query_grads.append(
            jnp.einsum("shqk,skhe->sqhe", grad_scores, key_part, preferred_element_type=jnp.float32)
            * score_scale
        )
        key_grads.append(
            jnp.einsum(
                "shqk,sqhe->skhe", grad_scores, query_part, preferred_element_type=jnp.float32
            )
            * score_scale
        )
        value_grads.append(
            jnp.einsum(
                "shqk,sqhe->skhe",
                probs_again.astype(jnp.bfloat16),
                grad_part,
                preferred_element_type=jnp.float32,
            )
        )
    grad_query = jnp.concatenate(query_grads, axis=2).reshape(sequences, tile_rows, model_width)
    grad_key_full = jnp.concatenate(key_grads, axis=2).reshape(sequences, key_count, model_width)
    grad_value_full = jnp.concatenate(value_grads, axis=2).reshape(
        sequences, key_count, model_width
    )
    grad_shared_full = jnp.concatenate([grad_key_full, grad_value_full], axis=-1)
    grad_shared = lax.psum_scatter(
        grad_shared_full.astype(jnp.bfloat16), "tile", scatter_dimension=1, tiled=True
    ).astype(jnp.float32)
    grad_projected_low = (
        jnp.concatenate([grad_query, grad_shared], axis=-1)
        .astype(jnp.bfloat16)
        .reshape(count_rows, 3 * model_width)
    )
    qkv_grad = jnp.einsum(
        "nd,ne->de", normed_low, grad_projected_low, preferred_element_type=jnp.float32
    )
    column_sums = jnp.sum(grad_projected_low.astype(jnp.float32), axis=0)
    query_bias_grad = column_sums[:model_width]
    value_bias_grad = column_sums[2 * model_width :]
    grad_normed = jnp.einsum(
        "ne,de->nd", grad_projected_low, qkv_weight, preferred_element_type=jnp.float32
    )
    normed_first, norm_back_one = jax.vjp(layer_norm, flattened, gain_one, bias_one)
    grad_tokens_part, gain_one_grad, bias_one_grad = norm_back_one(grad_normed)
    grad_tokens = (
        (grad_hidden + grad_tokens_part)
        .astype(jnp.bfloat16)
        .reshape(sequences, tile_rows, model_width)
    )
    totals_small = lax.psum(
        (
            gain_one_grad,
            bias_one_grad,
            query_bias_grad,
            value_bias_grad,
            out_bias_grad,
            gain_two_grad,
            bias_two_grad,
            fc1_bias_grad,
            fc2_bias_grad,
            stats,
        ),
        ("dp", "tile"),
    )
    matrices = (qkv_grad, out_grad, fc1_grad, fc2_grad)
    row_shares = (
        lax.psum_scatter(
            matrices[0].astype(jnp.bfloat16), "dp", scatter_dimension=0, tiled=True
        ).astype(jnp.float32),
        lax.psum_scatter(
            matrices[1].astype(jnp.bfloat16), "dp", scatter_dimension=0, tiled=True
        ).astype(jnp.float32),
        lax.psum_scatter(
            matrices[2].astype(jnp.bfloat16), "dp", scatter_dimension=0, tiled=True
        ).astype(jnp.float32),
        lax.psum_scatter(
            matrices[3].astype(jnp.bfloat16), "dp", scatter_dimension=0, tiled=True
        ).astype(jnp.float32),
    )
    reduced = (
        lax.psum_scatter(
            row_shares[0].astype(jnp.bfloat16), "tile", scatter_dimension=1, tiled=True
        ).astype(jnp.float32),
        lax.psum_scatter(
            row_shares[1].astype(jnp.bfloat16), "tile", scatter_dimension=1, tiled=True
        ).astype(jnp.float32),
        lax.psum_scatter(
            row_shares[2].astype(jnp.bfloat16), "tile", scatter_dimension=1, tiled=True
        ).astype(jnp.float32),
        lax.psum_scatter(
            row_shares[3].astype(jnp.bfloat16), "tile", scatter_dimension=1, tiled=True
        ).astype(jnp.float32),
    )
    totals = totals_small[9]
    root_mean = jnp.sqrt(totals[:4] / (totals[4] * model_width))
    return (
        output,
        grad_tokens,
        totals_small[0],
        totals_small[1],
        reduced[0],
        totals_small[2],
        totals_small[3],
        reduced[1],
        totals_small[4],
        totals_small[5],
        totals_small[6],
        reduced[2],
        totals_small[7],
        reduced[3],
        totals_small[8],
        root_mean,
    )


def on_device(tokens,segment_ids,keep_mask,gain_one,bias_one,qkv_weight,query_bias,value_bias,out_weight,out_bias,gain_two,bias_two,fc1_weight,fc1_bias,fc2_weight,fc2_bias,cotangent):
    _,rows,width=tokens.shape; half=rows//2
    t=lax.axis_index("tile"); base=t*rows
    ofs=(base+t*half,base+(1-t)*half,(1-t)*rows+t*half)
    def order(v): return jnp.concatenate([lax.dynamic_slice_in_dim(v,o,half,0) for o in ofs])
    s=order(segment_ids[0]); k=order(keep_mask[0])
    info=jnp.concatenate([jnp.stack([s,jnp.where(k==1,s,-1)]),jnp.zeros((6,s.shape[0]),jnp.int32)])
    row=lambda v:v[None]
    pb=jnp.concatenate([query_bias,jnp.zeros_like(query_bias),value_bias])[None]
    proj,norm,att,lse=call_forward(tokens[0],info,row(gain_one),row(bias_one),qkv_weight,pb)
    kc=jnp.broadcast_to(k[:rows,None].astype(jnp.float32),(rows,128))
    out,dh,db,da,delta,vec,*parts=call_feed_forward(tokens[0],att,cotangent[0],kc,out_weight,row(out_bias),row(gain_two),row(bias_two),fc1_weight,fc1_bias,fc2_weight,row(fc2_bias))
    gt,qg,og,f1,f2,vec,late=call_attention_backward(tokens[0],info,row(gain_one),proj,norm,att,dh,db,da,lse,delta,qkv_weight,vec,*parts)
    r=list(call_finish(out,gt,qg,og,f1,f2,vec,late,fc1_weight.shape[1]))
    r[0]=r[0][None]; r[1]=r[1][None]; r[15]=r[15][:,0]
    return tuple(r)
def fits(mesh):
    return mesh.shape["tile"] == 2 and mesh.shape["dp"] == 16


def solution(mesh):
    S=P("dp","tile",None); D=P("dp",None)
    placed=(S,D,D)+(P(),)*13+(S,)
    T=P("dp","tile")
    return jax.shard_map(on_device if fits(mesh) else on_device_general,mesh=mesh,in_specs=placed,out_specs=(S,S,P(),P(),T,P(),P(),T,P(),P(),P(),T,P(),T,P(),P()),check_vma=False)
```

```python
import itertools

import jax
import jax.numpy as jnp
from jax import lax
from jax.experimental import pallas as pl
from jax.experimental.pallas import tpu as pltpu
from jax.sharding import PartitionSpec as P

HEAD_DIM = 64
PAIR = 2 * HEAD_DIM
MASKED = -1e30
MESH = pl.DeviceIdType.MESH
BF = jnp.bfloat16
F32 = jnp.float32
NT = (((1,), (1,)), ((), ()))
TN = (((0,), (0,)), ((), ()))


def mm(a, b):
    return jnp.dot(a, b, preferred_element_type=F32)


def mm_nt(a, b):
    return lax.dot_general(a, b, NT, preferred_element_type=F32)


def mm_tn(a, b):
    return lax.dot_general(a, b, TN, preferred_element_type=F32)


def any_spec():
    return pl.BlockSpec(memory_space=pl.ANY)


def vmem_spec():
    return pl.BlockSpec(memory_space=pltpu.VMEM)


def gelu_and_slope(z):
    bell = jnp.exp(z * z * -0.5)
    t = 1.0 / (1.0 + jnp.abs(z) * (0.3275911 * 0.7071067811865476))
    tail = t * (0.127414796 + t * (-0.142248368 + t * (0.7107068705 + t * (-0.7265760135 + t * 0.5307027145)))) * bell
    upper = jnp.where(z >= 0, 1.0 - tail, tail)
    return z * upper, upper + z * bell * 0.3989422804014327


def place():
    d = lax.axis_index("dp")
    return dict(core=d % 2, y=d // 2 % 2, z0=d // 4 % 2, z1=d // 8, x=lax.axis_index("tile"))


def peer(at, bit):
    if bit == "x":
        return {"tile": 1 - at["x"]}
    step = dict(core=1, y=2, z0=4, z1=8)[bit]
    return {"dp": lax.axis_index("dp") + step - 2 * step * at[bit]}


def send(at, bit, src, dst, send_sem, recv_sem):
    c = pltpu.make_async_remote_copy(src, dst, send_sem, recv_sem, device_id=peer(at, bit), device_id_type=MESH)
    c.start()
    return c


class Share:
    def __init__(self, at, ref, dims, order, buffers, send_sems, recv_sems, first):
        self.at, self.ref, self.dims, self.buffers = at, ref, dims, list(buffers)
        self.order, self.sems, self.next = list(order), (send_sems, recv_sems), first

    def start(self):
        bit = self.order.pop(0)
        self.axis = self.dims.index(bit)
        self.mine = self.at[bit]
        lead = (slice(None),) * self.axis
        self.other = self.buffers.pop(0)
        i, self.next = self.next, self.next + 1
        self.copy = send(self.at, bit, self.ref.at[lead + (1 - self.mine,)], self.other, self.sems[0].at[i], self.sems[1].at[i])

    def kept(self, index):
        return self.ref[index[: self.axis] + (self.mine,) + index[self.axis :]]

    def finish(self):
        self.copy.wait()
        for index in itertools.product(*map(range, self.other.shape[:-2])):
            self.other[index] = self.other[index] + self.kept(index)
        self.ref = self.other
        self.dims = self.dims[: self.axis] + self.dims[self.axis + 1 :]

    def step(self):
        self.finish()
        self.start()

    def last(self, put):
        self.copy.wait()
        for index in itertools.product(*map(range, self.other.shape[:-2])):
            put(index, self.other[index].astype(F32) + self.kept(index).astype(F32))


class Total:
    def __init__(self, at, ref, buffers, send_sems, recv_sems, first):
        self.at, self.ref, self.buffers = at, ref, buffers
        self.sems, self.next, self.stage = (send_sems, recv_sems), first, 0

    def start(self):
        i = self.next + self.stage
        self.copy = send(self.at, BITS[self.stage], self.ref, self.buffers.at[self.stage], self.sems[0].at[i], self.sems[1].at[i])

    def finish(self):
        self.copy.wait()
        got = self.buffers.at[self.stage]
        got[...] = self.ref[...] + got[...]
        self.ref, self.stage = got, self.stage + 1

    def step(self):
        self.finish()
        self.start()


BITS = ("core", "y", "z0", "z1", "x")
PART_A = (("z1", "z0", "y"), ("z0", "y", "z1"))
PART_B = (("z1", "z0", "x"), ("x", "z0", "z1"))
PART_C = (("x", "j", "z1", "z0"), ("z0", "x", "z1"))
PART_D = (("x", "j", "z1", "y"), ("y", "x", "z1"))
MATRIX = ("z1", "z0", "y", "core", "x")
ORDERS = (("core", "x", "y", "z0", "z1"), ("core", "y", "z0", "x", "z1"), ("core", "z0", "x", "y", "z1"))
OUT_ORDER = ("core", "y", "z0", "x", "z1")


def stage_shapes(dims, order, rows, cols):
    left, shapes = list(dims), []
    for bit in order:
        left.remove(bit)
        shapes.append((2,) * len(left) + (rows, cols))
    return shapes


def everything(
    tok, seg_hbm, keep_hbm, g1_hbm, bias1_hbm, wqkv_hbm, qb_hbm, vb_hbm, ow_hbm, ob_hbm, g2_hbm, bias2_hbm, w1_hbm, b1_hbm, w2_hbm, c2_hbm, dy_hbm,
    out_hbm, gt_hbm, qkv_hbm, o_hbm, fc1_hbm, fc2_hbm, vec_hbm, late_hbm,
    seg, keep, g1, bias1, ob, g2, bias2, c2, qb, vb, b1,
    x, xn, wqkv, proj, att, scale_two, lse, delta, stat, mask, dy, ow, w1, w2, hidden, xhat, rstd, n2, n2t, z, da, act, di,
    f1, f2, r1, r2, pa, pb, pc, pd, d_att, qg, biases, vec, late, early_buf, late_buf, *rest,
):
    rows, width = x.shape
    half = rows // 2
    heads = width // HEAD_DIM
    cols = width
    chunks = w2.shape[0] // cols
    stage_bufs = list(rest[:-7])
    sems, send_sems, recv_sems, core_send, core_recv, next_send, next_recv = rest[-7:]
    at = place()
    t = at["x"]
    far, near = t * half, (1 - t) * half
    own_rows, halo_rows, near_rows = pl.ds(0, rows), pl.ds(rows, half), pl.ds(half, half)
    barrier = pltpu.get_barrier_semaphore()
    for bit in BITS:
        pl.semaphore_signal(barrier, inc=1, device_id=peer(at, bit), device_id_type=MESH)

    def fetch(src, dst, i):
        c = pltpu.make_async_copy(src, dst, sems.at[i])
        c.start()
        return c

    small = ((seg_hbm, seg), (keep_hbm, keep), (g1_hbm, g1), (bias1_hbm, bias1), (ob_hbm, ob), (g2_hbm, g2), (bias2_hbm, bias2), (c2_hbm, c2), (qb_hbm, qb), (vb_hbm, vb), (b1_hbm, b1))
    got_small = [fetch(src, dst, 6 + 2 * chunks + i) for i, (src, dst) in enumerate(small)]
    got_x = [fetch(tok.at[pl.ds(far, half)], x.at[pl.ds(0, half)], 0), fetch(tok.at[pl.ds(near, half)], x.at[near_rows], 1)]
    got_wqkv = fetch(wqkv_hbm, wqkv, 2)
    got_dy = [fetch(dy_hbm.at[pl.ds(far, half)], dy.at[pl.ds(0, half)], 3), fetch(dy_hbm.at[pl.ds(near, half)], dy.at[near_rows], 4)]
    got_ow = fetch(ow_hbm, ow, 5)
    pl.semaphore_wait(barrier, len(BITS))
    used = [0]

    def job(bit, src, dst):
        i, used[0] = used[0], used[0] + 1
        return send(at, bit, src, dst, send_sems.at[i], recv_sems.at[i])

    token_halo = job("x", tok.at[pl.ds(near, half)], xn.at[halo_rows])

    for g in got_small:
        g.wait()
    starts = (t * (rows + half), t * rows + (1 - t) * half, (1 - t) * rows + t * half)
    slots = [pl.ds(pl.multiple_of(s, 128), half) for s in starts]
    ids = jnp.concatenate([seg[:, s] for s in slots], axis=1)
    kept_row = jnp.concatenate([keep[:, s] for s in slots], axis=1)
    key_row = jnp.where(kept_row == 1, ids, -1)
    table = jnp.concatenate([ids, key_row, kept_row, jnp.zeros((5, rows + half), jnp.int32)], axis=0)
    columns = jnp.transpose(table.astype(F32))
    id_col, key_col, kept_col = columns[:, 0:1], columns[:, 1:2], columns[:, 2:3]
    id_row, key_row = ids.astype(F32), key_row.astype(F32)
    query_at = lax.broadcasted_iota(jnp.int32, (half, rows + half), 0)
    key_at = lax.broadcasted_iota(jnp.int32, (half, rows + half), 1)
    for part in range(2):
        same = id_col[part * half : (part + 1) * half] == key_row
        mask[pl.ds(part * half, half), :] = jnp.where(same | (query_at + part * half == key_at), 0.0, MASKED)
    rstd[...] = jnp.broadcast_to(kept_col[:rows], rstd.shape)
    for i in range(chunks):
        biases[i : i + 1, :] = b1[i * cols : (i + 1) * cols].reshape(1, cols)
    for i, ref in enumerate((g1, bias1, ob, g2, bias2, c2, qb, vb)):
        biases[8 + i : 9 + i, :] = ref[...].reshape(1, width)
    gain_one, bias_one, out_bias, gain_two, bias_two, fc2_bias = (biases[8 + i : 9 + i, :] for i in range(6))
    vec[...] = jnp.zeros_like(vec)
    late[...] = jnp.zeros_like(late)
    vec[12:13, 0:128] = jnp.sum(rstd[...], axis=0, keepdims=True)
    rb = 128

    def normalize(src, dst, start, count):
        def one(i, _):
            rs = pl.ds(pl.multiple_of(start + i * rb, rb), rb)
            v = src[rs, :].astype(F32)
            centred = v - jnp.mean(v, axis=-1, keepdims=True)
            var = jnp.mean(centred * centred, axis=-1, keepdims=True)
            dst[rs, :] = (centred * lax.rsqrt(var + 1e-06) * gain_one + bias_one).astype(BF)
            return 0

        lax.fori_loop(0, count // rb, one, 0)

    def project(start, count, which):
        rs = pl.ds(start, count)
        for j in which:
            js = pl.ds(j * width, width)
            v = mm(xn[rs, :], wqkv[:, js])
            if j == 0:
                proj[rs, js] = (v + biases[14:15, :]).astype(BF) * BF(HEAD_DIM ** (-0.5))
            elif j == 1:
                proj[rs, js] = v.astype(BF)
            else:
                proj[rs, js] = (v + biases[15:16, :]).astype(BF)

    lane = lax.broadcasted_iota(jnp.int32, (1, PAIR), 1)

    def cut(v, head):
        return jnp.where((lane < HEAD_DIM) == (head == 0), v, 0).astype(BF)

    def both(a, b):
        return jnp.where(lane < HEAD_DIM, a, b)

    def scores(p, query_rows, mask_rows, key_start, keys):
        c = pl.multiple_of(p * PAIR, PAIR)
        ks = pl.ds(key_start, keys)
        q, k, v = proj[query_rows, pl.ds(c, PAIR)], proj[ks, pl.ds(width + c, PAIR)], proj[ks, pl.ds(2 * width + c, PAIR)]
        total, new_tops = None, []
        for head in range(2):
            s = mm_nt(cut(q, head), k) + mask[mask_rows, ks]
            top = jnp.max(s, axis=-1, keepdims=True)
            e = jnp.exp(s - top).astype(BF)
            ones = jnp.broadcast_to(cut(jnp.ones((1, PAIR), BF), head), (keys, PAIR))
            part = mm(e, jnp.concatenate([cut(v, head), ones], axis=1))
            total = part if total is None else total + part
            new_tops.append(top)
        return total[:, :PAIR], total[:, PAIR:], both(new_tops[0], new_tops[1])

    def attended(p, rs, value, sums, tops):
        c = pl.ds(pl.multiple_of(p * PAIR, PAIR), PAIR)
        att[rs, c] = (value / sums).astype(BF)
        hidden[rs, c] = tops + jnp.log(sums)

    def attend_far(p, _):
        rs = pl.ds(0, half)
        attended(p, rs, *scores(p, rs, rs, 0, rows))
        return 0

    def attend_near(p, _):
        c = pl.ds(pl.multiple_of(p * PAIR, PAIR), PAIR)
        z[pl.ds(0, half), c], z[near_rows, c], da[near_rows, c] = scores(p, near_rows, near_rows, 0, rows)
        return 0

    def attend_halo(p, _):
        c = pl.ds(pl.multiple_of(p * PAIR, PAIR), PAIR)
        before = da[near_rows, c]
        value, sums, after = scores(p, near_rows, near_rows, rows, half)
        tops = jnp.maximum(before, after)
        old, new = jnp.exp(before - tops), jnp.exp(after - tops)
        attended(p, near_rows, value * new + z[pl.ds(0, half), c] * old, sums * new + z[near_rows, c] * old, tops)
        return 0

    for g in got_x:
        g.wait()
    normalize(x, xn, 0, rows)
    got_wqkv.wait()
    got_w = []
    for c in range(chunks):
        got_w.append(fetch(w1_hbm.at[:, pl.ds(c * cols, cols)], w1.at[:, pl.ds(c * cols, cols)], 6 + 2 * c))
        got_w.append(fetch(w2_hbm.at[pl.ds(c * cols, cols)], w2.at[pl.ds(c * cols, cols)], 7 + 2 * c))
    project(0, rows, (0, 1, 2))
    lax.fori_loop(0, heads // 2, attend_far, 0, unroll=3)
    lax.fori_loop(0, heads // 2, attend_near, 0, unroll=3)
    token_halo.wait()
    normalize(xn, xn, rows, half)
    project(rows, half, (1, 2, 0))
    lax.fori_loop(0, heads // 2, attend_halo, 0, unroll=3)
    head_row = lax.broadcasted_iota(jnp.int32, (16, width), 0) * HEAD_DIM
    lane_at = lax.broadcasted_iota(jnp.int32, (16, width), 1)
    first = jnp.where(lane_at == head_row, 1.0, 0.0).astype(BF)
    logs = hidden[...]
    high = logs.astype(BF)
    mid = (logs - high.astype(F32)).astype(BF)
    low = (logs - high.astype(F32) - mid.astype(F32)).astype(BF)
    lse[...] = mm_nt(first, high) + mm_nt(first, mid) + mm_nt(first, low)
    got_ow.wait()

    def add_vec(ref, i, v):
        ref[i : i + 1, :] += jnp.sum(v, axis=0, keepdims=True)

    def front(i, _):
        rs = pl.ds(pl.multiple_of(i * rb, rb), rb)
        branch = mm(att[rs, :], ow[...]) + out_bias
        xs = x[rs, :].astype(F32)
        h = xs + branch
        hidden[rs, :] = h
        kept = rstd[rs, :][:, 0:1]
        add_vec(vec, 0, kept * xs * xs)
        add_vec(vec, 1, kept * branch * branch)
        centred = h - jnp.mean(h, axis=-1, keepdims=True)
        r = lax.rsqrt(jnp.mean(centred * centred, axis=-1, keepdims=True) + 1e-06)
        xh = centred * r
        xhat[rs, :] = xh
        scale_two[rs, :] = jnp.broadcast_to(r, (rb, PAIR))
        n2[rs, :] = (xh * gain_two + bias_two).astype(BF)
        return 0

    lax.fori_loop(0, rows // rb, front, 0)
    n2t[...] = jnp.transpose(n2[...])
    for g in got_dy:
        g.wait()

    def core_copies(c):
        hi, lo = c // 2, c % 2
        other = 1 - at["core"]
        pairs = ((f1.at[:, :, :, other], r1.at[hi, lo]), (f2.at[:, :, other], r2.at[hi, lo]))
        return [
            pltpu.make_async_remote_copy(s, d, core_send.at[i, c], core_recv.at[i, c], device_id=peer(at, "core"), device_id_type=MESH)
            for i, (s, d) in enumerate(pairs)
        ]

    def next_copies(c):
        hi, lo = c // 2, c % 2
        jobs = (
            ("x", r2.at[hi, lo, 1 - t, :, :, pl.ds(0, 256)], pa.at[hi, lo]),
            ("y", r2.at[hi, lo, :, 1 - at["y"], :, pl.ds(256, 128)], pb.at[hi, lo]),
            ("y", r1.at[hi, lo, :, :, 1 - at["y"], :, pl.ds(0, 256)], pc.at[hi, lo]),
            ("z0", r1.at[hi, lo, :, 1 - at["z0"], :, :, pl.ds(256, 512)], pd.at[hi, lo]),
        )
        return [
            pltpu.make_async_remote_copy(s, d, next_send.at[i, c], next_recv.at[i, c], device_id=peer(at, bit), device_id_type=MESH)
            for i, (bit, s, d) in enumerate(jobs)
        ]

    def pass_on(c):
        hi, lo = c // 2, c % 2
        mine = at["core"]
        for copy in core_copies(c):
            copy.wait()

        def one(i, _):
            a, b, d = i // 4, i // 2 % 2, i % 2
            r1[hi, lo, a, b, d] += f1[a, b, d, mine]
            return 0

        lax.fori_loop(0, 8, one, 0, unroll=2)

        def two(i, _):
            r2[hi, lo, i // 2, i % 2] += f2[i // 2, i % 2, mine]
            return 0

        lax.fori_loop(0, 4, two, 0)
        for copy in next_copies(c):
            copy.start()

    def chunk(c, _):
        for i in range(2):
            pltpu.make_async_copy(w2_hbm.at[pl.ds(0, cols)], w2.at[pl.ds(0, cols)], sems.at[6 + 2 * c + i]).wait()
        here = pl.ds(pl.multiple_of(c * cols, cols), cols)
        z[...] = mm(n2[...], w1[:, here]) + biases[pl.ds(c, 1), :]
        da[...] = mm_nt(dy[...], w2[here, :])
        gr = 64
        bsum = jnp.zeros((1, cols), F32)
        for i in range(rows // gr):
            rs = pl.ds(i * gr, gr)
            a, s = gelu_and_slope(z[rs, :])
            act[rs, here] = a.astype(BF)
            d = (da[rs, :] * s).astype(BF)
            di[rs, here] = d
            bsum = bsum + jnp.sum(d.astype(F32), axis=0, keepdims=True)
        vec[pl.ds(8 + c, 1), :] = bsum

        @pl.when(c > 0)
        def _():
            pass_on(c - 1)

        f1[...] = mm(n2t[...], di[:, here]).astype(BF).reshape(f1.shape)
        g = mm_tn(act[:, here], dy[...]).astype(BF)
        f2[0] = g[:, : width // 2].reshape(f2.shape[1:])
        f2[1] = g[:, width // 2 :].reshape(f2.shape[1:])
        for copy in core_copies(c):
            copy.start()
        return 0

    lax.fori_loop(0, chunks, chunk, 0)
    da[...] = mm_nt(di[...], w1[...])
    pass_on(chunks - 1)

    def middle(i, _):
        rs = pl.ds(pl.multiple_of(i * rb, rb), rb)
        g = da[rs, :]
        xh = xhat[rs, :]
        add_vec(vec, 4, g * xh)
        add_vec(vec, 5, g)
        gy = g * gain_two
        mean_gy = jnp.mean(gy, axis=-1, keepdims=True)
        mean_gx = jnp.mean(gy * xh, axis=-1, keepdims=True)
        dys = dy[rs, :].astype(F32)
        add_vec(vec, 7, dys)
        dh = dys + scale_two[rs, :][:, 0:1] * (gy - mean_gy - xh * mean_gx)
        xhat[rs, :] = dh
        low = dh.astype(BF)
        n2[rs, :] = low
        add_vec(vec, 6, low.astype(F32))
        return 0

    lax.fori_loop(0, rows // rb, middle, 0)
    d_att[own_rows, :] = mm_nt(n2[...], ow[...]).astype(BF)
    mine = jnp.where((lane_at >= head_row) & (lane_at < head_row + HEAD_DIM), 1.0, 0.0).astype(BF)
    prod = d_att[own_rows, :].astype(F32) * att[...].astype(F32)
    hi = prod.astype(BF)
    lo = (prod - hi.astype(F32)).astype(BF)
    delta[...] = mm_nt(mine, hi) + mm_nt(mine, lo)
    halos = [
        job("x", d_att.at[near_rows], d_att.at[halo_rows]),
        job("x", lse.at[:, near_rows], stat.at[0]),
        job("x", delta.at[:, near_rows], stat.at[1]),
    ]

    def share(ref, dims, order):
        bufs = [stage_bufs.pop(0) for _ in order]
        first, used[0] = used[0], used[0] + len(order)
        return Share(at, ref, dims, order, bufs, send_sems, recv_sems, first)

    og = qg.at[2]
    A, B, C, D = (share(ref, *part) for ref, part in ((pa, PART_A), (pb, PART_B), (pc, PART_C), (pd, PART_D)))
    O = share(og, MATRIX, OUT_ORDER)
    Q = [share(qg.at[i], MATRIX, ORDERS[i]) for i in range(3)]
    early = Total(at, vec, early_buf, send_sems, recv_sems, used[0])
    later = Total(at, late, late_buf, send_sems, recv_sems, used[0] + 5)
    early.start()
    def settle(c, _):
        hi, lo = c // 2, c % 2
        for copy in next_copies(c):
            copy.wait()
        for i in range(2):
            pa[hi, lo, i] += r2[hi, lo, t, i, :, 0:256]
            pb[hi, lo, i] += r2[hi, lo, i, at["y"], :, 256:384]
            for j in range(2):
                pc[hi, lo, i, j] += r1[hi, lo, i, j, at["y"], :, 0:256]
                pd[hi, lo, i, j] += r1[hi, lo, i, at["z0"], j, :, 256:768]
        return 0

    n2t[...] = jnp.transpose(att[...])
    for i in range(2):
        og_half = mm(n2t[...], n2[:, i * (width // 2) : (i + 1) * (width // 2)]).astype(BF)
        og[:, :, :, :, i] = og_half.reshape((2, 2, 2, 2) + og.shape[-2:])
    O.start()

    key_at = lax.broadcasted_iota(jnp.int32, (half, rows), 0)
    query_at = lax.broadcasted_iota(jnp.int32, (half, rows), 1)
    for part in range(2):
        same = key_col[part * half : (part + 1) * half] == id_row[:, :rows]
        mask[pl.ds(part * half, half), pl.ds(0, rows)] = jnp.where(same | (query_at == key_at + part * half), 0.0, MASKED)
    mask[pl.ds(0, half), halo_rows] = jnp.where(key_col[half:rows] == id_row[:, rows:], 0.0, MASKED)
    mask[near_rows, halo_rows] = jnp.where(key_col[rows:] == id_row[:, half:rows], 0.0, MASKED)

    def own(p, _):
        c = pl.multiple_of(p * PAIR, PAIR)
        col, kcol, vcol = pl.ds(c, PAIR), pl.ds(width + c, PAIR), pl.ds(2 * width + c, PAIR)
        q, k, v = proj[own_rows, col], proj[:, kcol], proj[:, vcol]
        do = d_att[own_rows, col]
        gq = gk = gv = gn = None
        for head in range(2):
            qh, kh, doh = cut(q, head), cut(k, head), cut(do, head)
            ls = lse[pl.ds(2 * p + head, 1), :]
            de = delta[pl.ds(2 * p + head, 1), :]
            prob = jnp.exp(mm_nt(k[:rows], qh) + mask[:, pl.ds(0, rows)] - ls)
            ds = (prob * (mm_nt(v[:rows], doh) - de)).astype(BF)
            a = mm(prob.astype(BF), doh)
            b = mm(ds, qh)
            c = mm_tn(ds, kh[:rows])
            prob = jnp.exp(mm_nt(k[rows:], qh[half:]) + mask[near_rows, halo_rows] - ls[:, half:])
            ds = (prob * (mm_nt(v[rows:], doh[half:]) - de[:, half:])).astype(BF)
            d = mm_tn(ds, kh[rows:])
            gv = a if gv is None else gv + a
            gk = b if gk is None else gk + b
            gq = c if gq is None else gq + c
            gn = d if gn is None else gn + d
        scale = HEAD_DIM ** (-0.5)
        di[pl.ds(0, half), col] = (gq[:half] * scale).astype(BF)
        di[near_rows, col] = ((gq[half:] + gn) * scale).astype(BF)
        di[pl.ds(0, half), kcol] = gk[:half].astype(BF)
        di[pl.ds(0, half), vcol] = gv[:half].astype(BF)
        z[pl.ds(0, half), col] = gk[half:]
        z[near_rows, col] = gv[half:]
        return 0

    def halo(p, _):
        c = pl.multiple_of(p * PAIR, PAIR)
        col, kcol, vcol = pl.ds(c, PAIR), pl.ds(width + c, PAIR), pl.ds(2 * width + c, PAIR)
        q, k, v = proj[halo_rows, col], proj[near_rows, kcol], proj[near_rows, vcol]
        do = d_att[halo_rows, col]
        gk, gv = z[pl.ds(0, half), col], z[near_rows, col]
        for head in range(2):
            qh, doh = cut(q, head), cut(do, head)
            ls = stat[0, pl.ds(2 * p + head, 1), :]
            de = stat[1, pl.ds(2 * p + head, 1), :]
            prob = jnp.exp(mm_nt(k, qh) + mask[pl.ds(0, half), halo_rows] - ls)
            ds = (prob * (mm_nt(v, doh) - de)).astype(BF)
            gv = gv + mm(prob.astype(BF), doh)
            gk = gk + mm(ds, qh)
        di[near_rows, kcol] = gk.astype(BF)
        di[near_rows, vcol] = gv.astype(BF)
        return 0

    n2t[...] = jnp.transpose(xn[own_rows, :])
    early.step()
    lax.fori_loop(0, 2, own, 0, unroll=2)
    lax.fori_loop(0, chunks, settle, 0)
    for s in (A, B, C, D):
        s.start()
    O.step()
    early.step()
    lax.fori_loop(2, heads // 2, own, 0, unroll=2)
    for h in halos:
        h.wait()
    lax.fori_loop(0, heads // 2, halo, 0, unroll=3)
    early.step()
    third = width // 2

    def weigh(j):
        g = mm(n2t[...], di[:, pl.ds(j * width, width)]).astype(BF)
        for i in range(2):
            side, part = divmod(2 * j + i, 3)
            qg[part, :, :, :, :, side] = g[:, i * third : (i + 1) * third].reshape((2, 2, 2, 2) + qg.shape[-2:])

    weigh(0)
    weigh(1)
    Q[0].start()
    weigh(2)
    Q[1].start()
    Q[2].start()
    early.step()
    da[...] = mm_nt(di[:, pl.ds(0, 3 * width)], wqkv[...])
    for s in (A, B, C, D):
        s.step()
    for s in Q:
        s.step()
    O.step()
    z[...] = mm(act[...], w2[...])

    def back(i, _):
        rs = pl.ds(pl.multiple_of(i * rb, rb), rb)
        xs = x[rs, :].astype(F32)
        centred = xs - jnp.mean(xs, axis=-1, keepdims=True)
        r = lax.rsqrt(jnp.mean(centred * centred, axis=-1, keepdims=True) + 1e-06)
        xh = centred * r
        g = da[rs, :]
        add_vec(late, 0, g * xh)
        add_vec(late, 1, g)
        gy = g * gain_one
        mean_gy = jnp.mean(gy, axis=-1, keepdims=True)
        mean_gx = jnp.mean(gy * xh, axis=-1, keepdims=True)
        w1[rs, pl.ds(width, width)] = (xhat[rs, :] + r * (gy - mean_gy - xh * mean_gx)).astype(BF)
        add_vec(late, 2, di[rs, pl.ds(0, width)].astype(F32))
        add_vec(late, 3, di[rs, pl.ds(2 * width, width)].astype(F32))
        branch = z[rs, :] + fc2_bias
        result = hidden[rs, :] + branch
        w1[rs, pl.ds(0, width)] = result.astype(BF)
        kept = rstd[rs, :][:, 0:1]
        add_vec(late, 4, kept * branch * branch)
        add_vec(late, 5, kept * result * result)
        return 0

    lax.fori_loop(0, rows // rb, back, 0)
    later.start()
    copies = [
        fetch(w1.at[pl.ds(0, half), pl.ds(0, width)], out_hbm.at[pl.ds(far, half)], 0),
        fetch(w1.at[near_rows, pl.ds(0, width)], out_hbm.at[pl.ds(near, half)], 1),
        fetch(w1.at[pl.ds(0, half), pl.ds(width, width)], gt_hbm.at[pl.ds(far, half)], 2),
        fetch(w1.at[near_rows, pl.ds(width, width)], gt_hbm.at[pl.ds(near, half)], 3),
    ]

    block, wide = width // 16, w2.shape[0] // 16

    def put_a(_, v):
        z[pl.ds(0, wide), 0:256] = v

    def put_b(_, v):
        z[pl.ds(0, wide), 256:384] = v

    def put_c(i, v):
        z[pl.ds(wide + i[0] * block, block), 0:256] = v

    def put_d(i, v):
        z[pl.ds(wide + i[0] * block, block), 256:768] = v

    def put_o(_, v):
        z[pl.ds(wide + 2 * block, block), 0:384] = v

    early.finish()
    copies.append(fetch(early.ref, vec_hbm, 4))
    for s in (A, B, C, D):
        s.step()
    O.step()
    for s in Q:
        s.step()
    later.step()
    for s in Q:
        s.step()
    later.step()
    O.step()
    for s in Q:
        s.step()
    later.step()
    for s, put in ((A, put_a), (B, put_b), (C, put_c), (D, put_d)):
        s.last(put)
    O.last(put_o)
    copies += [
        fetch(z.at[pl.ds(0, wide), pl.ds(0, width // 2)], fc2_hbm, 5),
        fetch(z.at[pl.ds(wide, block)], fc1_hbm.at[:, pl.ds(0, width)], 6),
        fetch(z.at[pl.ds(wide + block, block)], fc1_hbm.at[:, pl.ds(width, width)], 7),
        fetch(z.at[pl.ds(wide + 2 * block, block), pl.ds(0, width // 2)], o_hbm, 8),
    ]
    later.step()
    for i in range(3):

        def put_q(_, v, i=i):
            da[pl.ds(i * block, block), 0:384] = v

        Q[i].last(put_q)
        copies.append(fetch(da.at[pl.ds(i * block, block), pl.ds(0, third)], qkv_hbm.at[:, pl.ds(i * third, third)], 10 + i))
    later.finish()
    copies.append(fetch(later.ref, late_hbm, 9))
    for c in copies:
        c.wait()


def call_everything(tokens, seg, keep, g1, bias1, wqkv, qb, vb, ow, ob, g2, bias2, w1, b1, w2, c2, dy):
    rows, width = tokens.shape
    half = rows // 2
    hid = w1.shape[1]
    chunks = hid // width
    block, wide = width // 16, hid // 16
    sds = jax.ShapeDtypeStruct
    V = pltpu.VMEM
    parts = ((2, 2, 2, wide, 256), (2, 2, 2, wide, 128), (2, 2, 2, 2, block, 256), (2, 2, 2, 2, block, 512))
    stages = (
        stage_shapes(*PART_A, wide, 256)
        + stage_shapes(*PART_B, wide, 128)
        + stage_shapes(*PART_C, block, 256)
        + stage_shapes(*PART_D, block, 512)
        + stage_shapes(MATRIX, OUT_ORDER, block, width // 2)
        + [s for order in ORDERS for s in stage_shapes(MATRIX, order, block, width // 2)]
    )
    jobs = 4 + len(stages) + 10
    DMA = pltpu.SemaphoreType.DMA
    return pl.pallas_call(
        everything,
        out_shape=(
            sds((rows, width), BF), sds((rows, width), BF), sds((block, 3 * width // 2), F32), sds((block, width // 2), F32),
            sds((block, hid // 2), F32), sds((wide, width // 2), F32), sds((16, width), F32), sds((8, width), F32),
        ),
        in_specs=[any_spec()] * 17,
        out_specs=(any_spec(),) * 8,
        scratch_shapes=[V(seg.shape, jnp.int32), V(keep.shape, jnp.int32)] + [V((width,), F32)] * 8 + [
            V((hid,), F32),
            V((rows, width), BF), V((rows + half, width), BF), V((width, 3 * width), BF), V((rows + half, 3 * width), BF),
            V((rows, width), BF), V((rows, PAIR), F32), V((16, rows), F32), V((16, rows), F32), V((2, 16, half), F32),
            V((rows, rows + half), F32), V((rows, width), BF), V((width, width), BF), V((width, hid), BF), V((hid, width), BF),
            V((rows, width), F32), V((rows, width), F32), V((rows, PAIR), F32), V((rows, width), BF), V((width, rows), BF),
            V((rows, width), F32), V((rows, width), F32), V((rows, hid), BF), V((rows, hid), BF),
            V((2, 2, 2, 2, block, width), BF), V((2, 2, 2, wide, width // 2), BF),
            V((2, 2, 2, 2, 2, block, width), BF), V((2, 2, 2, 2, wide, width // 2), BF),
        ] + [V(s, BF) for s in parts] + [
            V((rows + half, width), BF), V((3, 2, 2, 2, 2, 2, block, width // 2), BF),
            V((16, width), F32), V((16, width), F32), V((8, width), F32), V((5, 16, width), F32), V((5, 8, width), F32),
        ] + [V(s, BF) for s in stages] + [
            DMA((17 + 2 * chunks,)), DMA((jobs,)), DMA((jobs,)),
            DMA((2, chunks)), DMA((2, chunks)), DMA((4, chunks)), DMA((4, chunks)),
        ],
        compiler_params=pltpu.CompilerParams(collective_id=0, has_side_effects=True, vmem_limit_bytes=67043328),
        name="everything",
    )(tokens, seg, keep, g1, bias1, wqkv, qb, vb, ow, ob, g2, bias2, w1, b1, w2, c2, dy)


def finish(*refs):
    ins, outs, bufs, sems = refs[:8], refs[8:24], refs[24:-1], refs[-1]
    loads = [pltpu.make_async_copy(src, buf, sems.at[i]) for i, (src, buf) in enumerate(zip(ins, bufs[:8]))]
    for c in loads:
        c.start()
    vec, late = bufs[6:8]
    lines = bufs[8:]
    width = lines[0].shape[0]
    out, gt, g1, b1, qkv, qb, vb, o, ob, g2, b2, f1, f1b, f2, f2b, rm = outs
    stores = []

    def store(src, dst):
        c = pltpu.make_async_copy(src, dst, sems.at[8 + len(stores)])
        c.start()
        stores.append(c)

    loads[6].wait()
    loads[7].wait()
    rows = ((g1, late, 0), (b1, late, 1), (qb, late, 2), (vb, late, 3), (ob, vec, 6), (g2, vec, 4), (b2, vec, 5), (f2b, vec, 7))
    for (dst, src, i), line in zip(rows, lines):
        line[...] = src[i, :]
        store(line, dst)
    for i in range(4):
        lines[8][pl.ds(i * width, width)] = vec[8 + i, :]
    store(lines[8], f1b)
    squares = jnp.concatenate([vec[0:2, :], late[4:6, :]], axis=0)
    ratio = jnp.sqrt(jnp.sum(squares, axis=1, keepdims=True) / (vec[12:13, 0:1] * width))
    diagonal = lax.broadcasted_iota(jnp.int32, (4, 128), 0) == lax.broadcasted_iota(jnp.int32, (4, 128), 1)
    lines[9][...] = jnp.sum(jnp.where(diagonal, ratio, 0.0), axis=0, keepdims=True)
    store(lines[9], rm)
    for i, dst in enumerate((out, gt, qkv, o, f1, f2)):
        loads[i].wait()
        store(bufs[i], dst)
    for c in stores:
        c.wait()


def call_finish(out, gt, qkv, o, f1, f2, vec, late, hid):
    width = out.shape[1]
    sds = jax.ShapeDtypeStruct
    line = sds((width,), F32)
    shapes = (
        sds(out.shape, BF), sds(gt.shape, BF), line, line, sds(qkv.shape, F32), line, line, sds(o.shape, F32), line, line, line,
        sds(f1.shape, F32), sds((hid,), F32), sds(f2.shape, F32), line, sds((1, 128), F32),
    )
    args = (out, gt, qkv, o, f1, f2, vec, late)
    return pl.pallas_call(
        finish,
        out_shape=shapes,
        in_specs=[any_spec()] * 8,
        out_specs=(any_spec(),) * 16,
        scratch_shapes=[pltpu.VMEM(v.shape, v.dtype) for v in args] + [pltpu.VMEM((width,), F32)] * 8
        + [pltpu.VMEM((hid,), F32), pltpu.VMEM((1, 128), F32), pltpu.SemaphoreType.DMA((24,))],
        name="finish",
    )(*args)


def layer_norm(values, norm_gain, norm_bias):
    average = jnp.mean(values, axis=-1, keepdims=True)
    centred = values - average
    variance = jnp.mean(centred * centred, axis=-1, keepdims=True)
    return centred * lax.rsqrt(variance + 1e-06) * norm_gain + norm_bias


def exact_gelu(values):
    return jax.nn.gelu(values, approximate=False)


def on_device_general(
    tokens,
    segment_ids,
    keep_mask,
    gain_one,
    bias_one,
    qkv_weight,
    query_bias,
    value_bias,
    out_weight,
    out_bias,
    gain_two,
    bias_two,
    fc1_weight,
    fc1_bias,
    fc2_weight,
    fc2_bias,
    cotangent,
):
    sequences, tile_rows, model_width = tokens.shape
    length = segment_ids.shape[1]
    count_rows = sequences * tile_rows
    head_block = 4 * HEAD_DIM
    score_scale = HEAD_DIM ** (-0.5)
    offset = lax.axis_index("tile") * tile_rows
    query_ids = lax.dynamic_slice_in_dim(segment_ids, offset, tile_rows, 1)
    query_keep = lax.dynamic_slice_in_dim(keep_mask, offset, tile_rows, 1)
    positions = offset + jnp.arange(tile_rows, dtype=jnp.int32)
    key_places = jnp.arange(length, dtype=jnp.int32)
    own_slot = positions[:, None] == key_places[None, :]
    usable = (keep_mask[:, None, :] == 1) | own_slot[None]
    allowed = ((query_ids[:, :, None] == segment_ids[:, None, :]) & usable)[:, None]
    flattened = tokens.reshape(count_rows, model_width).astype(jnp.float32)
    normed = layer_norm(flattened, gain_one, bias_one)
    normed_low = normed.astype(jnp.bfloat16)
    key_bias = jnp.zeros_like(query_bias)
    projected = jnp.dot(
        normed_low, qkv_weight, preferred_element_type=jnp.float32
    ) + jnp.concatenate([query_bias, key_bias, value_bias])
    projected_low = projected.astype(jnp.bfloat16).reshape(sequences, tile_rows, 3 * model_width)
    queries = projected_low[..., :model_width]
    shared_local = projected_low[..., model_width:]
    shared_all = lax.all_gather(shared_local, "tile", axis=1, tiled=True)
    keys_all = shared_all[..., :model_width]
    values_all = shared_all[..., model_width:]
    key_count = shared_all.shape[1]

    def split_heads(source, column):
        sliced = source[..., column : column + head_block]
        return sliced.reshape(sliced.shape[0], sliced.shape[1], 4, HEAD_DIM)

    def block_scores(query_part, key_part):
        scores = (
            jnp.einsum("sqhe,skhe->shqk", query_part, key_part, preferred_element_type=jnp.float32)
            * score_scale
        )
        return jnp.where(allowed, scores, -1e30)

    attended_parts = []
    logsums = []
    for column in range(0, model_width, head_block):
        masked = block_scores(split_heads(queries, column), split_heads(keys_all, column))
        row_peak = jnp.max(masked, axis=-1, keepdims=True)
        exponent = jnp.exp(masked - row_peak)
        row_total = jnp.sum(exponent, axis=-1, keepdims=True)
        softmax_probs = (exponent / row_total).astype(jnp.bfloat16)
        logsums.append(row_peak + jnp.log(row_total))
        attended_parts.append(
            jnp.einsum(
                "shqk,skhe->sqhe",
                softmax_probs,
                split_heads(values_all, column),
                preferred_element_type=jnp.float32,
            )
        )
    attended = jnp.concatenate(attended_parts, axis=2)
    attended_low = attended.reshape(count_rows, model_width).astype(jnp.bfloat16)
    branch_one = jnp.dot(attended_low, out_weight, preferred_element_type=jnp.float32) + out_bias
    hidden = flattened + branch_one
    normed_two = layer_norm(hidden, gain_two, bias_two)
    normed_two_low = normed_two.astype(jnp.bfloat16)
    inner = jnp.dot(normed_two_low, fc1_weight, preferred_element_type=jnp.float32) + fc1_bias
    active_low = exact_gelu(inner).astype(jnp.bfloat16)
    branch_two = jnp.dot(active_low, fc2_weight, preferred_element_type=jnp.float32) + fc2_bias
    result = hidden + branch_two
    output = result.astype(jnp.bfloat16).reshape(sequences, tile_rows, model_width)
    weighting = query_keep.reshape(count_rows, 1).astype(jnp.float32)
    squares = [
        jnp.sum(weighting * member * member)
        for member in (flattened, branch_one, branch_two, result)
    ]
    stats = jnp.stack(squares + [jnp.sum(weighting)])
    grad_result = cotangent.reshape(count_rows, model_width)
    fc2_grad = jnp.einsum("nf,nd->fd", active_low, grad_result, preferred_element_type=jnp.float32)
    fc2_bias_grad = jnp.sum(grad_result.astype(jnp.float32), axis=0)
    grad_active = jnp.einsum(
        "nd,fd->nf", grad_result, fc2_weight, preferred_element_type=jnp.float32
    )
    inner_value, gelu_back = jax.vjp(exact_gelu, inner)
    grad_inner_low = gelu_back(grad_active)[0].astype(jnp.bfloat16)
    fc1_grad = jnp.einsum(
        "nd,nf->df", normed_two_low, grad_inner_low, preferred_element_type=jnp.float32
    )
    fc1_bias_grad = jnp.sum(grad_inner_low.astype(jnp.float32), axis=0)
    grad_normed_two = jnp.einsum(
        "nf,df->nd", grad_inner_low, fc1_weight, preferred_element_type=jnp.float32
    )
    normed_again, norm_back_two = jax.vjp(layer_norm, hidden, gain_two, bias_two)
    grad_hidden_part, gain_two_grad, bias_two_grad = norm_back_two(grad_normed_two)
    grad_hidden = grad_result.astype(jnp.float32) + grad_hidden_part
    grad_branch_low = grad_hidden.astype(jnp.bfloat16)
    out_grad = jnp.einsum(
        "nd,ne->de", attended_low, grad_branch_low, preferred_element_type=jnp.float32
    )
    out_bias_grad = jnp.sum(grad_branch_low.astype(jnp.float32), axis=0)
    grad_attended_low = (
        jnp.einsum("ne,de->nd", grad_branch_low, out_weight, preferred_element_type=jnp.float32)
        .astype(jnp.bfloat16)
        .reshape(sequences, tile_rows, model_width)
    )
    query_grads = []
    key_grads = []
    value_grads = []
    for block_index, column in enumerate(range(0, model_width, head_block)):
        query_part = split_heads(queries, column)
        key_part = split_heads(keys_all, column)
        value_part = split_heads(values_all, column)
        grad_part = split_heads(grad_attended_low, column)
        masked = block_scores(query_part, key_part)
        probs_again = jnp.exp(masked - logsums[block_index])
        grad_probs = jnp.einsum(
            "sqhe,skhe->shqk", grad_part, value_part, preferred_element_type=jnp.float32
        )
        centre = jnp.sum(probs_again * grad_probs, axis=-1, keepdims=True)
        grad_scores = (probs_again * (grad_probs - centre)).astype(jnp.bfloat16)
        query_grads.append(
            jnp.einsum("shqk,skhe->sqhe", grad_scores, key_part, preferred_element_type=jnp.float32)
            * score_scale
        )
        key_grads.append(
            jnp.einsum(
                "shqk,sqhe->skhe", grad_scores, query_part, preferred_element_type=jnp.float32
            )
            * score_scale
        )
        value_grads.append(
            jnp.einsum(
                "shqk,sqhe->skhe",
                probs_again.astype(jnp.bfloat16),
                grad_part,
                preferred_element_type=jnp.float32,
            )
        )
    grad_query = jnp.concatenate(query_grads, axis=2).reshape(sequences, tile_rows, model_width)
    grad_key_full = jnp.concatenate(key_grads, axis=2).reshape(sequences, key_count, model_width)
    grad_value_full = jnp.concatenate(value_grads, axis=2).reshape(
        sequences, key_count, model_width
    )
    grad_shared_full = jnp.concatenate([grad_key_full, grad_value_full], axis=-1)
    grad_shared = lax.psum_scatter(
        grad_shared_full.astype(jnp.bfloat16), "tile", scatter_dimension=1, tiled=True
    ).astype(jnp.float32)
    grad_projected_low = (
        jnp.concatenate([grad_query, grad_shared], axis=-1)
        .astype(jnp.bfloat16)
        .reshape(count_rows, 3 * model_width)
    )
    qkv_grad = jnp.einsum(
        "nd,ne->de", normed_low, grad_projected_low, preferred_element_type=jnp.float32
    )
    column_sums = jnp.sum(grad_projected_low.astype(jnp.float32), axis=0)
    query_bias_grad = column_sums[:model_width]
    value_bias_grad = column_sums[2 * model_width :]
    grad_normed = jnp.einsum(
        "ne,de->nd", grad_projected_low, qkv_weight, preferred_element_type=jnp.float32
    )
    normed_first, norm_back_one = jax.vjp(layer_norm, flattened, gain_one, bias_one)
    grad_tokens_part, gain_one_grad, bias_one_grad = norm_back_one(grad_normed)
    grad_tokens = (
        (grad_hidden + grad_tokens_part)
        .astype(jnp.bfloat16)
        .reshape(sequences, tile_rows, model_width)
    )
    totals_small = lax.psum(
        (
            gain_one_grad,
            bias_one_grad,
            query_bias_grad,
            value_bias_grad,
            out_bias_grad,
            gain_two_grad,
            bias_two_grad,
            fc1_bias_grad,
            fc2_bias_grad,
            stats,
        ),
        ("dp", "tile"),
    )
    matrices = (qkv_grad, out_grad, fc1_grad, fc2_grad)
    row_shares = (
        lax.psum_scatter(
            matrices[0].astype(jnp.bfloat16), "dp", scatter_dimension=0, tiled=True
        ).astype(jnp.float32),
        lax.psum_scatter(
            matrices[1].astype(jnp.bfloat16), "dp", scatter_dimension=0, tiled=True
        ).astype(jnp.float32),
        lax.psum_scatter(
            matrices[2].astype(jnp.bfloat16), "dp", scatter_dimension=0, tiled=True
        ).astype(jnp.float32),
        lax.psum_scatter(
            matrices[3].astype(jnp.bfloat16), "dp", scatter_dimension=0, tiled=True
        ).astype(jnp.float32),
    )
    reduced = (
        lax.psum_scatter(
            row_shares[0].astype(jnp.bfloat16), "tile", scatter_dimension=1, tiled=True
        ).astype(jnp.float32),
        lax.psum_scatter(
            row_shares[1].astype(jnp.bfloat16), "tile", scatter_dimension=1, tiled=True
        ).astype(jnp.float32),
        lax.psum_scatter(
            row_shares[2].astype(jnp.bfloat16), "tile", scatter_dimension=1, tiled=True
        ).astype(jnp.float32),
        lax.psum_scatter(
            row_shares[3].astype(jnp.bfloat16), "tile", scatter_dimension=1, tiled=True
        ).astype(jnp.float32),
    )
    totals = totals_small[9]
    root_mean = jnp.sqrt(totals[:4] / (totals[4] * model_width))
    return (
        output,
        grad_tokens,
        totals_small[0],
        totals_small[1],
        reduced[0],
        totals_small[2],
        totals_small[3],
        reduced[1],
        totals_small[4],
        totals_small[5],
        totals_small[6],
        reduced[2],
        totals_small[7],
        reduced[3],
        totals_small[8],
        root_mean,
    )


def on_device(tokens, segment_ids, keep_mask, gain_one, bias_one, qkv_weight, query_bias, value_bias, out_weight, out_bias, gain_two, bias_two, fc1_weight, fc1_bias, fc2_weight, fc2_bias, cotangent):
    out, gt, qg, og, f1, f2, vec, late = call_everything(
        tokens[0], segment_ids, keep_mask, gain_one, bias_one, qkv_weight, query_bias, value_bias, out_weight, out_bias,
        gain_two, bias_two, fc1_weight, fc1_bias, fc2_weight, fc2_bias, cotangent[0],
    )
    r = list(call_finish(out, gt, qg, og, f1, f2, vec, late, fc1_weight.shape[1]))
    r[0] = r[0][None]
    r[1] = r[1][None]
    r[15] = r[15][0, :4]
    return tuple(r)


def fits(mesh):
    return mesh.shape["tile"] == 2 and mesh.shape["dp"] == 16


def solution(mesh):
    S, D, T = P("dp", "tile", None), P("dp", None), P("dp", "tile")
    return jax.shard_map(
        on_device if fits(mesh) else on_device_general,
        mesh=mesh,
        in_specs=(S, D, D) + (P(),) * 13 + (S,),
        out_specs=(S, S, P(), P(), T, P(), P(), T, P(), P(), P(), T, P(), T, P(), P()),
        check_vma=False,
    )
```

```python
import itertools

import jax
import jax.numpy as jnp
from jax import lax
from jax.experimental import pallas as pl
from jax.experimental.pallas import tpu as pltpu
from jax.sharding import PartitionSpec as P

HEAD_DIM = 64
PAIR = 2 * HEAD_DIM
MASKED = -1e30
MESH = pl.DeviceIdType.MESH
BF = jnp.bfloat16
F32 = jnp.float32
NT = (((1,), (1,)), ((), ()))
TN = (((0,), (0,)), ((), ()))


def mm(a, b):
    return jnp.dot(a, b, preferred_element_type=F32)


def mm_nt(a, b):
    return lax.dot_general(a, b, NT, preferred_element_type=F32)


def mm_tn(a, b):
    return lax.dot_general(a, b, TN, preferred_element_type=F32)


def any_spec():
    return pl.BlockSpec(memory_space=pl.ANY)


def vmem_spec():
    return pl.BlockSpec(memory_space=pltpu.VMEM)


def gelu_and_slope(z):
    bell = jnp.exp(z * z * -0.5)
    t = 1.0 / (1.0 + jnp.abs(z) * (0.3275911 * 0.7071067811865476))
    tail = t * (0.127414796 + t * (-0.142248368 + t * (0.7107068705 + t * (-0.7265760135 + t * 0.5307027145)))) * bell
    upper = jnp.where(z >= 0, 1.0 - tail, tail)
    return z * upper, upper + z * bell * 0.3989422804014327


def place():
    d = lax.axis_index("dp")
    return dict(core=d % 2, y=d // 2 % 2, z0=d // 4 % 2, z1=d // 8, x=lax.axis_index("tile"))


def peer(at, bit):
    if bit == "x":
        return {"tile": 1 - at["x"]}
    step = dict(core=1, y=2, z0=4, z1=8)[bit]
    return {"dp": lax.axis_index("dp") + step - 2 * step * at[bit]}


def send(at, bit, src, dst, send_sem, recv_sem):
    c = pltpu.make_async_remote_copy(src, dst, send_sem, recv_sem, device_id=peer(at, bit), device_id_type=MESH)
    c.start()
    return c


class Share:
    def __init__(self, at, ref, dims, order, buffers, send_sems, recv_sems, first):
        self.at, self.ref, self.dims, self.buffers = at, ref, dims, list(buffers)
        self.order, self.sems, self.next = list(order), (send_sems, recv_sems), first

    def start(self):
        bit = self.order.pop(0)
        self.axis = self.dims.index(bit)
        self.mine = self.at[bit]
        lead = (slice(None),) * self.axis
        self.other = self.buffers.pop(0)
        i, self.next = self.next, self.next + 1
        self.copy = send(self.at, bit, self.ref.at[lead + (1 - self.mine,)], self.other, self.sems[0].at[i], self.sems[1].at[i])

    def kept(self, index):
        return self.ref[index[: self.axis] + (self.mine,) + index[self.axis :]]

    def finish(self):
        self.copy.wait()
        for index in itertools.product(*map(range, self.other.shape[:-2])):
            self.other[index] = self.other[index] + self.kept(index)
        self.ref = self.other
        self.dims = self.dims[: self.axis] + self.dims[self.axis + 1 :]

    def step(self):
        self.finish()
        self.start()

    def last(self, put):
        self.copy.wait()
        for index in itertools.product(*map(range, self.other.shape[:-2])):
            put(index, self.other[index].astype(F32) + self.kept(index).astype(F32))


class Total:
    def __init__(self, at, ref, buffers, send_sems, recv_sems, first):
        self.at, self.ref, self.buffers = at, ref, buffers
        self.sems, self.next, self.stage = (send_sems, recv_sems), first, 0

    def start(self):
        i = self.next + self.stage
        self.copy = send(self.at, BITS[self.stage], self.ref, self.buffers.at[self.stage], self.sems[0].at[i], self.sems[1].at[i])

    def finish(self):
        self.copy.wait()
        got = self.buffers.at[self.stage]
        got[...] = self.ref[...] + got[...]
        self.ref, self.stage = got, self.stage + 1

    def step(self):
        self.finish()
        self.start()


BITS = ("core", "z1", "y", "z0", "x")
PART_A = (("z1", "z0", "y"), ("z0", "y", "z1"))
PART_B = (("z1", "z0", "x"), ("x", "z0", "z1"))
PART_C = (("x", "j", "z1", "z0"), ("z0", "x", "z1"))
PART_D = (("x", "j", "z1", "y"), ("y", "x", "z1"))
MATRIX = ("z1", "z0", "y", "core", "x")
ORDERS = (("core", "x", "y", "z0", "z1"), ("core", "y", "z0", "x", "z1"), ("core", "z0", "x", "y", "z1"))
OUT_ORDER = ("core", "x", "y", "z0", "z1")


def stage_shapes(dims, order, rows, cols):
    left, shapes = list(dims), []
    for bit in order:
        left.remove(bit)
        shapes.append((2,) * len(left) + (rows, cols))
    return shapes


def everything(
    tok, seg_hbm, keep_hbm, g1_hbm, bias1_hbm, wqkv_hbm, qb_hbm, vb_hbm, ow_hbm, ob_hbm, g2_hbm, bias2_hbm, w1_hbm, b1_hbm, w2_hbm, c2_hbm, dy_hbm,
    out_hbm, gt_hbm, qkv_hbm, o_hbm, fc1_hbm, fc2_hbm, vec_hbm, late_hbm,
    seg, keep, g1, bias1, ob, g2, bias2, c2, qb, vb, b1,
    x, xn, wqkv, proj, att, scale_two, lse, delta, stat, mask, dy, ow, w1, w2, hidden, xhat, rstd, n2, n2t, z, da, act, di,
    f1, f2, r1, r2, pa, pb, pc, pd, d_att, qg, biases, vec, late, early_buf, late_buf, *rest,
):
    rows, width = x.shape
    half = rows // 2
    heads = width // HEAD_DIM
    cols = width
    chunks = w2.shape[0] // cols
    stage_bufs = list(rest[:-7])
    sems, send_sems, recv_sems, core_send, core_recv, next_send, next_recv = rest[-7:]
    at = place()
    t = at["x"]
    far, near = t * half, (1 - t) * half
    own_rows, halo_rows, near_rows = pl.ds(0, rows), pl.ds(rows, half), pl.ds(half, half)
    barrier = pltpu.get_barrier_semaphore()
    for bit in BITS:
        pl.semaphore_signal(barrier, inc=1, device_id=peer(at, bit), device_id_type=MESH)

    def fetch(src, dst, i):
        c = pltpu.make_async_copy(src, dst, sems.at[i])
        c.start()
        return c

    small = ((seg_hbm, seg), (keep_hbm, keep), (g1_hbm, g1), (bias1_hbm, bias1), (ob_hbm, ob), (g2_hbm, g2), (bias2_hbm, bias2), (c2_hbm, c2), (qb_hbm, qb), (vb_hbm, vb), (b1_hbm, b1))
    got_small = [fetch(src, dst, 6 + 2 * chunks + i) for i, (src, dst) in enumerate(small)]
    got_x = [fetch(tok.at[pl.ds(far, half)], x.at[pl.ds(0, half)], 0), fetch(tok.at[pl.ds(near, half)], x.at[near_rows], 1)]
    got_wqkv = fetch(wqkv_hbm, wqkv, 2)
    pl.semaphore_wait(barrier, len(BITS))
    used = [0]

    def job(bit, src, dst):
        i, used[0] = used[0], used[0] + 1
        return send(at, bit, src, dst, send_sems.at[i], recv_sems.at[i])

    token_halo = job("x", tok.at[pl.ds(near, half)], xn.at[halo_rows])

    for g in got_small:
        g.wait()
    starts = (t * (rows + half), t * rows + (1 - t) * half, (1 - t) * rows + t * half)
    slots = [pl.ds(pl.multiple_of(s, 128), half) for s in starts]
    ids = jnp.concatenate([seg[:, s] for s in slots], axis=1)
    kept_row = jnp.concatenate([keep[:, s] for s in slots], axis=1)
    key_row = jnp.where(kept_row == 1, ids, -1)
    table = jnp.concatenate([ids, key_row, kept_row, jnp.zeros((5, rows + half), jnp.int32)], axis=0)
    columns = jnp.transpose(table.astype(F32))
    id_col, key_col, kept_col = columns[:, 0:1], columns[:, 1:2], columns[:, 2:3]
    id_row, key_row = ids.astype(F32), key_row.astype(F32)
    query_at = lax.broadcasted_iota(jnp.int32, (half, rows + half), 0)
    key_at = lax.broadcasted_iota(jnp.int32, (half, rows + half), 1)
    for part in range(2):
        same = id_col[part * half : (part + 1) * half] == key_row
        mask[pl.ds(part * half, half), :] = jnp.where(same | (query_at + part * half == key_at), 0.0, MASKED)
    rstd[...] = jnp.broadcast_to(kept_col[:rows], rstd.shape)
    for i in range(chunks):
        biases[i : i + 1, :] = b1[i * cols : (i + 1) * cols].reshape(1, cols)
    for i, ref in enumerate((g1, bias1, ob, g2, bias2, c2, qb, vb)):
        biases[8 + i : 9 + i, :] = ref[...].reshape(1, width)
    gain_one, bias_one, out_bias, gain_two, bias_two, fc2_bias = (biases[8 + i : 9 + i, :] for i in range(6))
    vec[...] = jnp.zeros_like(vec)
    late[...] = jnp.zeros_like(late)
    vec[12:13, 0:128] = jnp.sum(rstd[...], axis=0, keepdims=True)
    rb = 128

    def normalize(src, dst, start, count):
        def one(i, _):
            rs = pl.ds(pl.multiple_of(start + i * rb, rb), rb)
            v = src[rs, :].astype(F32)
            centred = v - jnp.mean(v, axis=-1, keepdims=True)
            var = jnp.mean(centred * centred, axis=-1, keepdims=True)
            dst[rs, :] = (centred * lax.rsqrt(var + 1e-06) * gain_one + bias_one).astype(BF)
            return 0

        lax.fori_loop(0, count // rb, one, 0, unroll=2)

    def project(start, count, which):
        rs = pl.ds(start, count)
        for j in which:
            js = pl.ds(j * width, width)
            v = mm(xn[rs, :], wqkv[:, js])
            if j == 0:
                proj[rs, js] = (v + biases[14:15, :]).astype(BF) * BF(HEAD_DIM ** (-0.5))
            elif j == 1:
                proj[rs, js] = v.astype(BF)
            else:
                proj[rs, js] = (v + biases[15:16, :]).astype(BF)

    lane = lax.broadcasted_iota(jnp.int32, (1, PAIR), 1)

    def cut(v, head):
        return jnp.where((lane < HEAD_DIM) == (head == 0), v, 0).astype(BF)

    def both(a, b):
        return jnp.where(lane < HEAD_DIM, a, b)

    def scores(p, query_rows, mask_rows, key_start, keys):
        c = pl.multiple_of(p * PAIR, PAIR)
        ks = pl.ds(key_start, keys)
        q, k, v = proj[query_rows, pl.ds(c, PAIR)], proj[ks, pl.ds(width + c, PAIR)], proj[ks, pl.ds(2 * width + c, PAIR)]
        total, new_tops = None, []
        for head in range(2):
            s = mm_nt(cut(q, head), k) + mask[mask_rows, ks]
            top = jnp.max(s, axis=-1, keepdims=True)
            e = jnp.exp(s - top).astype(BF)
            ones = jnp.broadcast_to(cut(jnp.ones((1, PAIR), BF), head), (keys, PAIR))
            part = mm(e, jnp.concatenate([cut(v, head), ones], axis=1))
            total = part if total is None else total + part
            new_tops.append(top)
        return total[:, :PAIR], total[:, PAIR:], both(new_tops[0], new_tops[1])

    def attended(p, rs, value, sums, tops):
        c = pl.ds(pl.multiple_of(p * PAIR, PAIR), PAIR)
        att[rs, c] = (value / sums).astype(BF)
        hidden[rs, c] = tops + jnp.log(sums)

    def attend_far(p, _):
        rs = pl.ds(0, half)
        attended(p, rs, *scores(p, rs, rs, 0, rows))
        return 0

    def attend_near(p, _):
        c = pl.ds(pl.multiple_of(p * PAIR, PAIR), PAIR)
        z[pl.ds(0, half), c], z[near_rows, c], da[near_rows, c] = scores(p, near_rows, near_rows, 0, rows)
        return 0

    def attend_halo(p, _):
        c = pl.ds(pl.multiple_of(p * PAIR, PAIR), PAIR)
        before = da[near_rows, c]
        value, sums, after = scores(p, near_rows, near_rows, rows, half)
        tops = jnp.maximum(before, after)
        old, new = jnp.exp(before - tops), jnp.exp(after - tops)
        attended(p, near_rows, value * new + z[pl.ds(0, half), c] * old, sums * new + z[near_rows, c] * old, tops)
        return 0

    for g in got_x:
        g.wait()
    normalize(x, xn, 0, rows)
    got_wqkv.wait()
    got_dy = [fetch(dy_hbm.at[pl.ds(far, half)], dy.at[pl.ds(0, half)], 3), fetch(dy_hbm.at[pl.ds(near, half)], dy.at[near_rows], 4)]
    got_ow = fetch(ow_hbm, ow, 5)
    got_w = []
    for c in range(chunks):
        got_w.append(fetch(w1_hbm.at[:, pl.ds(c * cols, cols)], w1.at[:, pl.ds(c * cols, cols)], 6 + 2 * c))
        got_w.append(fetch(w2_hbm.at[pl.ds(c * cols, cols)], w2.at[pl.ds(c * cols, cols)], 7 + 2 * c))
    project(0, rows, (0, 1, 2))
    lax.fori_loop(0, heads // 2, attend_far, 0, unroll=3)
    lax.fori_loop(0, heads // 2, attend_near, 0, unroll=3)
    token_halo.wait()
    normalize(xn, xn, rows, half)
    project(rows, half, (1, 2))
    lax.fori_loop(0, heads // 2, attend_halo, 0, unroll=3)
    head_row = lax.broadcasted_iota(jnp.int32, (16, width), 0) * HEAD_DIM
    lane_at = lax.broadcasted_iota(jnp.int32, (16, width), 1)
    first = jnp.where(lane_at == head_row, 1.0, 0.0).astype(BF)
    logs = hidden[...]
    high = logs.astype(BF)
    mid = (logs - high.astype(F32)).astype(BF)
    low = (logs - high.astype(F32) - mid.astype(F32)).astype(BF)
    lse[...] = mm_nt(first, high) + mm_nt(first, mid) + mm_nt(first, low)
    got_ow.wait()

    def add_vec(ref, i, v):
        ref[i : i + 1, :] += jnp.sum(v, axis=0, keepdims=True)

    def front(i, _):
        rs = pl.ds(pl.multiple_of(i * rb, rb), rb)
        branch = mm(att[rs, :], ow[...]) + out_bias
        xs = x[rs, :].astype(F32)
        h = xs + branch
        hidden[rs, :] = h
        kept = rstd[rs, :][:, 0:1]
        add_vec(vec, 0, kept * xs * xs)
        add_vec(vec, 1, kept * branch * branch)
        centred = h - jnp.mean(h, axis=-1, keepdims=True)
        r = lax.rsqrt(jnp.mean(centred * centred, axis=-1, keepdims=True) + 1e-06)
        xh = centred * r
        xhat[rs, :] = xh
        scale_two[rs, :] = jnp.broadcast_to(r, (rb, PAIR))
        n2[rs, :] = (xh * gain_two + bias_two).astype(BF)
        return 0

    lax.fori_loop(0, rows // rb, front, 0, unroll=2)
    n2t[...] = jnp.transpose(n2[...])
    for g in got_dy:
        g.wait()

    def core_copies(c):
        hi, lo = c // 2, c % 2
        other = 1 - at["core"]
        pairs = ((f1.at[:, :, :, other], r1.at[hi, lo]), (f2.at[:, :, other], r2.at[hi, lo]))
        return [
            pltpu.make_async_remote_copy(s, d, core_send.at[i, c], core_recv.at[i, c], device_id=peer(at, "core"), device_id_type=MESH)
            for i, (s, d) in enumerate(pairs)
        ]

    def next_copies(c):
        hi, lo = c // 2, c % 2
        jobs = (
            ("x", r2.at[hi, lo, 1 - t, :, :, pl.ds(0, 256)], pa.at[hi, lo]),
            ("y", r2.at[hi, lo, :, 1 - at["y"], :, pl.ds(256, 128)], pb.at[hi, lo]),
            ("y", r1.at[hi, lo, :, :, 1 - at["y"], :, pl.ds(0, 256)], pc.at[hi, lo]),
            ("z0", r1.at[hi, lo, :, 1 - at["z0"], :, :, pl.ds(256, 512)], pd.at[hi, lo]),
        )
        return [
            pltpu.make_async_remote_copy(s, d, next_send.at[i, c], next_recv.at[i, c], device_id=peer(at, bit), device_id_type=MESH)
            for i, (bit, s, d) in enumerate(jobs)
        ]

    def pass_on(c):
        hi, lo = c // 2, c % 2
        mine = at["core"]
        for copy in core_copies(c):
            copy.wait()

        def one(i, _):
            a, b, d = i // 4, i // 2 % 2, i % 2
            r1[hi, lo, a, b, d] += f1[a, b, d, mine]
            return 0

        lax.fori_loop(0, 8, one, 0, unroll=2)

        def two(i, _):
            r2[hi, lo, i // 2, i % 2] += f2[i // 2, i % 2, mine]
            return 0

        lax.fori_loop(0, 4, two, 0)
        for copy in next_copies(c):
            copy.start()

    def chunk(c, _):
        for i in range(2):
            pltpu.make_async_copy(w2_hbm.at[pl.ds(0, cols)], w2.at[pl.ds(0, cols)], sems.at[6 + 2 * c + i]).wait()
        here = pl.ds(pl.multiple_of(c * cols, cols), cols)
        z[...] = mm(n2[...], w1[:, here]) + biases[pl.ds(c, 1), :]
        da[...] = mm_nt(dy[...], w2[here, :])
        gr = 64
        bsum = jnp.zeros((1, cols), F32)
        for i in range(rows // gr):
            rs = pl.ds(i * gr, gr)
            a, s = gelu_and_slope(z[rs, :])
            act[rs, here] = a.astype(BF)
            d = (da[rs, :] * s).astype(BF)
            di[rs, here] = d
            bsum = bsum + jnp.sum(d.astype(F32), axis=0, keepdims=True)
        vec[pl.ds(8 + c, 1), :] = bsum

        @pl.when(c > 0)
        def _():
            pass_on(c - 1)

        f1[...] = mm(n2t[...], di[:, here]).astype(BF).reshape(f1.shape)
        g = mm_tn(act[:, here], dy[...]).astype(BF)
        f2[0] = g[:, : width // 2].reshape(f2.shape[1:])
        f2[1] = g[:, width // 2 :].reshape(f2.shape[1:])
        for copy in core_copies(c):
            copy.start()
        return 0

    lax.fori_loop(0, chunks, chunk, 0)
    da[...] = mm_nt(di[...], w1[...])
    pass_on(chunks - 1)

    def middle(i, _):
        rs = pl.ds(pl.multiple_of(i * rb, rb), rb)
        g = da[rs, :]
        xh = xhat[rs, :]
        add_vec(vec, 4, g * xh)
        add_vec(vec, 5, g)
        gy = g * gain_two
        mean_gy = jnp.mean(gy, axis=-1, keepdims=True)
        mean_gx = jnp.mean(gy * xh, axis=-1, keepdims=True)
        dys = dy[rs, :].astype(F32)
        add_vec(vec, 7, dys)
        dh = dys + scale_two[rs, :][:, 0:1] * (gy - mean_gy - xh * mean_gx)
        xhat[rs, :] = dh
        low = dh.astype(BF)
        n2[rs, :] = low
        add_vec(vec, 6, low.astype(F32))
        return 0

    lax.fori_loop(0, rows // rb, middle, 0)
    d_att[own_rows, :] = mm_nt(n2[...], ow[...]).astype(BF)
    mine = jnp.where((lane_at >= head_row) & (lane_at < head_row + HEAD_DIM), 1.0, 0.0).astype(BF)
    prod = d_att[own_rows, :].astype(F32) * att[...].astype(F32)
    hi = prod.astype(BF)
    lo = (prod - hi.astype(F32)).astype(BF)
    delta[...] = mm_nt(mine, hi) + mm_nt(mine, lo)
    halos = [
        job("x", d_att.at[near_rows], d_att.at[halo_rows]),
        job("x", lse.at[:, near_rows], stat.at[0]),
        job("x", delta.at[:, near_rows], stat.at[1]),
    ]

    def share(ref, dims, order):
        bufs = [stage_bufs.pop(0) for _ in order]
        first, used[0] = used[0], used[0] + len(order)
        return Share(at, ref, dims, order, bufs, send_sems, recv_sems, first)

    og = qg.at[2]
    A, B, C, D = (share(ref, *part) for ref, part in ((pa, PART_A), (pb, PART_B), (pc, PART_C), (pd, PART_D)))
    O = share(og, MATRIX, OUT_ORDER)
    Q = [share(qg.at[i], MATRIX, ORDERS[i]) for i in range(3)]
    early = Total(at, vec, early_buf, send_sems, recv_sems, used[0])
    later = Total(at, late, late_buf, send_sems, recv_sems, used[0] + 5)
    early.start()
    def settle(c, _):
        hi, lo = c // 2, c % 2
        for copy in next_copies(c):
            copy.wait()
        for i in range(2):
            pa[hi, lo, i] += r2[hi, lo, t, i, :, 0:256]
            pb[hi, lo, i] += r2[hi, lo, i, at["y"], :, 256:384]
            for j in range(2):
                pc[hi, lo, i, j] += r1[hi, lo, i, j, at["y"], :, 0:256]
                pd[hi, lo, i, j] += r1[hi, lo, i, at["z0"], j, :, 256:768]
        return 0

    n2t[...] = jnp.transpose(att[...])
    for i in range(2):
        og_half = mm(n2t[...], n2[:, i * (width // 2) : (i + 1) * (width // 2)]).astype(BF)
        og[:, :, :, :, i] = og_half.reshape((2, 2, 2, 2) + og.shape[-2:])
    O.start()

    key_at = lax.broadcasted_iota(jnp.int32, (half, rows), 0)
    query_at = lax.broadcasted_iota(jnp.int32, (half, rows), 1)
    for part in range(2):
        same = key_col[part * half : (part + 1) * half] == id_row[:, :rows]
        mask[pl.ds(part * half, half), pl.ds(0, rows)] = jnp.where(same | (query_at == key_at + part * half), 0.0, MASKED)
    mask[pl.ds(0, half), halo_rows] = jnp.where(key_col[half:rows] == id_row[:, rows:], 0.0, MASKED)
    mask[near_rows, halo_rows] = jnp.where(key_col[rows:] == id_row[:, half:rows], 0.0, MASKED)

    def own(p, _):
        c = pl.multiple_of(p * PAIR, PAIR)
        col, kcol, vcol = pl.ds(c, PAIR), pl.ds(width + c, PAIR), pl.ds(2 * width + c, PAIR)
        q, k, v = proj[own_rows, col], proj[:, kcol], proj[:, vcol]
        do = d_att[own_rows, col]
        gq = gk = gv = gn = None
        for head in range(2):
            qh, kh, doh = cut(q, head), cut(k, head), cut(do, head)
            ls = lse[pl.ds(2 * p + head, 1), :]
            de = delta[pl.ds(2 * p + head, 1), :]
            prob = jnp.exp(mm_nt(k[:rows], qh) + mask[:, pl.ds(0, rows)] - ls)
            ds = (prob * (mm_nt(v[:rows], doh) - de)).astype(BF)
            a = mm(prob.astype(BF), doh)
            b = mm(ds, qh)
            c = mm_tn(ds, kh[:rows])
            prob = jnp.exp(mm_nt(k[rows:], qh[half:]) + mask[near_rows, halo_rows] - ls[:, half:])
            ds = (prob * (mm_nt(v[rows:], doh[half:]) - de[:, half:])).astype(BF)
            d = mm_tn(ds, kh[rows:])
            gv = a if gv is None else gv + a
            gk = b if gk is None else gk + b
            gq = c if gq is None else gq + c
            gn = d if gn is None else gn + d
        scale = HEAD_DIM ** (-0.5)
        di[pl.ds(0, half), col] = (gq[:half] * scale).astype(BF)
        di[near_rows, col] = ((gq[half:] + gn) * scale).astype(BF)
        di[pl.ds(0, half), kcol] = gk[:half].astype(BF)
        di[pl.ds(0, half), vcol] = gv[:half].astype(BF)
        z[pl.ds(0, half), col] = gk[half:]
        z[near_rows, col] = gv[half:]
        return 0

    def halo(p, _):
        c = pl.multiple_of(p * PAIR, PAIR)
        col, kcol, vcol = pl.ds(c, PAIR), pl.ds(width + c, PAIR), pl.ds(2 * width + c, PAIR)
        q, k, v = proj[halo_rows, col], proj[near_rows, kcol], proj[near_rows, vcol]
        do = d_att[halo_rows, col]
        gk, gv = z[pl.ds(0, half), col], z[near_rows, col]
        for head in range(2):
            qh, doh = cut(q, head), cut(do, head)
            ls = stat[0, pl.ds(2 * p + head, 1), :]
            de = stat[1, pl.ds(2 * p + head, 1), :]
            prob = jnp.exp(mm_nt(k, qh) + mask[pl.ds(0, half), halo_rows] - ls)
            ds = (prob * (mm_nt(v, doh) - de)).astype(BF)
            gv = gv + mm(prob.astype(BF), doh)
            gk = gk + mm(ds, qh)
        di[near_rows, kcol] = gk.astype(BF)
        di[near_rows, vcol] = gv.astype(BF)
        return 0

    n2t[...] = jnp.transpose(xn[own_rows, :])
    project(rows, half, (0,))
    lax.fori_loop(0, 2, own, 0, unroll=2)
    early.step()
    O.step()
    lax.fori_loop(0, chunks, settle, 0)
    for s in (B, C, A, D):
        s.start()
    lax.fori_loop(2, heads // 2, own, 0, unroll=2)
    early.step()
    for h in halos:
        h.wait()
    lax.fori_loop(0, heads // 2, halo, 0, unroll=3)
    third = width // 2

    def weigh(j):
        g = mm(n2t[...], di[:, pl.ds(j * width, width)]).astype(BF)
        for i in range(2):
            side, part = divmod(2 * j + i, 3)
            qg[part, :, :, :, :, side] = g[:, i * third : (i + 1) * third].reshape((2, 2, 2, 2) + qg.shape[-2:])

    weigh(0)
    weigh(1)
    Q[0].start()
    weigh(2)
    Q[1].start()
    Q[2].start()
    z[...] = mm(act[...], w2[...])
    early.step()
    for s in (B, C, A, D):
        s.step()
    for s in Q:
        s.step()
    O.step()
    da[...] = mm_nt(di[:, pl.ds(0, 3 * width)], wqkv[...])

    def back(i, _):
        rs = pl.ds(pl.multiple_of(i * rb, rb), rb)
        xs = x[rs, :].astype(F32)
        centred = xs - jnp.mean(xs, axis=-1, keepdims=True)
        r = lax.rsqrt(jnp.mean(centred * centred, axis=-1, keepdims=True) + 1e-06)
        xh = centred * r
        g = da[rs, :]
        add_vec(late, 0, g * xh)
        add_vec(late, 1, g)
        gy = g * gain_one
        mean_gy = jnp.mean(gy, axis=-1, keepdims=True)
        mean_gx = jnp.mean(gy * xh, axis=-1, keepdims=True)
        w1[rs, pl.ds(width, width)] = (xhat[rs, :] + r * (gy - mean_gy - xh * mean_gx)).astype(BF)
        add_vec(late, 2, di[rs, pl.ds(0, width)].astype(F32))
        add_vec(late, 3, di[rs, pl.ds(2 * width, width)].astype(F32))
        branch = z[rs, :] + fc2_bias
        result = hidden[rs, :] + branch
        w1[rs, pl.ds(0, width)] = result.astype(BF)
        kept = rstd[rs, :][:, 0:1]
        add_vec(late, 4, kept * branch * branch)
        add_vec(late, 5, kept * result * result)
        return 0

    lax.fori_loop(0, rows // rb, back, 0)
    later.start()
    copies = [
        fetch(w1.at[pl.ds(0, half), pl.ds(0, width)], out_hbm.at[pl.ds(far, half)], 0),
        fetch(w1.at[near_rows, pl.ds(0, width)], out_hbm.at[pl.ds(near, half)], 1),
        fetch(w1.at[pl.ds(0, half), pl.ds(width, width)], gt_hbm.at[pl.ds(far, half)], 2),
        fetch(w1.at[near_rows, pl.ds(width, width)], gt_hbm.at[pl.ds(near, half)], 3),
    ]

    block, wide = width // 16, w2.shape[0] // 16

    def put_a(_, v):
        z[pl.ds(0, wide), 0:256] = v

    def put_b(_, v):
        z[pl.ds(0, wide), 256:384] = v

    def put_c(i, v):
        z[pl.ds(wide + i[0] * block, block), 0:256] = v

    def put_d(i, v):
        z[pl.ds(wide + i[0] * block, block), 256:768] = v

    def put_o(_, v):
        z[pl.ds(wide + 2 * block, block), 0:384] = v

    early.step()
    later.step()
    for s in (B, C, A, D):
        s.step()
    for _ in range(3):
        for s in Q:
            s.finish()
        later.step()
        for s in Q:
            s.start()
        if O.order:
            O.step()
    early.finish()
    copies.append(fetch(early.ref, vec_hbm, 4))
    for s, put in ((A, put_a), (B, put_b), (C, put_c), (D, put_d)):
        s.last(put)
    O.last(put_o)
    copies += [
        fetch(z.at[pl.ds(0, wide), pl.ds(0, width // 2)], fc2_hbm, 5),
        fetch(z.at[pl.ds(wide, block)], fc1_hbm.at[:, pl.ds(0, width)], 6),
        fetch(z.at[pl.ds(wide + block, block)], fc1_hbm.at[:, pl.ds(width, width)], 7),
        fetch(z.at[pl.ds(wide + 2 * block, block), pl.ds(0, width // 2)], o_hbm, 8),
    ]
    for i in range(3):

        def put_q(_, v, i=i):
            da[pl.ds(i * block, block), 0:384] = v

        Q[i].last(put_q)
        copies.append(fetch(da.at[pl.ds(i * block, block), pl.ds(0, third)], qkv_hbm.at[:, pl.ds(i * third, third)], 10 + i))
    later.finish()
    copies.append(fetch(later.ref, late_hbm, 9))
    for c in copies:
        c.wait()


def call_everything(tokens, seg, keep, g1, bias1, wqkv, qb, vb, ow, ob, g2, bias2, w1, b1, w2, c2, dy):
    rows, width = tokens.shape
    half = rows // 2
    hid = w1.shape[1]
    chunks = hid // width
    block, wide = width // 16, hid // 16
    sds = jax.ShapeDtypeStruct
    V = pltpu.VMEM
    parts = ((2, 2, 2, wide, 256), (2, 2, 2, wide, 128), (2, 2, 2, 2, block, 256), (2, 2, 2, 2, block, 512))
    stages = (
        stage_shapes(*PART_A, wide, 256)
        + stage_shapes(*PART_B, wide, 128)
        + stage_shapes(*PART_C, block, 256)
        + stage_shapes(*PART_D, block, 512)
        + stage_shapes(MATRIX, OUT_ORDER, block, width // 2)
        + [s for order in ORDERS for s in stage_shapes(MATRIX, order, block, width // 2)]
    )
    jobs = 4 + len(stages) + 10
    DMA = pltpu.SemaphoreType.DMA
    return pl.pallas_call(
        everything,
        out_shape=(
            sds((rows, width), BF), sds((rows, width), BF), sds((block, 3 * width // 2), F32), sds((block, width // 2), F32),
            sds((block, hid // 2), F32), sds((wide, width // 2), F32), sds((16, width), F32), sds((8, width), F32),
        ),
        in_specs=[any_spec()] * 17,
        out_specs=(any_spec(),) * 8,
        scratch_shapes=[V(seg.shape, jnp.int32), V(keep.shape, jnp.int32)] + [V((width,), F32)] * 8 + [
            V((hid,), F32),
            V((rows, width), BF), V((rows + half, width), BF), V((width, 3 * width), BF), V((rows + half, 3 * width), BF),
            V((rows, width), BF), V((rows, PAIR), F32), V((16, rows), F32), V((16, rows), F32), V((2, 16, half), F32),
            V((rows, rows + half), F32), V((rows, width), BF), V((width, width), BF), V((width, hid), BF), V((hid, width), BF),
            V((rows, width), F32), V((rows, width), F32), V((rows, PAIR), F32), V((rows, width), BF), V((width, rows), BF),
            V((rows, width), F32), V((rows, width), F32), V((rows, hid), BF), V((rows, hid), BF),
            V((2, 2, 2, 2, block, width), BF), V((2, 2, 2, wide, width // 2), BF),
            V((2, 2, 2, 2, 2, block, width), BF), V((2, 2, 2, 2, wide, width // 2), BF),
        ] + [V(s, BF) for s in parts] + [
            V((rows + half, width), BF), V((3, 2, 2, 2, 2, 2, block, width // 2), BF),
            V((16, width), F32), V((16, width), F32), V((8, width), F32), V((5, 16, width), F32), V((5, 8, width), F32),
        ] + [V(s, BF) for s in stages] + [
            DMA((17 + 2 * chunks,)), DMA((jobs,)), DMA((jobs,)),
            DMA((2, chunks)), DMA((2, chunks)), DMA((4, chunks)), DMA((4, chunks)),
        ],
        compiler_params=pltpu.CompilerParams(collective_id=0, has_side_effects=True, vmem_limit_bytes=67043328),
        name="everything",
    )(tokens, seg, keep, g1, bias1, wqkv, qb, vb, ow, ob, g2, bias2, w1, b1, w2, c2, dy)


def finish(*refs):
    ins, outs, bufs, sems = refs[:8], refs[8:24], refs[24:-1], refs[-1]
    loads = [pltpu.make_async_copy(src, buf, sems.at[i]) for i, (src, buf) in enumerate(zip(ins, bufs[:8]))]
    for c in loads:
        c.start()
    vec, late = bufs[6:8]
    lines = bufs[8:]
    width = lines[0].shape[0]
    out, gt, g1, b1, qkv, qb, vb, o, ob, g2, b2, f1, f1b, f2, f2b, rm = outs
    stores = []

    def store(src, dst):
        c = pltpu.make_async_copy(src, dst, sems.at[8 + len(stores)])
        c.start()
        stores.append(c)

    loads[6].wait()
    loads[7].wait()
    rows = ((g1, late, 0), (b1, late, 1), (qb, late, 2), (vb, late, 3), (ob, vec, 6), (g2, vec, 4), (b2, vec, 5), (f2b, vec, 7))
    for (dst, src, i), line in zip(rows, lines):
        line[...] = src[i, :]
        store(line, dst)
    for i in range(4):
        lines[8][pl.ds(i * width, width)] = vec[8 + i, :]
    store(lines[8], f1b)
    squares = jnp.concatenate([vec[0:2, :], late[4:6, :]], axis=0)
    ratio = jnp.sqrt(jnp.sum(squares, axis=1, keepdims=True) / (vec[12:13, 0:1] * width))
    diagonal = lax.broadcasted_iota(jnp.int32, (4, 128), 0) == lax.broadcasted_iota(jnp.int32, (4, 128), 1)
    lines[9][...] = jnp.sum(jnp.where(diagonal, ratio, 0.0), axis=0, keepdims=True)
    store(lines[9], rm)
    for i, dst in enumerate((out, gt, qkv, o, f1, f2)):
        loads[i].wait()
        store(bufs[i], dst)
    for c in stores:
        c.wait()


def call_finish(out, gt, qkv, o, f1, f2, vec, late, hid):
    width = out.shape[1]
    sds = jax.ShapeDtypeStruct
    line = sds((width,), F32)
    shapes = (
        sds(out.shape, BF), sds(gt.shape, BF), line, line, sds(qkv.shape, F32), line, line, sds(o.shape, F32), line, line, line,
        sds(f1.shape, F32), sds((hid,), F32), sds(f2.shape, F32), line, sds((1, 128), F32),
    )
    args = (out, gt, qkv, o, f1, f2, vec, late)
    return pl.pallas_call(
        finish,
        out_shape=shapes,
        in_specs=[any_spec()] * 8,
        out_specs=(any_spec(),) * 16,
        scratch_shapes=[pltpu.VMEM(v.shape, v.dtype) for v in args] + [pltpu.VMEM((width,), F32)] * 8
        + [pltpu.VMEM((hid,), F32), pltpu.VMEM((1, 128), F32), pltpu.SemaphoreType.DMA((24,))],
        name="finish",
    )(*args)


def layer_norm(values, norm_gain, norm_bias):
    average = jnp.mean(values, axis=-1, keepdims=True)
    centred = values - average
    variance = jnp.mean(centred * centred, axis=-1, keepdims=True)
    return centred * lax.rsqrt(variance + 1e-06) * norm_gain + norm_bias


def exact_gelu(values):
    return jax.nn.gelu(values, approximate=False)


def on_device_general(
    tokens,
    segment_ids,
    keep_mask,
    gain_one,
    bias_one,
    qkv_weight,
    query_bias,
    value_bias,
    out_weight,
    out_bias,
    gain_two,
    bias_two,
    fc1_weight,
    fc1_bias,
    fc2_weight,
    fc2_bias,
    cotangent,
):
    sequences, tile_rows, model_width = tokens.shape
    length = segment_ids.shape[1]
    count_rows = sequences * tile_rows
    head_block = 4 * HEAD_DIM
    score_scale = HEAD_DIM ** (-0.5)
    offset = lax.axis_index("tile") * tile_rows
    query_ids = lax.dynamic_slice_in_dim(segment_ids, offset, tile_rows, 1)
    query_keep = lax.dynamic_slice_in_dim(keep_mask, offset, tile_rows, 1)
    positions = offset + jnp.arange(tile_rows, dtype=jnp.int32)
    key_places = jnp.arange(length, dtype=jnp.int32)
    own_slot = positions[:, None] == key_places[None, :]
    usable = (keep_mask[:, None, :] == 1) | own_slot[None]
    allowed = ((query_ids[:, :, None] == segment_ids[:, None, :]) & usable)[:, None]
    flattened = tokens.reshape(count_rows, model_width).astype(jnp.float32)
    normed = layer_norm(flattened, gain_one, bias_one)
    normed_low = normed.astype(jnp.bfloat16)
    key_bias = jnp.zeros_like(query_bias)
    projected = jnp.dot(
        normed_low, qkv_weight, preferred_element_type=jnp.float32
    ) + jnp.concatenate([query_bias, key_bias, value_bias])
    projected_low = projected.astype(jnp.bfloat16).reshape(sequences, tile_rows, 3 * model_width)
    queries = projected_low[..., :model_width]
    shared_local = projected_low[..., model_width:]
    shared_all = lax.all_gather(shared_local, "tile", axis=1, tiled=True)
    keys_all = shared_all[..., :model_width]
    values_all = shared_all[..., model_width:]
    key_count = shared_all.shape[1]

    def split_heads(source, column):
        sliced = source[..., column : column + head_block]
        return sliced.reshape(sliced.shape[0], sliced.shape[1], 4, HEAD_DIM)

    def block_scores(query_part, key_part):
        scores = (
            jnp.einsum("sqhe,skhe->shqk", query_part, key_part, preferred_element_type=jnp.float32)
            * score_scale
        )
        return jnp.where(allowed, scores, -1e30)

    attended_parts = []
    logsums = []
    for column in range(0, model_width, head_block):
        masked = block_scores(split_heads(queries, column), split_heads(keys_all, column))
        row_peak = jnp.max(masked, axis=-1, keepdims=True)
        exponent = jnp.exp(masked - row_peak)
        row_total = jnp.sum(exponent, axis=-1, keepdims=True)
        softmax_probs = (exponent / row_total).astype(jnp.bfloat16)
        logsums.append(row_peak + jnp.log(row_total))
        attended_parts.append(
            jnp.einsum(
                "shqk,skhe->sqhe",
                softmax_probs,
                split_heads(values_all, column),
                preferred_element_type=jnp.float32,
            )
        )
    attended = jnp.concatenate(attended_parts, axis=2)
    attended_low = attended.reshape(count_rows, model_width).astype(jnp.bfloat16)
    branch_one = jnp.dot(attended_low, out_weight, preferred_element_type=jnp.float32) + out_bias
    hidden = flattened + branch_one
    normed_two = layer_norm(hidden, gain_two, bias_two)
    normed_two_low = normed_two.astype(jnp.bfloat16)
    inner = jnp.dot(normed_two_low, fc1_weight, preferred_element_type=jnp.float32) + fc1_bias
    active_low = exact_gelu(inner).astype(jnp.bfloat16)
    branch_two = jnp.dot(active_low, fc2_weight, preferred_element_type=jnp.float32) + fc2_bias
    result = hidden + branch_two
    output = result.astype(jnp.bfloat16).reshape(sequences, tile_rows, model_width)
    weighting = query_keep.reshape(count_rows, 1).astype(jnp.float32)
    squares = [
        jnp.sum(weighting * member * member)
        for member in (flattened, branch_one, branch_two, result)
    ]
    stats = jnp.stack(squares + [jnp.sum(weighting)])
    grad_result = cotangent.reshape(count_rows, model_width)
    fc2_grad = jnp.einsum("nf,nd->fd", active_low, grad_result, preferred_element_type=jnp.float32)
    fc2_bias_grad = jnp.sum(grad_result.astype(jnp.float32), axis=0)
    grad_active = jnp.einsum(
        "nd,fd->nf", grad_result, fc2_weight, preferred_element_type=jnp.float32
    )
    inner_value, gelu_back = jax.vjp(exact_gelu, inner)
    grad_inner_low = gelu_back(grad_active)[0].astype(jnp.bfloat16)
    fc1_grad = jnp.einsum(
        "nd,nf->df", normed_two_low, grad_inner_low, preferred_element_type=jnp.float32
    )
    fc1_bias_grad = jnp.sum(grad_inner_low.astype(jnp.float32), axis=0)
    grad_normed_two = jnp.einsum(
        "nf,df->nd", grad_inner_low, fc1_weight, preferred_element_type=jnp.float32
    )
    normed_again, norm_back_two = jax.vjp(layer_norm, hidden, gain_two, bias_two)
    grad_hidden_part, gain_two_grad, bias_two_grad = norm_back_two(grad_normed_two)
    grad_hidden = grad_result.astype(jnp.float32) + grad_hidden_part
    grad_branch_low = grad_hidden.astype(jnp.bfloat16)
    out_grad = jnp.einsum(
        "nd,ne->de", attended_low, grad_branch_low, preferred_element_type=jnp.float32
    )
    out_bias_grad = jnp.sum(grad_branch_low.astype(jnp.float32), axis=0)
    grad_attended_low = (
        jnp.einsum("ne,de->nd", grad_branch_low, out_weight, preferred_element_type=jnp.float32)
        .astype(jnp.bfloat16)
        .reshape(sequences, tile_rows, model_width)
    )
    query_grads = []
    key_grads = []
    value_grads = []
    for block_index, column in enumerate(range(0, model_width, head_block)):
        query_part = split_heads(queries, column)
        key_part = split_heads(keys_all, column)
        value_part = split_heads(values_all, column)
        grad_part = split_heads(grad_attended_low, column)
        masked = block_scores(query_part, key_part)
        probs_again = jnp.exp(masked - logsums[block_index])
        grad_probs = jnp.einsum(
            "sqhe,skhe->shqk", grad_part, value_part, preferred_element_type=jnp.float32
        )
        centre = jnp.sum(probs_again * grad_probs, axis=-1, keepdims=True)
        grad_scores = (probs_again * (grad_probs - centre)).astype(jnp.bfloat16)
        query_grads.append(
            jnp.einsum("shqk,skhe->sqhe", grad_scores, key_part, preferred_element_type=jnp.float32)
            * score_scale
        )
        key_grads.append(
            jnp.einsum(
                "shqk,sqhe->skhe", grad_scores, query_part, preferred_element_type=jnp.float32
            )
            * score_scale
        )
        value_grads.append(
            jnp.einsum(
                "shqk,sqhe->skhe",
                probs_again.astype(jnp.bfloat16),
                grad_part,
                preferred_element_type=jnp.float32,
            )
        )
    grad_query = jnp.concatenate(query_grads, axis=2).reshape(sequences, tile_rows, model_width)
    grad_key_full = jnp.concatenate(key_grads, axis=2).reshape(sequences, key_count, model_width)
    grad_value_full = jnp.concatenate(value_grads, axis=2).reshape(
        sequences, key_count, model_width
    )
    grad_shared_full = jnp.concatenate([grad_key_full, grad_value_full], axis=-1)
    grad_shared = lax.psum_scatter(
        grad_shared_full.astype(jnp.bfloat16), "tile", scatter_dimension=1, tiled=True
    ).astype(jnp.float32)
    grad_projected_low = (
        jnp.concatenate([grad_query, grad_shared], axis=-1)
        .astype(jnp.bfloat16)
        .reshape(count_rows, 3 * model_width)
    )
    qkv_grad = jnp.einsum(
        "nd,ne->de", normed_low, grad_projected_low, preferred_element_type=jnp.float32
    )
    column_sums = jnp.sum(grad_projected_low.astype(jnp.float32), axis=0)
    query_bias_grad = column_sums[:model_width]
    value_bias_grad = column_sums[2 * model_width :]
    grad_normed = jnp.einsum(
        "ne,de->nd", grad_projected_low, qkv_weight, preferred_element_type=jnp.float32
    )
    normed_first, norm_back_one = jax.vjp(layer_norm, flattened, gain_one, bias_one)
    grad_tokens_part, gain_one_grad, bias_one_grad = norm_back_one(grad_normed)
    grad_tokens = (
        (grad_hidden + grad_tokens_part)
        .astype(jnp.bfloat16)
        .reshape(sequences, tile_rows, model_width)
    )
    totals_small = lax.psum(
        (
            gain_one_grad,
            bias_one_grad,
            query_bias_grad,
            value_bias_grad,
            out_bias_grad,
            gain_two_grad,
            bias_two_grad,
            fc1_bias_grad,
            fc2_bias_grad,
            stats,
        ),
        ("dp", "tile"),
    )
    matrices = (qkv_grad, out_grad, fc1_grad, fc2_grad)
    row_shares = (
        lax.psum_scatter(
            matrices[0].astype(jnp.bfloat16), "dp", scatter_dimension=0, tiled=True
        ).astype(jnp.float32),
        lax.psum_scatter(
            matrices[1].astype(jnp.bfloat16), "dp", scatter_dimension=0, tiled=True
        ).astype(jnp.float32),
        lax.psum_scatter(
            matrices[2].astype(jnp.bfloat16), "dp", scatter_dimension=0, tiled=True
        ).astype(jnp.float32),
        lax.psum_scatter(
            matrices[3].astype(jnp.bfloat16), "dp", scatter_dimension=0, tiled=True
        ).astype(jnp.float32),
    )
    reduced = (
        lax.psum_scatter(
            row_shares[0].astype(jnp.bfloat16), "tile", scatter_dimension=1, tiled=True
        ).astype(jnp.float32),
        lax.psum_scatter(
            row_shares[1].astype(jnp.bfloat16), "tile", scatter_dimension=1, tiled=True
        ).astype(jnp.float32),
        lax.psum_scatter(
            row_shares[2].astype(jnp.bfloat16), "tile", scatter_dimension=1, tiled=True
        ).astype(jnp.float32),
        lax.psum_scatter(
            row_shares[3].astype(jnp.bfloat16), "tile", scatter_dimension=1, tiled=True
        ).astype(jnp.float32),
    )
    totals = totals_small[9]
    root_mean = jnp.sqrt(totals[:4] / (totals[4] * model_width))
    return (
        output,
        grad_tokens,
        totals_small[0],
        totals_small[1],
        reduced[0],
        totals_small[2],
        totals_small[3],
        reduced[1],
        totals_small[4],
        totals_small[5],
        totals_small[6],
        reduced[2],
        totals_small[7],
        reduced[3],
        totals_small[8],
        root_mean,
    )


def on_device(tokens, segment_ids, keep_mask, gain_one, bias_one, qkv_weight, query_bias, value_bias, out_weight, out_bias, gain_two, bias_two, fc1_weight, fc1_bias, fc2_weight, fc2_bias, cotangent):
    out, gt, qg, og, f1, f2, vec, late = call_everything(
        tokens[0], segment_ids, keep_mask, gain_one, bias_one, qkv_weight, query_bias, value_bias, out_weight, out_bias,
        gain_two, bias_two, fc1_weight, fc1_bias, fc2_weight, fc2_bias, cotangent[0],
    )
    r = list(call_finish(out, gt, qg, og, f1, f2, vec, late, fc1_weight.shape[1]))
    r[0] = r[0][None]
    r[1] = r[1][None]
    r[15] = r[15][0, :4]
    return tuple(r)


def fits(mesh):
    return mesh.shape["tile"] == 2 and mesh.shape["dp"] == 16


def solution(mesh):
    S, D, T = P("dp", "tile", None), P("dp", None), P("dp", "tile")
    return jax.shard_map(
        on_device if fits(mesh) else on_device_general,
        mesh=mesh,
        in_specs=(S, D, D) + (P(),) * 13 + (S,),
        out_specs=(S, S, P(), P(), T, P(), P(), T, P(), P(), P(), T, P(), T, P(), P()),
        check_vma=False,
    )
```

```python
import itertools

import jax
import jax.numpy as jnp
from jax import lax
from jax.experimental import pallas as pl
from jax.experimental.pallas import tpu as pltpu
from jax.sharding import PartitionSpec as P

HEAD_DIM = 64
PAIR = 2 * HEAD_DIM
MASKED = -1e30
MESH = pl.DeviceIdType.MESH
BF = jnp.bfloat16
F32 = jnp.float32
NT = (((1,), (1,)), ((), ()))
TN = (((0,), (0,)), ((), ()))


def mm(a, b):
    return jnp.dot(a, b, preferred_element_type=F32)


def mm_nt(a, b):
    return lax.dot_general(a, b, NT, preferred_element_type=F32)


def mm_tn(a, b):
    return lax.dot_general(a, b, TN, preferred_element_type=F32)


def any_spec():
    return pl.BlockSpec(memory_space=pl.ANY)


def vmem_spec():
    return pl.BlockSpec(memory_space=pltpu.VMEM)


def gelu_and_slope(z):
    bell = jnp.exp(z * z * -0.5)
    t = 1.0 / (1.0 + jnp.abs(z) * (0.3275911 * 0.7071067811865476))
    tail = t * (0.127414796 + t * (-0.142248368 + t * (0.7107068705 + t * (-0.7265760135 + t * 0.5307027145)))) * bell
    upper = jnp.where(z >= 0, 1.0 - tail, tail)
    return z * upper, upper + z * bell * 0.3989422804014327


def place():
    d = lax.axis_index("dp")
    return dict(core=d % 2, y=d // 2 % 2, z0=d // 4 % 2, z1=d // 8, x=lax.axis_index("tile"))


def peer(at, bit):
    if bit == "x":
        return {"tile": 1 - at["x"]}
    step = dict(core=1, y=2, z0=4, z1=8)[bit]
    return {"dp": lax.axis_index("dp") + step - 2 * step * at[bit]}


def send(at, bit, src, dst, send_sem, recv_sem):
    c = pltpu.make_async_remote_copy(src, dst, send_sem, recv_sem, device_id=peer(at, bit), device_id_type=MESH)
    c.start()
    return c


class Share:
    def __init__(self, at, ref, dims, order, buffers, send_sems, recv_sems, first):
        self.at, self.ref, self.dims, self.buffers = at, ref, dims, list(buffers)
        self.order, self.sems, self.next = list(order), (send_sems, recv_sems), first

    def start(self):
        bit = self.order.pop(0)
        self.axis = self.dims.index(bit)
        self.mine = self.at[bit]
        lead = (slice(None),) * self.axis
        self.other = self.buffers.pop(0)
        i, self.next = self.next, self.next + 1
        self.copy = send(self.at, bit, self.ref.at[lead + (1 - self.mine,)], self.other, self.sems[0].at[i], self.sems[1].at[i])

    def kept(self, index):
        return self.ref[index[: self.axis] + (self.mine,) + index[self.axis :]]

    def finish(self):
        self.copy.wait()
        for index in itertools.product(*map(range, self.other.shape[:-2])):
            self.other[index] = self.other[index] + self.kept(index)
        self.ref = self.other
        self.dims = self.dims[: self.axis] + self.dims[self.axis + 1 :]

    def step(self):
        self.finish()
        self.start()

    def last(self, put):
        self.copy.wait()
        for index in itertools.product(*map(range, self.other.shape[:-2])):
            put(index, self.other[index].astype(F32) + self.kept(index).astype(F32))


class Total:
    def __init__(self, at, ref, buffers, send_sems, recv_sems, first):
        self.at, self.ref, self.buffers = at, ref, buffers
        self.sems, self.next, self.stage = (send_sems, recv_sems), first, 0

    def start(self):
        i = self.next + self.stage
        self.copy = send(self.at, BITS[self.stage], self.ref, self.buffers.at[self.stage], self.sems[0].at[i], self.sems[1].at[i])

    def finish(self):
        self.copy.wait()
        got = self.buffers.at[self.stage]
        got[...] = self.ref[...] + got[...]
        self.ref, self.stage = got, self.stage + 1

    def step(self):
        self.finish()
        self.start()


BITS = ("core", "z1", "y", "z0", "x")
PART_A = (("z1", "z0", "y"), ("z0", "y", "z1"))
PART_B = (("z1", "z0", "x"), ("x", "z0", "z1"))
PART_C = (("x", "j", "z1", "z0"), ("z0", "x", "z1"))
PART_D = (("x", "j", "z1", "y"), ("y", "x", "z1"))
MATRIX = ("z1", "z0", "y", "core", "x")
ORDERS = (("core", "x", "y", "z0", "z1"), ("core", "y", "z0", "x", "z1"), ("core", "z0", "x", "y", "z1"))
OUT_ORDER = ("core", "x", "y", "z0", "z1")


def stage_shapes(dims, order, rows, cols):
    left, shapes = list(dims), []
    for bit in order:
        left.remove(bit)
        shapes.append((2,) * len(left) + (rows, cols))
    return shapes


def everything(
    tok, seg_hbm, keep_hbm, g1_hbm, bias1_hbm, wqkv_hbm, qb_hbm, vb_hbm, ow_hbm, ob_hbm, g2_hbm, bias2_hbm, w1_hbm, b1_hbm, w2_hbm, c2_hbm, dy_hbm,
    out_hbm, gt_hbm, qkv_hbm, o_hbm, fc1_hbm, fc2_hbm, vec_hbm, late_hbm,
    seg, keep, g1, bias1, ob, g2, bias2, c2, qb, vb, b1,
    x, xn, wqkv, proj, att, scale_two, lse, delta, stat, mask, dy, ow, w1, w2, hidden, xhat, rstd, n2, n2t, z, da, act, di,
    f1, f2, r1, r2, pa, pb, pc, pd, d_att, qg, biases, vec, late, early_buf, late_buf, *rest,
):
    rows, width = x.shape
    half = rows // 2
    heads = width // HEAD_DIM
    cols = width
    chunks = w2.shape[0] // cols
    stage_bufs = list(rest[:-7])
    sems, send_sems, recv_sems, core_send, core_recv, next_send, next_recv = rest[-7:]
    at = place()
    t = at["x"]
    far, near = t * half, (1 - t) * half
    own_rows, halo_rows, near_rows = pl.ds(0, rows), pl.ds(rows, half), pl.ds(half, half)
    barrier = pltpu.get_barrier_semaphore()
    for bit in BITS:
        pl.semaphore_signal(barrier, inc=1, device_id=peer(at, bit), device_id_type=MESH)

    def fetch(src, dst, i):
        c = pltpu.make_async_copy(src, dst, sems.at[i])
        c.start()
        return c

    small = ((seg_hbm, seg), (keep_hbm, keep), (g1_hbm, g1), (bias1_hbm, bias1), (ob_hbm, ob), (g2_hbm, g2), (bias2_hbm, bias2), (c2_hbm, c2), (qb_hbm, qb), (vb_hbm, vb), (b1_hbm, b1))
    got_small = [fetch(src, dst, 6 + 2 * chunks + i) for i, (src, dst) in enumerate(small)]
    got_x = [fetch(tok.at[pl.ds(far, half)], x.at[pl.ds(0, half)], 0), fetch(tok.at[pl.ds(near, half)], x.at[near_rows], 1)]
    got_wqkv = fetch(wqkv_hbm, wqkv, 2)
    pl.semaphore_wait(barrier, len(BITS))
    used = [0]

    def job(bit, src, dst):
        i, used[0] = used[0], used[0] + 1
        return send(at, bit, src, dst, send_sems.at[i], recv_sems.at[i])

    token_halo = job("x", tok.at[pl.ds(near, half)], xn.at[halo_rows])

    for g in got_small:
        g.wait()
    starts = (t * (rows + half), t * rows + (1 - t) * half, (1 - t) * rows + t * half)
    slots = [pl.ds(pl.multiple_of(s, 128), half) for s in starts]
    ids = jnp.concatenate([seg[:, s] for s in slots], axis=1)
    kept_row = jnp.concatenate([keep[:, s] for s in slots], axis=1)
    key_row = jnp.where(kept_row == 1, ids, -1)
    table = jnp.concatenate([ids, key_row, kept_row, jnp.zeros((5, rows + half), jnp.int32)], axis=0)
    columns = jnp.transpose(table.astype(F32))
    id_col, key_col, kept_col = columns[:, 0:1], columns[:, 1:2], columns[:, 2:3]
    id_row, key_row = ids.astype(F32), key_row.astype(F32)
    query_at = lax.broadcasted_iota(jnp.int32, (half, rows + half), 0)
    key_at = lax.broadcasted_iota(jnp.int32, (half, rows + half), 1)
    for part in range(2):
        same = id_col[part * half : (part + 1) * half] == key_row
        mask[pl.ds(part * half, half), :] = jnp.where(same | (query_at + part * half == key_at), 0.0, MASKED)
    rstd[...] = jnp.broadcast_to(kept_col[:rows], rstd.shape)
    for i in range(chunks):
        biases[i : i + 1, :] = b1[i * cols : (i + 1) * cols].reshape(1, cols)
    for i, ref in enumerate((g1, bias1, ob, g2, bias2, c2, qb, vb)):
        biases[8 + i : 9 + i, :] = ref[...].reshape(1, width)
    gain_one, bias_one, out_bias, gain_two, bias_two, fc2_bias = (biases[8 + i : 9 + i, :] for i in range(6))
    vec[...] = jnp.zeros_like(vec)
    late[...] = jnp.zeros_like(late)
    vec[12:13, 0:128] = jnp.sum(rstd[...], axis=0, keepdims=True)
    rb = 128

    def normalize(src, dst, start, count):
        def one(i, _):
            rs = pl.ds(pl.multiple_of(start + i * rb, rb), rb)
            v = src[rs, :].astype(F32)
            centred = v - jnp.mean(v, axis=-1, keepdims=True)
            var = jnp.mean(centred * centred, axis=-1, keepdims=True)
            dst[rs, :] = (centred * lax.rsqrt(var + 1e-06) * gain_one + bias_one).astype(BF)
            return 0

        lax.fori_loop(0, count // rb, one, 0, unroll=2)

    def project(start, count, which):
        rs = pl.ds(start, count)
        for j in which:
            js = pl.ds(j * width, width)
            v = mm(xn[rs, :], wqkv[:, js])
            if j == 0:
                proj[rs, js] = (v + biases[14:15, :]).astype(BF) * BF(HEAD_DIM ** (-0.5))
            elif j == 1:
                proj[rs, js] = v.astype(BF)
            else:
                proj[rs, js] = (v + biases[15:16, :]).astype(BF)

    lane = lax.broadcasted_iota(jnp.int32, (1, PAIR), 1)

    def cut(v, head):
        return jnp.where((lane < HEAD_DIM) == (head == 0), v, 0).astype(BF)

    def both(a, b):
        return jnp.where(lane < HEAD_DIM, a, b)

    def scores(p, query_rows, mask_rows, key_start, keys):
        c = pl.multiple_of(p * PAIR, PAIR)
        ks = pl.ds(key_start, keys)
        q, k, v = proj[query_rows, pl.ds(c, PAIR)], proj[ks, pl.ds(width + c, PAIR)], proj[ks, pl.ds(2 * width + c, PAIR)]
        total, new_tops = None, []
        for head in range(2):
            s = mm_nt(cut(q, head), k) + mask[mask_rows, ks]
            top = jnp.max(s, axis=-1, keepdims=True)
            e = jnp.exp(s - top).astype(BF)
            ones = jnp.broadcast_to(cut(jnp.ones((1, PAIR), BF), head), (keys, PAIR))
            part = mm(e, jnp.concatenate([cut(v, head), ones], axis=1))
            total = part if total is None else total + part
            new_tops.append(top)
        return total[:, :PAIR], total[:, PAIR:], both(new_tops[0], new_tops[1])

    def attended(p, rs, value, sums, tops):
        c = pl.ds(pl.multiple_of(p * PAIR, PAIR), PAIR)
        att[rs, c] = (value / sums).astype(BF)
        hidden[rs, c] = tops + jnp.log(sums)

    def attend_far(p, _):
        rs = pl.ds(0, half)
        attended(p, rs, *scores(p, rs, rs, 0, rows))
        return 0

    def attend_near(p, _):
        c = pl.ds(pl.multiple_of(p * PAIR, PAIR), PAIR)
        z[pl.ds(0, half), c], z[near_rows, c], da[near_rows, c] = scores(p, near_rows, near_rows, 0, rows)
        return 0

    def attend_halo(p, _):
        c = pl.ds(pl.multiple_of(p * PAIR, PAIR), PAIR)
        before = da[near_rows, c]
        value, sums, after = scores(p, near_rows, near_rows, rows, half)
        tops = jnp.maximum(before, after)
        old, new = jnp.exp(before - tops), jnp.exp(after - tops)
        attended(p, near_rows, value * new + z[pl.ds(0, half), c] * old, sums * new + z[near_rows, c] * old, tops)
        return 0

    for g in got_x:
        g.wait()
    normalize(x, xn, 0, rows)
    got_wqkv.wait()
    got_dy = [fetch(dy_hbm.at[pl.ds(far, half)], dy.at[pl.ds(0, half)], 3), fetch(dy_hbm.at[pl.ds(near, half)], dy.at[near_rows], 4)]
    got_ow = fetch(ow_hbm, ow, 5)
    got_w = []
    for c in range(chunks):
        got_w.append(fetch(w1_hbm.at[:, pl.ds(c * cols, cols)], w1.at[:, pl.ds(c * cols, cols)], 6 + 2 * c))
        got_w.append(fetch(w2_hbm.at[pl.ds(c * cols, cols)], w2.at[pl.ds(c * cols, cols)], 7 + 2 * c))
    project(0, rows, (0, 1, 2))
    lax.fori_loop(0, heads // 2, attend_far, 0, unroll=3)
    lax.fori_loop(0, heads // 2, attend_near, 0, unroll=3)
    token_halo.wait()
    normalize(xn, xn, rows, half)
    project(rows, half, (1, 2))
    lax.fori_loop(0, heads // 2, attend_halo, 0, unroll=3)
    head_row = lax.broadcasted_iota(jnp.int32, (16, width), 0) * HEAD_DIM
    lane_at = lax.broadcasted_iota(jnp.int32, (16, width), 1)
    first = jnp.where(lane_at == head_row, 1.0, 0.0).astype(BF)
    logs = hidden[...]
    high = logs.astype(BF)
    mid = (logs - high.astype(F32)).astype(BF)
    low = (logs - high.astype(F32) - mid.astype(F32)).astype(BF)
    lse[...] = mm_nt(first, high) + mm_nt(first, mid) + mm_nt(first, low)
    got_ow.wait()

    def add_vec(ref, i, v):
        ref[i : i + 1, :] += jnp.sum(v, axis=0, keepdims=True)

    def front(i, _):
        rs = pl.ds(pl.multiple_of(i * rb, rb), rb)
        branch = mm(att[rs, :], ow[...]) + out_bias
        xs = x[rs, :].astype(F32)
        h = xs + branch
        hidden[rs, :] = h
        kept = rstd[rs, :][:, 0:1]
        add_vec(vec, 0, kept * xs * xs)
        add_vec(vec, 1, kept * branch * branch)
        centred = h - jnp.mean(h, axis=-1, keepdims=True)
        r = lax.rsqrt(jnp.mean(centred * centred, axis=-1, keepdims=True) + 1e-06)
        xh = centred * r
        xhat[rs, :] = xh
        scale_two[rs, :] = jnp.broadcast_to(r, (rb, PAIR))
        n2[rs, :] = (xh * gain_two + bias_two).astype(BF)
        return 0

    lax.fori_loop(0, rows // rb, front, 0, unroll=2)
    n2t[...] = jnp.transpose(n2[...])
    for g in got_dy:
        g.wait()

    def core_copies(c):
        hi, lo = c // 2, c % 2
        other = 1 - at["core"]
        pairs = ((f1.at[:, :, :, other], r1.at[hi, lo]), (f2.at[:, :, other], r2.at[hi, lo]))
        return [
            pltpu.make_async_remote_copy(s, d, core_send.at[i, c], core_recv.at[i, c], device_id=peer(at, "core"), device_id_type=MESH)
            for i, (s, d) in enumerate(pairs)
        ]

    def next_copies(c):
        hi, lo = c // 2, c % 2
        jobs = (
            ("x", r2.at[hi, lo, 1 - t, :, :, pl.ds(0, 256)], pa.at[hi, lo]),
            ("y", r2.at[hi, lo, :, 1 - at["y"], :, pl.ds(256, 128)], pb.at[hi, lo]),
            ("y", r1.at[hi, lo, :, :, 1 - at["y"], :, pl.ds(0, 256)], pc.at[hi, lo]),
            ("z0", r1.at[hi, lo, :, 1 - at["z0"], :, :, pl.ds(256, 512)], pd.at[hi, lo]),
        )
        return [
            pltpu.make_async_remote_copy(s, d, next_send.at[i, c], next_recv.at[i, c], device_id=peer(at, bit), device_id_type=MESH)
            for i, (bit, s, d) in enumerate(jobs)
        ]

    def pass_on(c):
        hi, lo = c // 2, c % 2
        mine = at["core"]
        for copy in core_copies(c):
            copy.wait()

        def one(i, _):
            a, b, d = i // 4, i // 2 % 2, i % 2
            r1[hi, lo, a, b, d] += f1[a, b, d, mine]
            return 0

        lax.fori_loop(0, 8, one, 0, unroll=2)

        def two(i, _):
            r2[hi, lo, i // 2, i % 2] += f2[i // 2, i % 2, mine]
            return 0

        lax.fori_loop(0, 4, two, 0)
        for copy in next_copies(c):
            copy.start()

    def chunk(c, _):
        for i in range(2):
            pltpu.make_async_copy(w2_hbm.at[pl.ds(0, cols)], w2.at[pl.ds(0, cols)], sems.at[6 + 2 * c + i]).wait()
        here = pl.ds(pl.multiple_of(c * cols, cols), cols)
        z[...] = mm(n2[...], w1[:, here]) + biases[pl.ds(c, 1), :]
        da[...] = mm_nt(dy[...], w2[here, :])
        gr = 64
        bsum = jnp.zeros((1, cols), F32)
        for i in range(rows // gr):
            rs = pl.ds(i * gr, gr)
            a, s = gelu_and_slope(z[rs, :])
            act[rs, here] = a.astype(BF)
            d = (da[rs, :] * s).astype(BF)
            di[rs, here] = d
            bsum = bsum + jnp.sum(d.astype(F32), axis=0, keepdims=True)
        vec[pl.ds(8 + c, 1), :] = bsum

        @pl.when(c > 0)
        def _():
            pass_on(c - 1)

        f1[...] = mm(n2t[...], di[:, here]).astype(BF).reshape(f1.shape)
        g = mm_tn(act[:, here], dy[...]).astype(BF)
        f2[0] = g[:, : width // 2].reshape(f2.shape[1:])
        f2[1] = g[:, width // 2 :].reshape(f2.shape[1:])
        for copy in core_copies(c):
            copy.start()
        return 0

    lax.fori_loop(0, chunks, chunk, 0)
    da[...] = mm_nt(di[...], w1[...])
    pass_on(chunks - 1)

    def middle(i, _):
        rs = pl.ds(pl.multiple_of(i * rb, rb), rb)
        g = da[rs, :]
        xh = xhat[rs, :]
        add_vec(vec, 4, g * xh)
        add_vec(vec, 5, g)
        gy = g * gain_two
        mean_gy = jnp.mean(gy, axis=-1, keepdims=True)
        mean_gx = jnp.mean(gy * xh, axis=-1, keepdims=True)
        dys = dy[rs, :].astype(F32)
        add_vec(vec, 7, dys)
        dh = dys + scale_two[rs, :][:, 0:1] * (gy - mean_gy - xh * mean_gx)
        xhat[rs, :] = dh
        low = dh.astype(BF)
        n2[rs, :] = low
        add_vec(vec, 6, low.astype(F32))
        return 0

    lax.fori_loop(0, rows // rb, middle, 0)
    d_att[own_rows, :] = mm_nt(n2[...], ow[...]).astype(BF)
    mine = jnp.where((lane_at >= head_row) & (lane_at < head_row + HEAD_DIM), 1.0, 0.0).astype(BF)
    prod = d_att[own_rows, :].astype(F32) * att[...].astype(F32)
    hi = prod.astype(BF)
    lo = (prod - hi.astype(F32)).astype(BF)
    delta[...] = mm_nt(mine, hi) + mm_nt(mine, lo)
    halos = [
        job("x", d_att.at[near_rows], d_att.at[halo_rows]),
        job("x", lse.at[:, near_rows], stat.at[0]),
        job("x", delta.at[:, near_rows], stat.at[1]),
    ]

    def share(ref, dims, order):
        bufs = [stage_bufs.pop(0) for _ in order]
        first, used[0] = used[0], used[0] + len(order)
        return Share(at, ref, dims, order, bufs, send_sems, recv_sems, first)

    og = qg.at[2]
    A, B, C, D = (share(ref, *part) for ref, part in ((pa, PART_A), (pb, PART_B), (pc, PART_C), (pd, PART_D)))
    O = share(og, MATRIX, OUT_ORDER)
    Q = [share(qg.at[i], MATRIX, ORDERS[i]) for i in range(3)]
    early = Total(at, vec, early_buf, send_sems, recv_sems, used[0])
    later = Total(at, late, late_buf, send_sems, recv_sems, used[0] + 5)
    early.start()
    def settle(c, _):
        hi, lo = c // 2, c % 2
        for copy in next_copies(c):
            copy.wait()
        for i in range(2):
            pa[hi, lo, i] += r2[hi, lo, t, i, :, 0:256]
            pb[hi, lo, i] += r2[hi, lo, i, at["y"], :, 256:384]
            for j in range(2):
                pc[hi, lo, i, j] += r1[hi, lo, i, j, at["y"], :, 0:256]
                pd[hi, lo, i, j] += r1[hi, lo, i, at["z0"], j, :, 256:768]
        return 0

    n2t[...] = jnp.transpose(att[...])
    for i in range(2):
        og_half = mm(n2t[...], n2[:, i * (width // 2) : (i + 1) * (width // 2)]).astype(BF)
        og[:, :, :, :, i] = og_half.reshape((2, 2, 2, 2) + og.shape[-2:])
    O.start()

    key_at = lax.broadcasted_iota(jnp.int32, (half, rows), 0)
    query_at = lax.broadcasted_iota(jnp.int32, (half, rows), 1)
    for part in range(2):
        same = key_col[part * half : (part + 1) * half] == id_row[:, :rows]
        mask[pl.ds(part * half, half), pl.ds(0, rows)] = jnp.where(same | (query_at == key_at + part * half), 0.0, MASKED)
    mask[pl.ds(0, half), halo_rows] = jnp.where(key_col[half:rows] == id_row[:, rows:], 0.0, MASKED)
    mask[near_rows, halo_rows] = jnp.where(key_col[rows:] == id_row[:, half:rows], 0.0, MASKED)

    def own(p, _):
        c = pl.multiple_of(p * PAIR, PAIR)
        col, kcol, vcol = pl.ds(c, PAIR), pl.ds(width + c, PAIR), pl.ds(2 * width + c, PAIR)
        q, k, v = proj[own_rows, col], proj[:, kcol], proj[:, vcol]
        do = d_att[own_rows, col]
        gq = gk = gv = gn = None
        for head in range(2):
            qh, kh, doh = cut(q, head), cut(k, head), cut(do, head)
            ls = lse[pl.ds(2 * p + head, 1), :]
            de = delta[pl.ds(2 * p + head, 1), :]
            prob = jnp.exp(mm_nt(k[:rows], qh) + mask[:, pl.ds(0, rows)] - ls)
            ds = (prob * (mm_nt(v[:rows], doh) - de)).astype(BF)
            a = mm(prob.astype(BF), doh)
            b = mm(ds, qh)
            c = mm_tn(ds, kh[:rows])
            prob = jnp.exp(mm_nt(k[rows:], qh[half:]) + mask[near_rows, halo_rows] - ls[:, half:])
            ds = (prob * (mm_nt(v[rows:], doh[half:]) - de[:, half:])).astype(BF)
            d = mm_tn(ds, kh[rows:])
            gv = a if gv is None else gv + a
            gk = b if gk is None else gk + b
            gq = c if gq is None else gq + c
            gn = d if gn is None else gn + d
        scale = HEAD_DIM ** (-0.5)
        di[pl.ds(0, half), col] = (gq[:half] * scale).astype(BF)
        di[near_rows, col] = ((gq[half:] + gn) * scale).astype(BF)
        di[pl.ds(0, half), kcol] = gk[:half].astype(BF)
        di[pl.ds(0, half), vcol] = gv[:half].astype(BF)
        z[pl.ds(0, half), col] = gk[half:]
        z[near_rows, col] = gv[half:]
        return 0

    def halo(p, _):
        c = pl.multiple_of(p * PAIR, PAIR)
        col, kcol, vcol = pl.ds(c, PAIR), pl.ds(width + c, PAIR), pl.ds(2 * width + c, PAIR)
        q, k, v = proj[halo_rows, col], proj[near_rows, kcol], proj[near_rows, vcol]
        do = d_att[halo_rows, col]
        gk, gv = z[pl.ds(0, half), col], z[near_rows, col]
        for head in range(2):
            qh, doh = cut(q, head), cut(do, head)
            ls = stat[0, pl.ds(2 * p + head, 1), :]
            de = stat[1, pl.ds(2 * p + head, 1), :]
            prob = jnp.exp(mm_nt(k, qh) + mask[pl.ds(0, half), halo_rows] - ls)
            ds = (prob * (mm_nt(v, doh) - de)).astype(BF)
            gv = gv + mm(prob.astype(BF), doh)
            gk = gk + mm(ds, qh)
        di[near_rows, kcol] = gk.astype(BF)
        di[near_rows, vcol] = gv.astype(BF)
        return 0

    n2t[...] = jnp.transpose(xn[own_rows, :])
    project(rows, half, (0,))
    lax.fori_loop(0, 2, own, 0, unroll=2)
    early.step()
    O.step()
    lax.fori_loop(0, chunks, settle, 0)
    for s in (B, C, A, D):
        s.start()
    lax.fori_loop(2, heads // 2, own, 0, unroll=2)
    early.step()
    for h in halos:
        h.wait()
    lax.fori_loop(0, heads // 2, halo, 0, unroll=3)
    third = width // 2

    def weigh(j):
        g = mm(n2t[...], di[:, pl.ds(j * width, width)]).astype(BF)
        for i in range(2):
            side, part = divmod(2 * j + i, 3)
            qg[part, :, :, :, :, side] = g[:, i * third : (i + 1) * third].reshape((2, 2, 2, 2) + qg.shape[-2:])

    weigh(0)
    weigh(1)
    Q[0].start()
    weigh(2)
    Q[1].start()
    Q[2].start()
    z[...] = mm(act[...], w2[...])
    early.step()
    for s in (B, C, A, D):
        s.step()
    for s in Q:
        s.step()
    O.step()
    da[...] = mm_nt(di[:, pl.ds(0, 3 * width)], wqkv[...])

    def back(i, _):
        rs = pl.ds(pl.multiple_of(i * rb, rb), rb)
        xs = x[rs, :].astype(F32)
        centred = xs - jnp.mean(xs, axis=-1, keepdims=True)
        r = lax.rsqrt(jnp.mean(centred * centred, axis=-1, keepdims=True) + 1e-06)
        xh = centred * r
        g = da[rs, :]
        add_vec(late, 0, g * xh)
        add_vec(late, 1, g)
        gy = g * gain_one
        mean_gy = jnp.mean(gy, axis=-1, keepdims=True)
        mean_gx = jnp.mean(gy * xh, axis=-1, keepdims=True)
        w1[rs, pl.ds(width, width)] = (xhat[rs, :] + r * (gy - mean_gy - xh * mean_gx)).astype(BF)
        add_vec(late, 2, di[rs, pl.ds(0, width)].astype(F32))
        add_vec(late, 3, di[rs, pl.ds(2 * width, width)].astype(F32))
        branch = z[rs, :] + fc2_bias
        result = hidden[rs, :] + branch
        w1[rs, pl.ds(0, width)] = result.astype(BF)
        kept = rstd[rs, :][:, 0:1]
        add_vec(late, 4, kept * branch * branch)
        add_vec(late, 5, kept * result * result)
        return 0

    lax.fori_loop(0, rows // rb, back, 0)
    later.start()
    copies = [
        fetch(w1.at[pl.ds(0, half), pl.ds(0, width)], out_hbm.at[pl.ds(far, half)], 0),
        fetch(w1.at[near_rows, pl.ds(0, width)], out_hbm.at[pl.ds(near, half)], 1),
        fetch(w1.at[pl.ds(0, half), pl.ds(width, width)], gt_hbm.at[pl.ds(far, half)], 2),
        fetch(w1.at[near_rows, pl.ds(width, width)], gt_hbm.at[pl.ds(near, half)], 3),
    ]

    block, wide = width // 16, w2.shape[0] // 16

    def put_a(_, v):
        z[pl.ds(0, wide), 0:256] = v

    def put_b(_, v):
        z[pl.ds(0, wide), 256:384] = v

    def put_c(i, v):
        z[pl.ds(wide + i[0] * block, block), 0:256] = v

    def put_d(i, v):
        z[pl.ds(wide + i[0] * block, block), 256:768] = v

    def put_o(_, v):
        z[pl.ds(wide + 2 * block, block), 0:384] = v

    early.step()
    later.step()
    for s in (B, C, A, D):
        s.step()
    for _ in range(3):
        for s in Q:
            s.finish()
        later.step()
        for s in Q:
            s.start()
        if O.order:
            O.step()
    early.finish()
    copies.append(fetch(early.ref, vec_hbm, 4))
    for s, put in ((A, put_a), (B, put_b), (C, put_c), (D, put_d)):
        s.last(put)
    O.last(put_o)
    copies += [
        fetch(z.at[pl.ds(0, wide), pl.ds(0, width // 2)], fc2_hbm, 5),
        fetch(z.at[pl.ds(wide, block)], fc1_hbm.at[:, pl.ds(0, width)], 6),
        fetch(z.at[pl.ds(wide + block, block)], fc1_hbm.at[:, pl.ds(width, width)], 7),
        fetch(z.at[pl.ds(wide + 2 * block, block), pl.ds(0, width // 2)], o_hbm, 8),
    ]
    for i in range(3):

        def put_q(_, v, i=i):
            da[pl.ds(i * block, block), 0:384] = v

        Q[i].last(put_q)
        copies.append(fetch(da.at[pl.ds(i * block, block), pl.ds(0, third)], qkv_hbm.at[:, pl.ds(i * third, third)], 10 + i))
    later.finish()
    copies.append(fetch(later.ref, late_hbm, 9))
    for c in copies:
        c.wait()


def call_everything(tokens, seg, keep, g1, bias1, wqkv, qb, vb, ow, ob, g2, bias2, w1, b1, w2, c2, dy):
    rows, width = tokens.shape
    half = rows // 2
    hid = w1.shape[1]
    chunks = hid // width
    block, wide = width // 16, hid // 16
    sds = jax.ShapeDtypeStruct
    V = pltpu.VMEM
    parts = ((2, 2, 2, wide, 256), (2, 2, 2, wide, 128), (2, 2, 2, 2, block, 256), (2, 2, 2, 2, block, 512))
    stages = (
        stage_shapes(*PART_A, wide, 256)
        + stage_shapes(*PART_B, wide, 128)
        + stage_shapes(*PART_C, block, 256)
        + stage_shapes(*PART_D, block, 512)
        + stage_shapes(MATRIX, OUT_ORDER, block, width // 2)
        + [s for order in ORDERS for s in stage_shapes(MATRIX, order, block, width // 2)]
    )
    jobs = 4 + len(stages) + 10
    DMA = pltpu.SemaphoreType.DMA
    return pl.pallas_call(
        everything,
        out_shape=(
            sds((rows, width), BF), sds((rows, width), BF), sds((block, 3 * width // 2), F32), sds((block, width // 2), F32),
            sds((block, hid // 2), F32), sds((wide, width // 2), F32), sds((16, width), F32), sds((8, width), F32),
        ),
        in_specs=[any_spec()] * 17,
        out_specs=(any_spec(),) * 8,
        scratch_shapes=[V(seg.shape, jnp.int32), V(keep.shape, jnp.int32)] + [V((width,), F32)] * 8 + [
            V((hid,), F32),
            V((rows, width), BF), V((rows + half, width), BF), V((width, 3 * width), BF), V((rows + half, 3 * width), BF),
            V((rows, width), BF), V((rows, PAIR), F32), V((16, rows), F32), V((16, rows), F32), V((2, 16, half), F32),
            V((rows, rows + half), F32), V((rows, width), BF), V((width, width), BF), V((width, hid), BF), V((hid, width), BF),
            V((rows, width), F32), V((rows, width), F32), V((rows, PAIR), F32), V((rows, width), BF), V((width, rows), BF),
            V((rows, width), F32), V((rows, width), F32), V((rows, hid), BF), V((rows, hid), BF),
            V((2, 2, 2, 2, block, width), BF), V((2, 2, 2, wide, width // 2), BF),
            V((2, 2, 2, 2, 2, block, width), BF), V((2, 2, 2, 2, wide, width // 2), BF),
        ] + [V(s, BF) for s in parts] + [
            V((rows + half, width), BF), V((3, 2, 2, 2, 2, 2, block, width // 2), BF),
            V((16, width), F32), V((16, width), F32), V((8, width), F32), V((5, 16, width), F32), V((5, 8, width), F32),
        ] + [V(s, BF) for s in stages] + [
            DMA((17 + 2 * chunks,)), DMA((jobs,)), DMA((jobs,)),
            DMA((2, chunks)), DMA((2, chunks)), DMA((4, chunks)), DMA((4, chunks)),
        ],
        compiler_params=pltpu.CompilerParams(collective_id=0, has_side_effects=True, vmem_limit_bytes=67043328),
        name="everything",
    )(tokens, seg, keep, g1, bias1, wqkv, qb, vb, ow, ob, g2, bias2, w1, b1, w2, c2, dy)


def finish(*refs):
    ins, outs, bufs, sems = refs[:8], refs[8:24], refs[24:-1], refs[-1]
    loads = [pltpu.make_async_copy(src, buf, sems.at[i]) for i, (src, buf) in enumerate(zip(ins, bufs[:8]))]
    for c in loads:
        c.start()
    vec, late = bufs[6:8]
    lines = bufs[8:]
    width = lines[0].shape[0]
    out, gt, g1, b1, qkv, qb, vb, o, ob, g2, b2, f1, f1b, f2, f2b, rm = outs
    stores = []

    def store(src, dst):
        c = pltpu.make_async_copy(src, dst, sems.at[8 + len(stores)])
        c.start()
        stores.append(c)

    loads[6].wait()
    loads[7].wait()
    rows = ((g1, late, 0), (b1, late, 1), (qb, late, 2), (vb, late, 3), (ob, vec, 6), (g2, vec, 4), (b2, vec, 5), (f2b, vec, 7))
    for (dst, src, i), line in zip(rows, lines):
        line[...] = src[i, :]
        store(line, dst)
    for i in range(4):
        lines[8][pl.ds(i * width, width)] = vec[8 + i, :]
    store(lines[8], f1b)
    squares = jnp.concatenate([vec[0:2, :], late[4:6, :]], axis=0)
    ratio = jnp.sqrt(jnp.sum(squares, axis=1, keepdims=True) / (vec[12:13, 0:1] * width))
    for i in range(4):
        rm[i] = ratio[i, 0]
    for i, dst in enumerate((out, gt, qkv, o, f1, f2)):
        loads[i].wait()
        store(bufs[i], dst)
    for c in stores:
        c.wait()


def call_finish(out, gt, qkv, o, f1, f2, vec, late, hid):
    width = out.shape[1]
    sds = jax.ShapeDtypeStruct
    line = sds((width,), F32)
    shapes = (
        sds(out.shape, BF), sds(gt.shape, BF), line, line, sds(qkv.shape, F32), line, line, sds(o.shape, F32), line, line, line,
        sds(f1.shape, F32), sds((hid,), F32), sds(f2.shape, F32), line, sds((4,), F32),
    )
    args = (out, gt, qkv, o, f1, f2, vec, late)
    return pl.pallas_call(
        finish,
        out_shape=shapes,
        in_specs=[any_spec()] * 8,
        out_specs=(any_spec(),) * 15 + (pl.BlockSpec(memory_space=pltpu.SMEM),),
        scratch_shapes=[pltpu.VMEM(v.shape, v.dtype) for v in args] + [pltpu.VMEM((width,), F32)] * 8
        + [pltpu.VMEM((hid,), F32), pltpu.SemaphoreType.DMA((24,))],
        name="finish",
    )(*args)


def layer_norm(values, norm_gain, norm_bias):
    average = jnp.mean(values, axis=-1, keepdims=True)
    centred = values - average
    variance = jnp.mean(centred * centred, axis=-1, keepdims=True)
    return centred * lax.rsqrt(variance + 1e-06) * norm_gain + norm_bias


def exact_gelu(values):
    return jax.nn.gelu(values, approximate=False)


def on_device_general(
    tokens,
    segment_ids,
    keep_mask,
    gain_one,
    bias_one,
    qkv_weight,
    query_bias,
    value_bias,
    out_weight,
    out_bias,
    gain_two,
    bias_two,
    fc1_weight,
    fc1_bias,
    fc2_weight,
    fc2_bias,
    cotangent,
):
    sequences, tile_rows, model_width = tokens.shape
    length = segment_ids.shape[1]
    count_rows = sequences * tile_rows
    head_block = 4 * HEAD_DIM
    score_scale = HEAD_DIM ** (-0.5)
    offset = lax.axis_index("tile") * tile_rows
    query_ids = lax.dynamic_slice_in_dim(segment_ids, offset, tile_rows, 1)
    query_keep = lax.dynamic_slice_in_dim(keep_mask, offset, tile_rows, 1)
    positions = offset + jnp.arange(tile_rows, dtype=jnp.int32)
    key_places = jnp.arange(length, dtype=jnp.int32)
    own_slot = positions[:, None] == key_places[None, :]
    usable = (keep_mask[:, None, :] == 1) | own_slot[None]
    allowed = ((query_ids[:, :, None] == segment_ids[:, None, :]) & usable)[:, None]
    flattened = tokens.reshape(count_rows, model_width).astype(jnp.float32)
    normed = layer_norm(flattened, gain_one, bias_one)
    normed_low = normed.astype(jnp.bfloat16)
    key_bias = jnp.zeros_like(query_bias)
    projected = jnp.dot(
        normed_low, qkv_weight, preferred_element_type=jnp.float32
    ) + jnp.concatenate([query_bias, key_bias, value_bias])
    projected_low = projected.astype(jnp.bfloat16).reshape(sequences, tile_rows, 3 * model_width)
    queries = projected_low[..., :model_width]
    shared_local = projected_low[..., model_width:]
    shared_all = lax.all_gather(shared_local, "tile", axis=1, tiled=True)
    keys_all = shared_all[..., :model_width]
    values_all = shared_all[..., model_width:]
    key_count = shared_all.shape[1]

    def split_heads(source, column):
        sliced = source[..., column : column + head_block]
        return sliced.reshape(sliced.shape[0], sliced.shape[1], 4, HEAD_DIM)

    def block_scores(query_part, key_part):
        scores = (
            jnp.einsum("sqhe,skhe->shqk", query_part, key_part, preferred_element_type=jnp.float32)
            * score_scale
        )
        return jnp.where(allowed, scores, -1e30)

    attended_parts = []
    logsums = []
    for column in range(0, model_width, head_block):
        masked = block_scores(split_heads(queries, column), split_heads(keys_all, column))
        row_peak = jnp.max(masked, axis=-1, keepdims=True)
        exponent = jnp.exp(masked - row_peak)
        row_total = jnp.sum(exponent, axis=-1, keepdims=True)
        softmax_probs = (exponent / row_total).astype(jnp.bfloat16)
        logsums.append(row_peak + jnp.log(row_total))
        attended_parts.append(
            jnp.einsum(
                "shqk,skhe->sqhe",
                softmax_probs,
                split_heads(values_all, column),
                preferred_element_type=jnp.float32,
            )
        )
    attended = jnp.concatenate(attended_parts, axis=2)
    attended_low = attended.reshape(count_rows, model_width).astype(jnp.bfloat16)
    branch_one = jnp.dot(attended_low, out_weight, preferred_element_type=jnp.float32) + out_bias
    hidden = flattened + branch_one
    normed_two = layer_norm(hidden, gain_two, bias_two)
    normed_two_low = normed_two.astype(jnp.bfloat16)
    inner = jnp.dot(normed_two_low, fc1_weight, preferred_element_type=jnp.float32) + fc1_bias
    active_low = exact_gelu(inner).astype(jnp.bfloat16)
    branch_two = jnp.dot(active_low, fc2_weight, preferred_element_type=jnp.float32) + fc2_bias
    result = hidden + branch_two
    output = result.astype(jnp.bfloat16).reshape(sequences, tile_rows, model_width)
    weighting = query_keep.reshape(count_rows, 1).astype(jnp.float32)
    squares = [
        jnp.sum(weighting * member * member)
        for member in (flattened, branch_one, branch_two, result)
    ]
    stats = jnp.stack(squares + [jnp.sum(weighting)])
    grad_result = cotangent.reshape(count_rows, model_width)
    fc2_grad = jnp.einsum("nf,nd->fd", active_low, grad_result, preferred_element_type=jnp.float32)
    fc2_bias_grad = jnp.sum(grad_result.astype(jnp.float32), axis=0)
    grad_active = jnp.einsum(
        "nd,fd->nf", grad_result, fc2_weight, preferred_element_type=jnp.float32
    )
    inner_value, gelu_back = jax.vjp(exact_gelu, inner)
    grad_inner_low = gelu_back(grad_active)[0].astype(jnp.bfloat16)
    fc1_grad = jnp.einsum(
        "nd,nf->df", normed_two_low, grad_inner_low, preferred_element_type=jnp.float32
    )
    fc1_bias_grad = jnp.sum(grad_inner_low.astype(jnp.float32), axis=0)
    grad_normed_two = jnp.einsum(
        "nf,df->nd", grad_inner_low, fc1_weight, preferred_element_type=jnp.float32
    )
    normed_again, norm_back_two = jax.vjp(layer_norm, hidden, gain_two, bias_two)
    grad_hidden_part, gain_two_grad, bias_two_grad = norm_back_two(grad_normed_two)
    grad_hidden = grad_result.astype(jnp.float32) + grad_hidden_part
    grad_branch_low = grad_hidden.astype(jnp.bfloat16)
    out_grad = jnp.einsum(
        "nd,ne->de", attended_low, grad_branch_low, preferred_element_type=jnp.float32
    )
    out_bias_grad = jnp.sum(grad_branch_low.astype(jnp.float32), axis=0)
    grad_attended_low = (
        jnp.einsum("ne,de->nd", grad_branch_low, out_weight, preferred_element_type=jnp.float32)
        .astype(jnp.bfloat16)
        .reshape(sequences, tile_rows, model_width)
    )
    query_grads = []
    key_grads = []
    value_grads = []
    for block_index, column in enumerate(range(0, model_width, head_block)):
        query_part = split_heads(queries, column)
        key_part = split_heads(keys_all, column)
        value_part = split_heads(values_all, column)
        grad_part = split_heads(grad_attended_low, column)
        masked = block_scores(query_part, key_part)
        probs_again = jnp.exp(masked - logsums[block_index])
        grad_probs = jnp.einsum(
            "sqhe,skhe->shqk", grad_part, value_part, preferred_element_type=jnp.float32
        )
        centre = jnp.sum(probs_again * grad_probs, axis=-1, keepdims=True)
        grad_scores = (probs_again * (grad_probs - centre)).astype(jnp.bfloat16)
        query_grads.append(
            jnp.einsum("shqk,skhe->sqhe", grad_scores, key_part, preferred_element_type=jnp.float32)
            * score_scale
        )
        key_grads.append(
            jnp.einsum(
                "shqk,sqhe->skhe", grad_scores, query_part, preferred_element_type=jnp.float32
            )
            * score_scale
        )
        value_grads.append(
            jnp.einsum(
                "shqk,sqhe->skhe",
                probs_again.astype(jnp.bfloat16),
                grad_part,
                preferred_element_type=jnp.float32,
            )
        )
    grad_query = jnp.concatenate(query_grads, axis=2).reshape(sequences, tile_rows, model_width)
    grad_key_full = jnp.concatenate(key_grads, axis=2).reshape(sequences, key_count, model_width)
    grad_value_full = jnp.concatenate(value_grads, axis=2).reshape(
        sequences, key_count, model_width
    )
    grad_shared_full = jnp.concatenate([grad_key_full, grad_value_full], axis=-1)
    grad_shared = lax.psum_scatter(
        grad_shared_full.astype(jnp.bfloat16), "tile", scatter_dimension=1, tiled=True
    ).astype(jnp.float32)
    grad_projected_low = (
        jnp.concatenate([grad_query, grad_shared], axis=-1)
        .astype(jnp.bfloat16)
        .reshape(count_rows, 3 * model_width)
    )
    qkv_grad = jnp.einsum(
        "nd,ne->de", normed_low, grad_projected_low, preferred_element_type=jnp.float32
    )
    column_sums = jnp.sum(grad_projected_low.astype(jnp.float32), axis=0)
    query_bias_grad = column_sums[:model_width]
    value_bias_grad = column_sums[2 * model_width :]
    grad_normed = jnp.einsum(
        "ne,de->nd", grad_projected_low, qkv_weight, preferred_element_type=jnp.float32
    )
    normed_first, norm_back_one = jax.vjp(layer_norm, flattened, gain_one, bias_one)
    grad_tokens_part, gain_one_grad, bias_one_grad = norm_back_one(grad_normed)
    grad_tokens = (
        (grad_hidden + grad_tokens_part)
        .astype(jnp.bfloat16)
        .reshape(sequences, tile_rows, model_width)
    )
    totals_small = lax.psum(
        (
            gain_one_grad,
            bias_one_grad,
            query_bias_grad,
            value_bias_grad,
            out_bias_grad,
            gain_two_grad,
            bias_two_grad,
            fc1_bias_grad,
            fc2_bias_grad,
            stats,
        ),
        ("dp", "tile"),
    )
    matrices = (qkv_grad, out_grad, fc1_grad, fc2_grad)
    row_shares = (
        lax.psum_scatter(
            matrices[0].astype(jnp.bfloat16), "dp", scatter_dimension=0, tiled=True
        ).astype(jnp.float32),
        lax.psum_scatter(
            matrices[1].astype(jnp.bfloat16), "dp", scatter_dimension=0, tiled=True
        ).astype(jnp.float32),
        lax.psum_scatter(
            matrices[2].astype(jnp.bfloat16), "dp", scatter_dimension=0, tiled=True
        ).astype(jnp.float32),
        lax.psum_scatter(
            matrices[3].astype(jnp.bfloat16), "dp", scatter_dimension=0, tiled=True
        ).astype(jnp.float32),
    )
    reduced = (
        lax.psum_scatter(
            row_shares[0].astype(jnp.bfloat16), "tile", scatter_dimension=1, tiled=True
        ).astype(jnp.float32),
        lax.psum_scatter(
            row_shares[1].astype(jnp.bfloat16), "tile", scatter_dimension=1, tiled=True
        ).astype(jnp.float32),
        lax.psum_scatter(
            row_shares[2].astype(jnp.bfloat16), "tile", scatter_dimension=1, tiled=True
        ).astype(jnp.float32),
        lax.psum_scatter(
            row_shares[3].astype(jnp.bfloat16), "tile", scatter_dimension=1, tiled=True
        ).astype(jnp.float32),
    )
    totals = totals_small[9]
    root_mean = jnp.sqrt(totals[:4] / (totals[4] * model_width))
    return (
        output,
        grad_tokens,
        totals_small[0],
        totals_small[1],
        reduced[0],
        totals_small[2],
        totals_small[3],
        reduced[1],
        totals_small[4],
        totals_small[5],
        totals_small[6],
        reduced[2],
        totals_small[7],
        reduced[3],
        totals_small[8],
        root_mean,
    )


def on_device(tokens, segment_ids, keep_mask, gain_one, bias_one, qkv_weight, query_bias, value_bias, out_weight, out_bias, gain_two, bias_two, fc1_weight, fc1_bias, fc2_weight, fc2_bias, cotangent):
    out, gt, qg, og, f1, f2, vec, late = call_everything(
        tokens[0], segment_ids, keep_mask, gain_one, bias_one, qkv_weight, query_bias, value_bias, out_weight, out_bias,
        gain_two, bias_two, fc1_weight, fc1_bias, fc2_weight, fc2_bias, cotangent[0],
    )
    r = list(call_finish(out, gt, qg, og, f1, f2, vec, late, fc1_weight.shape[1]))
    r[0] = r[0][None]
    r[1] = r[1][None]
    return tuple(r)


def fits(mesh):
    return mesh.shape["tile"] == 2 and mesh.shape["dp"] == 16


def solution(mesh):
    S, D, T = P("dp", "tile", None), P("dp", None), P("dp", "tile")
    return jax.shard_map(
        on_device if fits(mesh) else on_device_general,
        mesh=mesh,
        in_specs=(S, D, D) + (P(),) * 13 + (S,),
        out_specs=(S, S, P(), P(), T, P(), P(), T, P(), P(), P(), T, P(), T, P(), P()),
        check_vma=False,
    )
```

```python
import itertools

import jax
import jax.numpy as jnp
from jax import lax
from jax.experimental import pallas as pl
from jax.experimental.pallas import tpu as pltpu
from jax.sharding import PartitionSpec as P

HEAD_DIM = 64
PAIR = 2 * HEAD_DIM
MASKED = -1e30
MESH = pl.DeviceIdType.MESH
BF = jnp.bfloat16
F32 = jnp.float32
NT = (((1,), (1,)), ((), ()))
TN = (((0,), (0,)), ((), ()))


def mm(a, b):
    return jnp.dot(a, b, preferred_element_type=F32)


def mm_nt(a, b):
    return lax.dot_general(a, b, NT, preferred_element_type=F32)


def mm_tn(a, b):
    return lax.dot_general(a, b, TN, preferred_element_type=F32)


def any_spec():
    return pl.BlockSpec(memory_space=pl.ANY)


def vmem_spec():
    return pl.BlockSpec(memory_space=pltpu.VMEM)


def gelu_and_slope(z):
    bell = jnp.exp(z * z * -0.5)
    t = 1.0 / (1.0 + jnp.abs(z) * (0.3275911 * 0.7071067811865476))
    tail = t * (0.127414796 + t * (-0.142248368 + t * (0.7107068705 + t * (-0.7265760135 + t * 0.5307027145)))) * bell
    upper = jnp.where(z >= 0, 1.0 - tail, tail)
    return z * upper, upper + z * bell * 0.3989422804014327


def place():
    d = lax.axis_index("dp")
    return dict(core=d % 2, y=d // 2 % 2, z0=d // 4 % 2, z1=d // 8, x=lax.axis_index("tile"))


def peer(at, bit):
    if bit == "x":
        return {"tile": 1 - at["x"]}
    step = dict(core=1, y=2, z0=4, z1=8)[bit]
    return {"dp": lax.axis_index("dp") + step - 2 * step * at[bit]}


def send(at, bit, src, dst, send_sem, recv_sem):
    c = pltpu.make_async_remote_copy(src, dst, send_sem, recv_sem, device_id=peer(at, bit), device_id_type=MESH)
    c.start()
    return c


class Share:
    def __init__(self, at, ref, dims, order, buffers, send_sems, recv_sems, first):
        self.at, self.ref, self.dims, self.buffers = at, ref, dims, list(buffers)
        self.order, self.sems, self.next = list(order), (send_sems, recv_sems), first

    def start(self):
        bit = self.order.pop(0)
        self.axis = self.dims.index(bit)
        self.mine = self.at[bit]
        lead = (slice(None),) * self.axis
        self.other = self.buffers.pop(0)
        i, self.next = self.next, self.next + 1
        self.copy = send(self.at, bit, self.ref.at[lead + (1 - self.mine,)], self.other, self.sems[0].at[i], self.sems[1].at[i])

    def kept(self, index):
        return self.ref[index[: self.axis] + (self.mine,) + index[self.axis :]]

    def finish(self):
        self.copy.wait()
        for index in itertools.product(*map(range, self.other.shape[:-2])):
            self.other[index] = self.other[index] + self.kept(index)
        self.ref = self.other
        self.dims = self.dims[: self.axis] + self.dims[self.axis + 1 :]

    def step(self):
        self.finish()
        self.start()

    def last(self, put):
        self.copy.wait()
        for index in itertools.product(*map(range, self.other.shape[:-2])):
            put(index, self.other[index].astype(F32) + self.kept(index).astype(F32))


class Total:
    def __init__(self, at, ref, buffers, send_sems, recv_sems, first):
        self.at, self.ref, self.buffers = at, ref, buffers
        self.sems, self.next, self.stage = (send_sems, recv_sems), first, 0

    def start(self):
        i = self.next + self.stage
        self.copy = send(self.at, BITS[self.stage], self.ref, self.buffers.at[self.stage], self.sems[0].at[i], self.sems[1].at[i])

    def finish(self):
        self.copy.wait()
        got = self.buffers.at[self.stage]
        got[...] = self.ref[...] + got[...]
        self.ref, self.stage = got, self.stage + 1

    def step(self):
        self.finish()
        self.start()


BITS = ("core", "z1", "y", "z0", "x")
PART_A = (("z1", "z0", "y"), ("z0", "y", "z1"))
PART_B = (("z1", "z0", "x"), ("x", "z0", "z1"))
PART_C = (("x", "j", "z1", "z0"), ("z0", "x", "z1"))
PART_D = (("x", "j", "z1", "y"), ("y", "x", "z1"))
MATRIX = ("z1", "z0", "y", "core", "x")
ORDERS = (("core", "x", "y", "z0", "z1"), ("core", "y", "z0", "x", "z1"), ("core", "z0", "x", "y", "z1"))
OUT_ORDER = ("core", "x", "y", "z0", "z1")


def stage_shapes(dims, order, rows, cols):
    left, shapes = list(dims), []
    for bit in order:
        left.remove(bit)
        shapes.append((2,) * len(left) + (rows, cols))
    return shapes


def everything(
    tok, seg_hbm, keep_hbm, g1_hbm, bias1_hbm, wqkv_hbm, qb_hbm, vb_hbm, ow_hbm, ob_hbm, g2_hbm, bias2_hbm, w1_hbm, b1_hbm, w2_hbm, c2_hbm, dy_hbm,
    out_hbm, gt_hbm, qkv_hbm, o_hbm, fc1_hbm, fc2_hbm, vec_hbm, late_hbm,
    seg, keep, g1, bias1, ob, g2, bias2, c2, qb, vb, b1,
    x, xn, wqkv, proj, att, scale_two, lse, delta, stat, mask, dy, ow, w1, w2, hidden, xhat, rstd, n2, n2t, z, da, act, di,
    f1, f2, r1, r2, pa, pb, pc, pd, d_att, qg, biases, vec, late, early_buf, late_buf, *rest,
):
    rows, width = x.shape
    half = rows // 2
    heads = width // HEAD_DIM
    cols = width
    chunks = w2.shape[0] // cols
    stage_bufs = list(rest[:-7])
    sems, send_sems, recv_sems, core_send, core_recv, next_send, next_recv = rest[-7:]
    at = place()
    t = at["x"]
    far, near = t * half, (1 - t) * half
    own_rows, halo_rows, near_rows = pl.ds(0, rows), pl.ds(rows, half), pl.ds(half, half)
    barrier = pltpu.get_barrier_semaphore()
    for bit in BITS:
        pl.semaphore_signal(barrier, inc=1, device_id=peer(at, bit), device_id_type=MESH)

    def fetch(src, dst, i):
        c = pltpu.make_async_copy(src, dst, sems.at[i])
        c.start()
        return c

    small = ((seg_hbm, seg), (keep_hbm, keep), (g1_hbm, g1), (bias1_hbm, bias1), (ob_hbm, ob), (g2_hbm, g2), (bias2_hbm, bias2), (c2_hbm, c2), (qb_hbm, qb), (vb_hbm, vb), (b1_hbm, b1))
    got_small = [fetch(src, dst, 6 + 2 * chunks + i) for i, (src, dst) in enumerate(small)]
    got_x = [fetch(tok.at[pl.ds(far, half)], x.at[pl.ds(0, half)], 0), fetch(tok.at[pl.ds(near, half)], x.at[near_rows], 1)]
    got_wqkv = fetch(wqkv_hbm, wqkv, 2)
    pl.semaphore_wait(barrier, len(BITS))
    used = [0]

    def job(bit, src, dst):
        i, used[0] = used[0], used[0] + 1
        return send(at, bit, src, dst, send_sems.at[i], recv_sems.at[i])

    token_halo = job("x", tok.at[pl.ds(near, half)], xn.at[halo_rows])

    for g in got_small:
        g.wait()
    starts = (t * (rows + half), t * rows + (1 - t) * half, (1 - t) * rows + t * half)
    slots = [pl.ds(pl.multiple_of(s, 128), half) for s in starts]
    ids = jnp.concatenate([seg[:, s] for s in slots], axis=1)
    kept_row = jnp.concatenate([keep[:, s] for s in slots], axis=1)
    key_row = jnp.where(kept_row == 1, ids, -1)
    table = jnp.concatenate([ids, key_row, kept_row, jnp.zeros((5, rows + half), jnp.int32)], axis=0)
    columns = jnp.transpose(table.astype(F32))
    id_col, key_col, kept_col = columns[:, 0:1], columns[:, 1:2], columns[:, 2:3]
    id_row, key_row = ids.astype(F32), key_row.astype(F32)
    query_at = lax.broadcasted_iota(jnp.int32, (half, rows + half), 0)
    key_at = lax.broadcasted_iota(jnp.int32, (half, rows + half), 1)
    for part in range(2):
        same = id_col[part * half : (part + 1) * half] == key_row
        mask[pl.ds(part * half, half), :] = jnp.where(same | (query_at + part * half == key_at), 0.0, MASKED)
    rstd[...] = jnp.broadcast_to(kept_col[:rows], rstd.shape)
    for i in range(chunks):
        biases[i : i + 1, :] = b1[i * cols : (i + 1) * cols].reshape(1, cols)
    for i, ref in enumerate((g1, bias1, ob, g2, bias2, c2, qb, vb)):
        biases[8 + i : 9 + i, :] = ref[...].reshape(1, width)
    gain_one, bias_one, out_bias, gain_two, bias_two, fc2_bias = (biases[8 + i : 9 + i, :] for i in range(6))
    vec[...] = jnp.zeros_like(vec)
    late[...] = jnp.zeros_like(late)
    vec[12:13, 0:128] = jnp.sum(rstd[...], axis=0, keepdims=True)
    rb = 128

    def normalize(src, dst, start, count):
        def one(i, _):
            rs = pl.ds(pl.multiple_of(start + i * rb, rb), rb)
            v = src[rs, :].astype(F32)
            centred = v - jnp.mean(v, axis=-1, keepdims=True)
            var = jnp.mean(centred * centred, axis=-1, keepdims=True)
            dst[rs, :] = (centred * lax.rsqrt(var + 1e-06) * gain_one + bias_one).astype(BF)
            return 0

        lax.fori_loop(0, count // rb, one, 0, unroll=2)

    def project(start, count, which):
        rs = pl.ds(start, count)
        for j in which:
            js = pl.ds(j * width, width)
            v = mm(xn[rs, :], wqkv[:, js])
            if j == 0:
                proj[rs, js] = (v + biases[14:15, :]).astype(BF) * BF(HEAD_DIM ** (-0.5))
            elif j == 1:
                proj[rs, js] = v.astype(BF)
            else:
                proj[rs, js] = (v + biases[15:16, :]).astype(BF)

    lane = lax.broadcasted_iota(jnp.int32, (1, PAIR), 1)

    def cut(v, head):
        return jnp.where((lane < HEAD_DIM) == (head == 0), v, 0).astype(BF)

    def both(a, b):
        return jnp.where(lane < HEAD_DIM, a, b)

    def scores(p, query_rows, mask_rows, key_start, keys):
        c = pl.multiple_of(p * PAIR, PAIR)
        ks = pl.ds(key_start, keys)
        q, k, v = proj[query_rows, pl.ds(c, PAIR)], proj[ks, pl.ds(width + c, PAIR)], proj[ks, pl.ds(2 * width + c, PAIR)]
        total, new_tops = None, []
        for head in range(2):
            s = mm_nt(cut(q, head), k) + mask[mask_rows, ks]
            top = jnp.max(s, axis=-1, keepdims=True)
            e = jnp.exp(s - top).astype(BF)
            ones = jnp.broadcast_to(cut(jnp.ones((1, PAIR), BF), head), (keys, PAIR))
            part = mm(e, jnp.concatenate([cut(v, head), ones], axis=1))
            total = part if total is None else total + part
            new_tops.append(top)
        return total[:, :PAIR], total[:, PAIR:], both(new_tops[0], new_tops[1])

    def attended(p, rs, value, sums, tops):
        c = pl.ds(pl.multiple_of(p * PAIR, PAIR), PAIR)
        att[rs, c] = (value / sums).astype(BF)
        hidden[rs, c] = tops + jnp.log(sums)

    def attend_far(p, _):
        rs = pl.ds(0, half)
        attended(p, rs, *scores(p, rs, rs, 0, rows))
        return 0

    def attend_near(p, _):
        c = pl.ds(pl.multiple_of(p * PAIR, PAIR), PAIR)
        z[pl.ds(0, half), c], z[near_rows, c], da[near_rows, c] = scores(p, near_rows, near_rows, 0, rows)
        return 0

    def attend_halo(p, _):
        c = pl.ds(pl.multiple_of(p * PAIR, PAIR), PAIR)
        before = da[near_rows, c]
        value, sums, after = scores(p, near_rows, near_rows, rows, half)
        tops = jnp.maximum(before, after)
        old, new = jnp.exp(before - tops), jnp.exp(after - tops)
        attended(p, near_rows, value * new + z[pl.ds(0, half), c] * old, sums * new + z[near_rows, c] * old, tops)
        return 0

    for g in got_x:
        g.wait()
    normalize(x, xn, 0, rows)
    got_wqkv.wait()
    got_dy = [fetch(dy_hbm.at[pl.ds(far, half)], dy.at[pl.ds(0, half)], 3), fetch(dy_hbm.at[pl.ds(near, half)], dy.at[near_rows], 4)]
    got_ow = fetch(ow_hbm, ow, 5)
    got_w = []
    for c in range(chunks):
        got_w.append(fetch(w1_hbm.at[:, pl.ds(c * cols, cols)], w1.at[:, pl.ds(c * cols, cols)], 6 + 2 * c))
        got_w.append(fetch(w2_hbm.at[pl.ds(c * cols, cols)], w2.at[pl.ds(c * cols, cols)], 7 + 2 * c))
    project(0, rows, (0, 1, 2))
    lax.fori_loop(0, heads // 2, attend_far, 0, unroll=6)
    lax.fori_loop(0, heads // 2, attend_near, 0, unroll=3)
    token_halo.wait()
    normalize(xn, xn, rows, half)
    project(rows, half, (1, 2))
    lax.fori_loop(0, heads // 2, attend_halo, 0, unroll=3)
    head_row = lax.broadcasted_iota(jnp.int32, (16, width), 0) * HEAD_DIM
    lane_at = lax.broadcasted_iota(jnp.int32, (16, width), 1)
    first = jnp.where(lane_at == head_row, 1.0, 0.0).astype(BF)
    logs = hidden[...]
    high = logs.astype(BF)
    mid = (logs - high.astype(F32)).astype(BF)
    low = (logs - high.astype(F32) - mid.astype(F32)).astype(BF)
    lse[...] = mm_nt(first, high) + mm_nt(first, mid) + mm_nt(first, low)
    got_ow.wait()

    def add_vec(ref, i, v):
        ref[i : i + 1, :] += jnp.sum(v, axis=0, keepdims=True)

    def front(i, _):
        rs = pl.ds(pl.multiple_of(i * rb, rb), rb)
        branch = mm(att[rs, :], ow[...]) + out_bias
        xs = x[rs, :].astype(F32)
        h = xs + branch
        hidden[rs, :] = h
        kept = rstd[rs, :][:, 0:1]
        add_vec(vec, 0, kept * xs * xs)
        add_vec(vec, 1, kept * branch * branch)
        centred = h - jnp.mean(h, axis=-1, keepdims=True)
        r = lax.rsqrt(jnp.mean(centred * centred, axis=-1, keepdims=True) + 1e-06)
        xh = centred * r
        xhat[rs, :] = xh
        scale_two[rs, :] = jnp.broadcast_to(r, (rb, PAIR))
        n2[rs, :] = (xh * gain_two + bias_two).astype(BF)
        return 0

    lax.fori_loop(0, rows // rb, front, 0, unroll=2)
    n2t[...] = jnp.transpose(n2[...])
    for g in got_dy:
        g.wait()

    def core_copies(c):
        hi, lo = c // 2, c % 2
        other = 1 - at["core"]
        pairs = ((f1.at[:, :, :, other], r1.at[hi, lo]), (f2.at[:, :, other], r2.at[hi, lo]))
        return [
            pltpu.make_async_remote_copy(s, d, core_send.at[i, c], core_recv.at[i, c], device_id=peer(at, "core"), device_id_type=MESH)
            for i, (s, d) in enumerate(pairs)
        ]

    def next_copies(c):
        hi, lo = c // 2, c % 2
        jobs = (
            ("x", r2.at[hi, lo, 1 - t, :, :, pl.ds(0, 256)], pa.at[hi, lo]),
            ("y", r2.at[hi, lo, :, 1 - at["y"], :, pl.ds(256, 128)], pb.at[hi, lo]),
            ("y", r1.at[hi, lo, :, :, 1 - at["y"], :, pl.ds(0, 256)], pc.at[hi, lo]),
            ("z0", r1.at[hi, lo, :, 1 - at["z0"], :, :, pl.ds(256, 512)], pd.at[hi, lo]),
        )
        return [
            pltpu.make_async_remote_copy(s, d, next_send.at[i, c], next_recv.at[i, c], device_id=peer(at, bit), device_id_type=MESH)
            for i, (bit, s, d) in enumerate(jobs)
        ]

    def pass_on(c):
        hi, lo = c // 2, c % 2
        mine = at["core"]
        for copy in core_copies(c):
            copy.wait()

        def one(i, _):
            a, b, d = i // 4, i // 2 % 2, i % 2
            r1[hi, lo, a, b, d] += f1[a, b, d, mine]
            return 0

        lax.fori_loop(0, 8, one, 0, unroll=2)

        def two(i, _):
            r2[hi, lo, i // 2, i % 2] += f2[i // 2, i % 2, mine]
            return 0

        lax.fori_loop(0, 4, two, 0)
        for copy in next_copies(c):
            copy.start()

    def chunk(c, _):
        for i in range(2):
            pltpu.make_async_copy(w2_hbm.at[pl.ds(0, cols)], w2.at[pl.ds(0, cols)], sems.at[6 + 2 * c + i]).wait()
        here = pl.ds(pl.multiple_of(c * cols, cols), cols)
        z[...] = mm(n2[...], w1[:, here]) + biases[pl.ds(c, 1), :]
        da[...] = mm_nt(dy[...], w2[here, :])
        gr = 64
        bsum = jnp.zeros((1, cols), F32)
        for i in range(rows // gr):
            rs = pl.ds(i * gr, gr)
            a, s = gelu_and_slope(z[rs, :])
            act[rs, here] = a.astype(BF)
            d = (da[rs, :] * s).astype(BF)
            di[rs, here] = d
            bsum = bsum + jnp.sum(d.astype(F32), axis=0, keepdims=True)
        vec[pl.ds(8 + c, 1), :] = bsum

        @pl.when(c > 0)
        def _():
            pass_on(c - 1)

        f1[...] = mm(n2t[...], di[:, here]).astype(BF).reshape(f1.shape)
        g = mm_tn(act[:, here], dy[...]).astype(BF)
        f2[0] = g[:, : width // 2].reshape(f2.shape[1:])
        f2[1] = g[:, width // 2 :].reshape(f2.shape[1:])
        for copy in core_copies(c):
            copy.start()
        return 0

    lax.fori_loop(0, chunks, chunk, 0)
    da[...] = mm_nt(di[...], w1[...])
    pass_on(chunks - 1)

    def middle(i, _):
        rs = pl.ds(pl.multiple_of(i * rb, rb), rb)
        g = da[rs, :]
        xh = xhat[rs, :]
        add_vec(vec, 4, g * xh)
        add_vec(vec, 5, g)
        gy = g * gain_two
        mean_gy = jnp.mean(gy, axis=-1, keepdims=True)
        mean_gx = jnp.mean(gy * xh, axis=-1, keepdims=True)
        dys = dy[rs, :].astype(F32)
        add_vec(vec, 7, dys)
        dh = dys + scale_two[rs, :][:, 0:1] * (gy - mean_gy - xh * mean_gx)
        xhat[rs, :] = dh
        low = dh.astype(BF)
        n2[rs, :] = low
        add_vec(vec, 6, low.astype(F32))
        return 0

    lax.fori_loop(0, rows // rb, middle, 0, unroll=2)
    d_att[own_rows, :] = mm_nt(n2[...], ow[...]).astype(BF)
    mine = jnp.where((lane_at >= head_row) & (lane_at < head_row + HEAD_DIM), 1.0, 0.0).astype(BF)
    prod = d_att[own_rows, :].astype(F32) * att[...].astype(F32)
    hi = prod.astype(BF)
    lo = (prod - hi.astype(F32)).astype(BF)
    delta[...] = mm_nt(mine, hi) + mm_nt(mine, lo)
    halos = [
        job("x", d_att.at[near_rows], d_att.at[halo_rows]),
        job("x", lse.at[:, near_rows], stat.at[0]),
        job("x", delta.at[:, near_rows], stat.at[1]),
    ]

    def share(ref, dims, order):
        bufs = [stage_bufs.pop(0) for _ in order]
        first, used[0] = used[0], used[0] + len(order)
        return Share(at, ref, dims, order, bufs, send_sems, recv_sems, first)

    og = qg.at[2]
    A, B, C, D = (share(ref, *part) for ref, part in ((pa, PART_A), (pb, PART_B), (pc, PART_C), (pd, PART_D)))
    O = share(og, MATRIX, OUT_ORDER)
    Q = [share(qg.at[i], MATRIX, ORDERS[i]) for i in range(3)]
    early = Total(at, vec, early_buf, send_sems, recv_sems, used[0])
    later = Total(at, late, late_buf, send_sems, recv_sems, used[0] + 5)
    early.start()
    def settle(c, _):
        hi, lo = c // 2, c % 2
        for copy in next_copies(c):
            copy.wait()
        for i in range(2):
            pa[hi, lo, i] += r2[hi, lo, t, i, :, 0:256]
            pb[hi, lo, i] += r2[hi, lo, i, at["y"], :, 256:384]
            for j in range(2):
                pc[hi, lo, i, j] += r1[hi, lo, i, j, at["y"], :, 0:256]
                pd[hi, lo, i, j] += r1[hi, lo, i, at["z0"], j, :, 256:768]
        return 0

    n2t[...] = jnp.transpose(att[...])
    for i in range(2):
        og_half = mm(n2t[...], n2[:, i * (width // 2) : (i + 1) * (width // 2)]).astype(BF)
        og[:, :, :, :, i] = og_half.reshape((2, 2, 2, 2) + og.shape[-2:])
    O.start()

    key_at = lax.broadcasted_iota(jnp.int32, (half, rows), 0)
    query_at = lax.broadcasted_iota(jnp.int32, (half, rows), 1)
    for part in range(2):
        same = key_col[part * half : (part + 1) * half] == id_row[:, :rows]
        mask[pl.ds(part * half, half), pl.ds(0, rows)] = jnp.where(same | (query_at == key_at + part * half), 0.0, MASKED)
    mask[pl.ds(0, half), halo_rows] = jnp.where(key_col[half:rows] == id_row[:, rows:], 0.0, MASKED)
    mask[near_rows, halo_rows] = jnp.where(key_col[rows:] == id_row[:, half:rows], 0.0, MASKED)

    def own(p, _):
        c = pl.multiple_of(p * PAIR, PAIR)
        col, kcol, vcol = pl.ds(c, PAIR), pl.ds(width + c, PAIR), pl.ds(2 * width + c, PAIR)
        q, k, v = proj[own_rows, col], proj[:, kcol], proj[:, vcol]
        do = d_att[own_rows, col]
        gq = gk = gv = gn = None
        for head in range(2):
            qh, kh, doh = cut(q, head), cut(k, head), cut(do, head)
            ls = lse[pl.ds(2 * p + head, 1), :]
            de = delta[pl.ds(2 * p + head, 1), :]
            prob = jnp.exp(mm_nt(k[:rows], qh) + mask[:, pl.ds(0, rows)] - ls)
            ds = (prob * (mm_nt(v[:rows], doh) - de)).astype(BF)
            a = mm(prob.astype(BF), doh)
            b = mm(ds, qh)
            c = mm_tn(ds, kh[:rows])
            prob = jnp.exp(mm_nt(k[rows:], qh[half:]) + mask[near_rows, halo_rows] - ls[:, half:])
            ds = (prob * (mm_nt(v[rows:], doh[half:]) - de[:, half:])).astype(BF)
            d = mm_tn(ds, kh[rows:])
            gv = a if gv is None else gv + a
            gk = b if gk is None else gk + b
            gq = c if gq is None else gq + c
            gn = d if gn is None else gn + d
        scale = HEAD_DIM ** (-0.5)
        di[pl.ds(0, half), col] = (gq[:half] * scale).astype(BF)
        di[near_rows, col] = ((gq[half:] + gn) * scale).astype(BF)
        di[pl.ds(0, half), kcol] = gk[:half].astype(BF)
        di[pl.ds(0, half), vcol] = gv[:half].astype(BF)
        z[pl.ds(0, half), col] = gk[half:]
        z[near_rows, col] = gv[half:]
        return 0

    def halo(p, _):
        c = pl.multiple_of(p * PAIR, PAIR)
        col, kcol, vcol = pl.ds(c, PAIR), pl.ds(width + c, PAIR), pl.ds(2 * width + c, PAIR)
        q, k, v = proj[halo_rows, col], proj[near_rows, kcol], proj[near_rows, vcol]
        do = d_att[halo_rows, col]
        gk, gv = z[pl.ds(0, half), col], z[near_rows, col]
        for head in range(2):
            qh, doh = cut(q, head), cut(do, head)
            ls = stat[0, pl.ds(2 * p + head, 1), :]
            de = stat[1, pl.ds(2 * p + head, 1), :]
            prob = jnp.exp(mm_nt(k, qh) + mask[pl.ds(0, half), halo_rows] - ls)
            ds = (prob * (mm_nt(v, doh) - de)).astype(BF)
            gv = gv + mm(prob.astype(BF), doh)
            gk = gk + mm(ds, qh)
        di[near_rows, kcol] = gk.astype(BF)
        di[near_rows, vcol] = gv.astype(BF)
        return 0

    n2t[...] = jnp.transpose(xn[own_rows, :])
    project(rows, half, (0,))
    lax.fori_loop(0, 2, own, 0, unroll=2)
    early.step()
    O.step()
    lax.fori_loop(0, chunks, settle, 0)
    for s in (B, C, A, D):
        s.start()
    lax.fori_loop(2, heads // 2, own, 0, unroll=2)
    early.step()
    for h in halos:
        h.wait()
    lax.fori_loop(0, heads // 2, halo, 0, unroll=3)
    third = width // 2

    def weigh(j):
        g = mm(n2t[...], di[:, pl.ds(j * width, width)]).astype(BF)
        for i in range(2):
            side, part = divmod(2 * j + i, 3)
            qg[part, :, :, :, :, side] = g[:, i * third : (i + 1) * third].reshape((2, 2, 2, 2) + qg.shape[-2:])

    weigh(0)
    weigh(1)
    Q[0].start()
    weigh(2)
    Q[1].start()
    Q[2].start()
    z[...] = mm(act[...], w2[...])
    early.step()
    for s in (B, C, A, D):
        s.step()
    for s in Q:
        s.step()
    O.step()
    da[...] = mm_nt(di[:, pl.ds(0, 3 * width)], wqkv[...])

    def back(i, _):
        rs = pl.ds(pl.multiple_of(i * rb, rb), rb)
        xs = x[rs, :].astype(F32)
        centred = xs - jnp.mean(xs, axis=-1, keepdims=True)
        r = lax.rsqrt(jnp.mean(centred * centred, axis=-1, keepdims=True) + 1e-06)
        xh = centred * r
        g = da[rs, :]
        add_vec(late, 0, g * xh)
        add_vec(late, 1, g)
        gy = g * gain_one
        mean_gy = jnp.mean(gy, axis=-1, keepdims=True)
        mean_gx = jnp.mean(gy * xh, axis=-1, keepdims=True)
        w1[rs, pl.ds(width, width)] = (xhat[rs, :] + r * (gy - mean_gy - xh * mean_gx)).astype(BF)
        add_vec(late, 2, di[rs, pl.ds(0, width)].astype(F32))
        add_vec(late, 3, di[rs, pl.ds(2 * width, width)].astype(F32))
        branch = z[rs, :] + fc2_bias
        result = hidden[rs, :] + branch
        w1[rs, pl.ds(0, width)] = result.astype(BF)
        kept = rstd[rs, :][:, 0:1]
        add_vec(late, 4, kept * branch * branch)
        add_vec(late, 5, kept * result * result)
        return 0

    lax.fori_loop(0, rows // rb, back, 0)
    later.start()
    copies = [
        fetch(w1.at[pl.ds(0, half), pl.ds(0, width)], out_hbm.at[pl.ds(far, half)], 0),
        fetch(w1.at[near_rows, pl.ds(0, width)], out_hbm.at[pl.ds(near, half)], 1),
        fetch(w1.at[pl.ds(0, half), pl.ds(width, width)], gt_hbm.at[pl.ds(far, half)], 2),
        fetch(w1.at[near_rows, pl.ds(width, width)], gt_hbm.at[pl.ds(near, half)], 3),
    ]

    block, wide = width // 16, w2.shape[0] // 16

    def put_a(_, v):
        z[pl.ds(0, wide), 0:256] = v

    def put_b(_, v):
        z[pl.ds(0, wide), 256:384] = v

    def put_c(i, v):
        z[pl.ds(wide + i[0] * block, block), 0:256] = v

    def put_d(i, v):
        z[pl.ds(wide + i[0] * block, block), 256:768] = v

    def put_o(_, v):
        z[pl.ds(wide + 2 * block, block), 0:384] = v

    early.step()
    later.step()
    for s in (B, C, A, D):
        s.step()
    for _ in range(3):
        for s in Q:
            s.finish()
        later.step()
        for s in Q:
            s.start()
        if O.order:
            O.step()
    early.finish()
    copies.append(fetch(early.ref, vec_hbm, 4))
    for s, put in ((A, put_a), (B, put_b), (C, put_c), (D, put_d)):
        s.last(put)
    O.last(put_o)
    copies += [
        fetch(z.at[pl.ds(0, wide), pl.ds(0, width // 2)], fc2_hbm, 5),
        fetch(z.at[pl.ds(wide, block)], fc1_hbm.at[:, pl.ds(0, width)], 6),
        fetch(z.at[pl.ds(wide + block, block)], fc1_hbm.at[:, pl.ds(width, width)], 7),
        fetch(z.at[pl.ds(wide + 2 * block, block), pl.ds(0, width // 2)], o_hbm, 8),
    ]
    for i in range(3):

        def put_q(_, v, i=i):
            da[pl.ds(i * block, block), 0:384] = v

        Q[i].last(put_q)
        copies.append(fetch(da.at[pl.ds(i * block, block), pl.ds(0, third)], qkv_hbm.at[:, pl.ds(i * third, third)], 10 + i))
    later.finish()
    copies.append(fetch(later.ref, late_hbm, 9))
    for c in copies:
        c.wait()


def call_everything(tokens, seg, keep, g1, bias1, wqkv, qb, vb, ow, ob, g2, bias2, w1, b1, w2, c2, dy):
    rows, width = tokens.shape
    half = rows // 2
    hid = w1.shape[1]
    chunks = hid // width
    block, wide = width // 16, hid // 16
    sds = jax.ShapeDtypeStruct
    V = pltpu.VMEM
    parts = ((2, 2, 2, wide, 256), (2, 2, 2, wide, 128), (2, 2, 2, 2, block, 256), (2, 2, 2, 2, block, 512))
    stages = (
        stage_shapes(*PART_A, wide, 256)
        + stage_shapes(*PART_B, wide, 128)
        + stage_shapes(*PART_C, block, 256)
        + stage_shapes(*PART_D, block, 512)
        + stage_shapes(MATRIX, OUT_ORDER, block, width // 2)
        + [s for order in ORDERS for s in stage_shapes(MATRIX, order, block, width // 2)]
    )
    jobs = 4 + len(stages) + 10
    DMA = pltpu.SemaphoreType.DMA
    return pl.pallas_call(
        everything,
        out_shape=(
            sds((rows, width), BF), sds((rows, width), BF), sds((block, 3 * width // 2), F32), sds((block, width // 2), F32),
            sds((block, hid // 2), F32), sds((wide, width // 2), F32), sds((16, width), F32), sds((8, width), F32),
        ),
        in_specs=[any_spec()] * 17,
        out_specs=(any_spec(),) * 8,
        scratch_shapes=[V(seg.shape, jnp.int32), V(keep.shape, jnp.int32)] + [V((width,), F32)] * 8 + [
            V((hid,), F32),
            V((rows, width), BF), V((rows + half, width), BF), V((width, 3 * width), BF), V((rows + half, 3 * width), BF),
            V((rows, width), BF), V((rows, PAIR), F32), V((16, rows), F32), V((16, rows), F32), V((2, 16, half), F32),
            V((rows, rows + half), F32), V((rows, width), BF), V((width, width), BF), V((width, hid), BF), V((hid, width), BF),
            V((rows, width), F32), V((rows, width), F32), V((rows, PAIR), F32), V((rows, width), BF), V((width, rows), BF),
            V((rows, width), F32), V((rows, width), F32), V((rows, hid), BF), V((rows, hid), BF),
            V((2, 2, 2, 2, block, width), BF), V((2, 2, 2, wide, width // 2), BF),
            V((2, 2, 2, 2, 2, block, width), BF), V((2, 2, 2, 2, wide, width // 2), BF),
        ] + [V(s, BF) for s in parts] + [
            V((rows + half, width), BF), V((3, 2, 2, 2, 2, 2, block, width // 2), BF),
            V((16, width), F32), V((16, width), F32), V((8, width), F32), V((5, 16, width), F32), V((5, 8, width), F32),
        ] + [V(s, BF) for s in stages] + [
            DMA((17 + 2 * chunks,)), DMA((jobs,)), DMA((jobs,)),
            DMA((2, chunks)), DMA((2, chunks)), DMA((4, chunks)), DMA((4, chunks)),
        ],
        compiler_params=pltpu.CompilerParams(collective_id=0, has_side_effects=True, vmem_limit_bytes=67043328),
        name="everything",
    )(tokens, seg, keep, g1, bias1, wqkv, qb, vb, ow, ob, g2, bias2, w1, b1, w2, c2, dy)


def finish(*refs):
    ins, outs, bufs, sems = refs[:8], refs[8:24], refs[24:-1], refs[-1]
    loads = [pltpu.make_async_copy(src, buf, sems.at[i]) for i, (src, buf) in enumerate(zip(ins, bufs[:8]))]
    for c in loads:
        c.start()
    vec, late = bufs[6:8]
    lines = bufs[8:]
    width = lines[0].shape[0]
    out, gt, g1, b1, qkv, qb, vb, o, ob, g2, b2, f1, f1b, f2, f2b, rm = outs
    stores = []

    def store(src, dst):
        c = pltpu.make_async_copy(src, dst, sems.at[8 + len(stores)])
        c.start()
        stores.append(c)

    loads[6].wait()
    loads[7].wait()
    rows = ((g1, late, 0), (b1, late, 1), (qb, late, 2), (vb, late, 3), (ob, vec, 6), (g2, vec, 4), (b2, vec, 5), (f2b, vec, 7))
    for (dst, src, i), line in zip(rows, lines):
        line[...] = src[i, :]
        store(line, dst)
    for i in range(4):
        lines[8][pl.ds(i * width, width)] = vec[8 + i, :]
    store(lines[8], f1b)
    squares = jnp.concatenate([vec[0:2, :], late[4:6, :]], axis=0)
    ratio = jnp.sqrt(jnp.sum(squares, axis=1, keepdims=True) / (vec[12:13, 0:1] * width))
    for i in range(4):
        rm[i] = ratio[i, 0]
    for i, dst in enumerate((out, gt, qkv, o, f1, f2)):
        loads[i].wait()
        store(bufs[i], dst)
    for c in stores:
        c.wait()


def call_finish(out, gt, qkv, o, f1, f2, vec, late, hid):
    width = out.shape[1]
    sds = jax.ShapeDtypeStruct
    line = sds((width,), F32)
    shapes = (
        sds(out.shape, BF), sds(gt.shape, BF), line, line, sds(qkv.shape, F32), line, line, sds(o.shape, F32), line, line, line,
        sds(f1.shape, F32), sds((hid,), F32), sds(f2.shape, F32), line, sds((4,), F32),
    )
    args = (out, gt, qkv, o, f1, f2, vec, late)
    return pl.pallas_call(
        finish,
        out_shape=shapes,
        in_specs=[any_spec()] * 8,
        out_specs=(any_spec(),) * 15 + (pl.BlockSpec(memory_space=pltpu.SMEM),),
        scratch_shapes=[pltpu.VMEM(v.shape, v.dtype) for v in args] + [pltpu.VMEM((width,), F32)] * 8
        + [pltpu.VMEM((hid,), F32), pltpu.SemaphoreType.DMA((24,))],
        name="finish",
    )(*args)


def layer_norm(values, norm_gain, norm_bias):
    average = jnp.mean(values, axis=-1, keepdims=True)
    centred = values - average
    variance = jnp.mean(centred * centred, axis=-1, keepdims=True)
    return centred * lax.rsqrt(variance + 1e-06) * norm_gain + norm_bias


def exact_gelu(values):
    return jax.nn.gelu(values, approximate=False)


def on_device_general(
    tokens,
    segment_ids,
    keep_mask,
    gain_one,
    bias_one,
    qkv_weight,
    query_bias,
    value_bias,
    out_weight,
    out_bias,
    gain_two,
    bias_two,
    fc1_weight,
    fc1_bias,
    fc2_weight,
    fc2_bias,
    cotangent,
):
    sequences, tile_rows, model_width = tokens.shape
    length = segment_ids.shape[1]
    count_rows = sequences * tile_rows
    head_block = 4 * HEAD_DIM
    score_scale = HEAD_DIM ** (-0.5)
    offset = lax.axis_index("tile") * tile_rows
    query_ids = lax.dynamic_slice_in_dim(segment_ids, offset, tile_rows, 1)
    query_keep = lax.dynamic_slice_in_dim(keep_mask, offset, tile_rows, 1)
    positions = offset + jnp.arange(tile_rows, dtype=jnp.int32)
    key_places = jnp.arange(length, dtype=jnp.int32)
    own_slot = positions[:, None] == key_places[None, :]
    usable = (keep_mask[:, None, :] == 1) | own_slot[None]
    allowed = ((query_ids[:, :, None] == segment_ids[:, None, :]) & usable)[:, None]
    flattened = tokens.reshape(count_rows, model_width).astype(jnp.float32)
    normed = layer_norm(flattened, gain_one, bias_one)
    normed_low = normed.astype(jnp.bfloat16)
    key_bias = jnp.zeros_like(query_bias)
    projected = jnp.dot(
        normed_low, qkv_weight, preferred_element_type=jnp.float32
    ) + jnp.concatenate([query_bias, key_bias, value_bias])
    projected_low = projected.astype(jnp.bfloat16).reshape(sequences, tile_rows, 3 * model_width)
    queries = projected_low[..., :model_width]
    shared_local = projected_low[..., model_width:]
    shared_all = lax.all_gather(shared_local, "tile", axis=1, tiled=True)
    keys_all = shared_all[..., :model_width]
    values_all = shared_all[..., model_width:]
    key_count = shared_all.shape[1]

    def split_heads(source, column):
        sliced = source[..., column : column + head_block]
        return sliced.reshape(sliced.shape[0], sliced.shape[1], 4, HEAD_DIM)

    def block_scores(query_part, key_part):
        scores = (
            jnp.einsum("sqhe,skhe->shqk", query_part, key_part, preferred_element_type=jnp.float32)
            * score_scale
        )
        return jnp.where(allowed, scores, -1e30)

    attended_parts = []
    logsums = []
    for column in range(0, model_width, head_block):
        masked = block_scores(split_heads(queries, column), split_heads(keys_all, column))
        row_peak = jnp.max(masked, axis=-1, keepdims=True)
        exponent = jnp.exp(masked - row_peak)
        row_total = jnp.sum(exponent, axis=-1, keepdims=True)
        softmax_probs = (exponent / row_total).astype(jnp.bfloat16)
        logsums.append(row_peak + jnp.log(row_total))
        attended_parts.append(
            jnp.einsum(
                "shqk,skhe->sqhe",
                softmax_probs,
                split_heads(values_all, column),
                preferred_element_type=jnp.float32,
            )
        )
    attended = jnp.concatenate(attended_parts, axis=2)
    attended_low = attended.reshape(count_rows, model_width).astype(jnp.bfloat16)
    branch_one = jnp.dot(attended_low, out_weight, preferred_element_type=jnp.float32) + out_bias
    hidden = flattened + branch_one
    normed_two = layer_norm(hidden, gain_two, bias_two)
    normed_two_low = normed_two.astype(jnp.bfloat16)
    inner = jnp.dot(normed_two_low, fc1_weight, preferred_element_type=jnp.float32) + fc1_bias
    active_low = exact_gelu(inner).astype(jnp.bfloat16)
    branch_two = jnp.dot(active_low, fc2_weight, preferred_element_type=jnp.float32) + fc2_bias
    result = hidden + branch_two
    output = result.astype(jnp.bfloat16).reshape(sequences, tile_rows, model_width)
    weighting = query_keep.reshape(count_rows, 1).astype(jnp.float32)
    squares = [
        jnp.sum(weighting * member * member)
        for member in (flattened, branch_one, branch_two, result)
    ]
    stats = jnp.stack(squares + [jnp.sum(weighting)])
    grad_result = cotangent.reshape(count_rows, model_width)
    fc2_grad = jnp.einsum("nf,nd->fd", active_low, grad_result, preferred_element_type=jnp.float32)
    fc2_bias_grad = jnp.sum(grad_result.astype(jnp.float32), axis=0)
    grad_active = jnp.einsum(
        "nd,fd->nf", grad_result, fc2_weight, preferred_element_type=jnp.float32
    )
    inner_value, gelu_back = jax.vjp(exact_gelu, inner)
    grad_inner_low = gelu_back(grad_active)[0].astype(jnp.bfloat16)
    fc1_grad = jnp.einsum(
        "nd,nf->df", normed_two_low, grad_inner_low, preferred_element_type=jnp.float32
    )
    fc1_bias_grad = jnp.sum(grad_inner_low.astype(jnp.float32), axis=0)
    grad_normed_two = jnp.einsum(
        "nf,df->nd", grad_inner_low, fc1_weight, preferred_element_type=jnp.float32
    )
    normed_again, norm_back_two = jax.vjp(layer_norm, hidden, gain_two, bias_two)
    grad_hidden_part, gain_two_grad, bias_two_grad = norm_back_two(grad_normed_two)
    grad_hidden = grad_result.astype(jnp.float32) + grad_hidden_part
    grad_branch_low = grad_hidden.astype(jnp.bfloat16)
    out_grad = jnp.einsum(
        "nd,ne->de", attended_low, grad_branch_low, preferred_element_type=jnp.float32
    )
    out_bias_grad = jnp.sum(grad_branch_low.astype(jnp.float32), axis=0)
    grad_attended_low = (
        jnp.einsum("ne,de->nd", grad_branch_low, out_weight, preferred_element_type=jnp.float32)
        .astype(jnp.bfloat16)
        .reshape(sequences, tile_rows, model_width)
    )
    query_grads = []
    key_grads = []
    value_grads = []
    for block_index, column in enumerate(range(0, model_width, head_block)):
        query_part = split_heads(queries, column)
        key_part = split_heads(keys_all, column)
        value_part = split_heads(values_all, column)
        grad_part = split_heads(grad_attended_low, column)
        masked = block_scores(query_part, key_part)
        probs_again = jnp.exp(masked - logsums[block_index])
        grad_probs = jnp.einsum(
            "sqhe,skhe->shqk", grad_part, value_part, preferred_element_type=jnp.float32
        )
        centre = jnp.sum(probs_again * grad_probs, axis=-1, keepdims=True)
        grad_scores = (probs_again * (grad_probs - centre)).astype(jnp.bfloat16)
        query_grads.append(
            jnp.einsum("shqk,skhe->sqhe", grad_scores, key_part, preferred_element_type=jnp.float32)
            * score_scale
        )
        key_grads.append(
            jnp.einsum(
                "shqk,sqhe->skhe", grad_scores, query_part, preferred_element_type=jnp.float32
            )
            * score_scale
        )
        value_grads.append(
            jnp.einsum(
                "shqk,sqhe->skhe",
                probs_again.astype(jnp.bfloat16),
                grad_part,
                preferred_element_type=jnp.float32,
            )
        )
    grad_query = jnp.concatenate(query_grads, axis=2).reshape(sequences, tile_rows, model_width)
    grad_key_full = jnp.concatenate(key_grads, axis=2).reshape(sequences, key_count, model_width)
    grad_value_full = jnp.concatenate(value_grads, axis=2).reshape(
        sequences, key_count, model_width
    )
    grad_shared_full = jnp.concatenate([grad_key_full, grad_value_full], axis=-1)
    grad_shared = lax.psum_scatter(
        grad_shared_full.astype(jnp.bfloat16), "tile", scatter_dimension=1, tiled=True
    ).astype(jnp.float32)
    grad_projected_low = (
        jnp.concatenate([grad_query, grad_shared], axis=-1)
        .astype(jnp.bfloat16)
        .reshape(count_rows, 3 * model_width)
    )
    qkv_grad = jnp.einsum(
        "nd,ne->de", normed_low, grad_projected_low, preferred_element_type=jnp.float32
    )
    column_sums = jnp.sum(grad_projected_low.astype(jnp.float32), axis=0)
    query_bias_grad = column_sums[:model_width]
    value_bias_grad = column_sums[2 * model_width :]
    grad_normed = jnp.einsum(
        "ne,de->nd", grad_projected_low, qkv_weight, preferred_element_type=jnp.float32
    )
    normed_first, norm_back_one = jax.vjp(layer_norm, flattened, gain_one, bias_one)
    grad_tokens_part, gain_one_grad, bias_one_grad = norm_back_one(grad_normed)
    grad_tokens = (
        (grad_hidden + grad_tokens_part)
        .astype(jnp.bfloat16)
        .reshape(sequences, tile_rows, model_width)
    )
    totals_small = lax.psum(
        (
            gain_one_grad,
            bias_one_grad,
            query_bias_grad,
            value_bias_grad,
            out_bias_grad,
            gain_two_grad,
            bias_two_grad,
            fc1_bias_grad,
            fc2_bias_grad,
            stats,
        ),
        ("dp", "tile"),
    )
    matrices = (qkv_grad, out_grad, fc1_grad, fc2_grad)
    row_shares = (
        lax.psum_scatter(
            matrices[0].astype(jnp.bfloat16), "dp", scatter_dimension=0, tiled=True
        ).astype(jnp.float32),
        lax.psum_scatter(
            matrices[1].astype(jnp.bfloat16), "dp", scatter_dimension=0, tiled=True
        ).astype(jnp.float32),
        lax.psum_scatter(
            matrices[2].astype(jnp.bfloat16), "dp", scatter_dimension=0, tiled=True
        ).astype(jnp.float32),
        lax.psum_scatter(
            matrices[3].astype(jnp.bfloat16), "dp", scatter_dimension=0, tiled=True
        ).astype(jnp.float32),
    )
    reduced = (
        lax.psum_scatter(
            row_shares[0].astype(jnp.bfloat16), "tile", scatter_dimension=1, tiled=True
        ).astype(jnp.float32),
        lax.psum_scatter(
            row_shares[1].astype(jnp.bfloat16), "tile", scatter_dimension=1, tiled=True
        ).astype(jnp.float32),
        lax.psum_scatter(
            row_shares[2].astype(jnp.bfloat16), "tile", scatter_dimension=1, tiled=True
        ).astype(jnp.float32),
        lax.psum_scatter(
            row_shares[3].astype(jnp.bfloat16), "tile", scatter_dimension=1, tiled=True
        ).astype(jnp.float32),
    )
    totals = totals_small[9]
    root_mean = jnp.sqrt(totals[:4] / (totals[4] * model_width))
    return (
        output,
        grad_tokens,
        totals_small[0],
        totals_small[1],
        reduced[0],
        totals_small[2],
        totals_small[3],
        reduced[1],
        totals_small[4],
        totals_small[5],
        totals_small[6],
        reduced[2],
        totals_small[7],
        reduced[3],
        totals_small[8],
        root_mean,
    )


def on_device(tokens, segment_ids, keep_mask, gain_one, bias_one, qkv_weight, query_bias, value_bias, out_weight, out_bias, gain_two, bias_two, fc1_weight, fc1_bias, fc2_weight, fc2_bias, cotangent):
    out, gt, qg, og, f1, f2, vec, late = call_everything(
        tokens[0], segment_ids, keep_mask, gain_one, bias_one, qkv_weight, query_bias, value_bias, out_weight, out_bias,
        gain_two, bias_two, fc1_weight, fc1_bias, fc2_weight, fc2_bias, cotangent[0],
    )
    r = list(call_finish(out, gt, qg, og, f1, f2, vec, late, fc1_weight.shape[1]))
    r[0] = r[0][None]
    r[1] = r[1][None]
    return tuple(r)


def fits(mesh):
    return mesh.shape["tile"] == 2 and mesh.shape["dp"] == 16


def solution(mesh):
    S, D, T = P("dp", "tile", None), P("dp", None), P("dp", "tile")
    return jax.shard_map(
        on_device if fits(mesh) else on_device_general,
        mesh=mesh,
        in_specs=(S, D, D) + (P(),) * 13 + (S,),
        out_specs=(S, S, P(), P(), T, P(), P(), T, P(), P(), P(), T, P(), T, P(), P()),
        check_vma=False,
    )
```
